32 devices in a mesh: ep: 8 (over z, y), tp: 4 (over x, core).
Axes of the slice: x: 2, y: 2, z: 4, core: 2. Of those that a mesh axis runs over, the one named last changes fastest.
Arguments:
- tokens: bfloat16 [16384, 1536], P(('ep', 'tp')), may hold values from -6 to 6
- norm1_gain: float32 [1536], replicated, may hold values from 0.5 to 1.5
- w_query: bfloat16 [1536, 1536], P(None, 'tp'), may hold values from -0.21875 to 0.21875
- key_weight: bfloat16 [1536, 512], P(None, 'tp'), may hold values from -0.21875 to 0.21875
- value_weight: bfloat16 [1536, 512], P(None, 'tp'), may hold values from -0.15625 to 0.15625
- w_out: bfloat16 [1536, 1536], P('tp'), may hold values from -1.25 to 1.25
- norm2_gain: float32 [1536], replicated, may hold values from 0.5 to 1.5
- w_router: bfloat16 [1536, 8], replicated, may hold values from -0.078125 to 0.078125
- w_gate: bfloat16 [8, 1536, 512], P('ep'), may hold values from -0.15625 to 0.15625
- w_up: bfloat16 [8, 1536, 512], P('ep'), may hold values from -0.15625 to 0.15625
- w_down: bfloat16 [8, 512, 1536], P('ep'), may hold values from -3 to 3
- routes: int32 [16384, 4], P(('ep', 'tp')), may hold values from 0 to 7, all different within a row; in each aligned block of 512 rows (0 to 511, 512 to 1023, ...) at most 384 rows name the same one
- piece_first_position: int32 [8, 4], P('ep'), may hold values from 0 to 1984, as said below
- piece_length: int32 [8, 4], P('ep'), may hold values from 64 to 256
- grad_out: bfloat16 [16384, 1536], P(('ep', 'tp')), may hold values from -6 to 6
Outputs:
- output: float32 [16384, 1536], P(('ep', 'tp'))
- grad_input: float32 [16384, 1536], P(('ep', 'tp'))
- grad_norm1: float32 [1536], P(('ep', 'tp'))
- grad_query: float32 [1536, 1536], P('ep', 'tp')
- grad_key: float32 [1536, 512], P('ep', 'tp')
- grad_value: float32 [1536, 512], P('ep', 'tp')
- grad_outproj: float32 [1536, 1536], P('tp', 'ep')
- grad_norm2: float32 [1536], P(('ep', 'tp'))
- grad_router: float32 [1536, 8], P(('ep', 'tp'))
- grad_gate: float32 [8, 1536, 512], P('ep', 'tp')
- grad_up: float32 [8, 1536, 512], P('ep', 'tp')
- grad_down: float32 [8, 512, 1536], P('ep', None, 'tp')
The draws below stay inside these ranges and needn't reach their ends.
Inputs may be any that keep to these rules, and one draw needn't show every extreme that they name: `routes`: each row names 4 different experts; within the rows of one device (aligned blocks of 512 rows) no expert is named by more than 384 rows. `piece_first_position`: piece j of a sequence lies within positions j * 512 to (j + 1) * 512 - 1.
All inputs are finite; a program needn't handle non-finite values.
Results may differ from the reference program's by a relative error of at most 0.023.
Values may be sent and summed in bfloat16 or wider, within the bound.
No kernel may reach another device: no remote copies, remote signals or barrier semaphores. Data moves between devices by JAX's collectives and lax.ppermute only.
A program may use at most 256 MiB of HBM per device.

```python
import math
import jax
import jax.numpy as jnp
import numpy as np
from jax import lax

MODEL_WIDTH = 1536
QUERY_HEADS = 24
KEY_VALUE_HEADS = 8
HEAD_SIZE = 64
FE = 512
SEQUENCE_LENGTH = 2048
PIECES = 4
PIECE_MAX = 256
EXPERTS = 8
TOPK = 4
TOK_DEV = 512
TOKEN_COUNT = 16384
SEQUENCE_COUNT = 8
CAP = 384
N_EP = 8
N_TP = 4


def piece_table(key):
    length_key = jax.random.fold_in(key, 101)
    place_key = jax.random.fold_in(key, 202)
    zone_width = SEQUENCE_LENGTH // PIECES
    lengths = jax.random.randint(length_key, (SEQUENCE_COUNT, PIECES), PIECE_MAX // 4, PIECE_MAX + 1)
    lengths = lengths.at[:, 0].set(PIECE_MAX)
    lengths = lengths.at[0, 1].set(PIECE_MAX // 4)
    lengths = lengths.at[0, PIECES - 1].set(PIECE_MAX // 4)
    room_left = zone_width - lengths + 1
    offsets = jax.random.randint(place_key, (SEQUENCE_COUNT, PIECES), 0, 1 << 20) % room_left
    offsets = offsets.at[0, 0].set(0)
    offsets = offsets.at[0, PIECES - 1].set(room_left[0, PIECES - 1] - 1)
    starts = jnp.arange(PIECES, dtype=jnp.int32)[None, :] * zone_width + offsets
    return (starts.astype(jnp.int32), lengths.astype(jnp.int32))


def draw_piece_first_position(key, part):
    return piece_table(key)[0]


def draw_piece_length(key, part):
    return piece_table(key)[1]


def level_of(key, extent, pieces, low, high):
    loudness, own = 1.0, jax.random.fold_in(key, 6)
    for position, parts in pieces:
        heights = jnp.exp(jax.random.uniform(jax.random.fold_in(own, position), (parts,), jnp.float32, low / len(pieces), high / len(pieces)))
        loudness = loudness * jnp.repeat(heights, extent[position] // parts).reshape([-1 if axis == position else 1 for axis in range(len(extent))])
    return loudness


def deal_out(own_key, own, number, rows, number_of, top, bound, slope):
    ranking = jax.random.permutation(own_key, number_of)
    heavy_load, usual = load_shares(number_of, rows * top, bound, slope, True), load_shares(number_of, rows * top, bound, slope, False)
    places = jnp.arange(number_of)

    def named(sizes, rotation):
        used = int((sizes > 0).sum())
        fixed = max(1, used // 4)
        moved = fixed + (places - fixed + rotation * (used - fixed)) % max(1, number_of - fixed)
        return jnp.zeros((number_of,), jnp.int32).at[ranking[jnp.where(places < fixed, places, moved)]].set(jnp.asarray(sizes, jnp.int32))

    sizes = jnp.where(number % 4 == 0, named(heavy_load, number // 4), named(usual, number - number // 4 - 1))
    mixed = jax.random.permutation(jax.random.fold_in(own, 3), number_of)
    source_of, sink = mixed[0:number_of // 2 * 2:2], mixed[1:number_of // 2 * 2:2]
    slack = jnp.minimum(sizes[source_of] - 1, bound - sizes[sink]) // 2
    slack = jnp.where((source_of == ranking[0]) | (sink == ranking[0]) | (sizes[sink] == 0), 0, jnp.maximum(slack, 0))
    moved = jax.random.randint(jax.random.fold_in(own, 4), (number_of // 2,), 0, 1 << 20) % (slack + 1)
    sizes = sizes.at[source_of].add(-moved).at[sink].add(moved)
    members = jnp.searchsorted(jnp.cumsum(sizes), jnp.arange(rows * top), side="right").astype(jnp.int32)
    table = members.reshape(top, rows).T
    table = table[jax.random.permutation(jax.random.fold_in(own, 1), rows)]
    rotation = jax.random.randint(jax.random.fold_in(own, 2), (rows, 1), 0, top)
    return jnp.take_along_axis(table, (jnp.arange(top)[None, :] + rotation) % top, axis=1)


def load_shares(number_of, total, limit, slope, full):
    weights = [(1 << 20) // math.isqrt(rank ** slope) + 1 for rank in range(1, number_of + 1)]
    largest = limit if full else min(limit, max(-(-total // number_of), total * weights[0] // sum(weights)))
    least = 1 if total - largest >= number_of - 1 else 0
    given, rest = [largest] + [least] * (number_of - 1), total - largest - least * (number_of - 1)
    while rest > 0:
        candidates = [i for i in range(1, number_of) if given[i] < largest] or [i for i in range(1, number_of) if given[i] < limit]
        mass, left = sum([weights[i] for i in candidates]), rest
        for i in candidates:
            addition = min(limit - given[i], max(1, left * weights[i] // mass), rest)
            given[i] = given[i] + addition
            rest = rest - addition
    return np.array(given)


def scatter_about(stream_key, dims, spread, most, cuts=(), kind=jnp.bfloat16):
    array = jax.random.normal(stream_key, dims, jnp.float32) * spread
    if len(cuts) > 0:
        array = level_of(stream_key, dims, cuts, -0.22, 0.18) * array
    return jnp.clip(array, min=-most, max=most).astype(kind)


def setup_inputs(seed: int = 0) -> dict:
    splits = jax.random.split(jax.random.key(seed), 16)
    tokens = scatter_about(splits[0], (TOKEN_COUNT, MODEL_WIDTH), 1.0, 6.0, ((0, 32),))
    norm1_gain = jnp.clip(1.0 + 0.1 * jax.random.normal(splits[1], (MODEL_WIDTH,), jnp.float32), 0.5, 1.5)
    w_query = scatter_about(splits[2], (MODEL_WIDTH, QUERY_HEADS * HEAD_SIZE), (MODEL_WIDTH // 2) ** -0.5, 0.21875, ((1, 4),))
    key_weight = scatter_about(splits[3], (MODEL_WIDTH, KEY_VALUE_HEADS * HEAD_SIZE), (MODEL_WIDTH // 2) ** -0.5, 0.21875, ((1, 4),))
    value_weight = scatter_about(splits[4], (MODEL_WIDTH, KEY_VALUE_HEADS * HEAD_SIZE), MODEL_WIDTH ** -0.5, 0.15625, ((1, 4),))
    w_out = scatter_about(splits[5], (QUERY_HEADS * HEAD_SIZE, MODEL_WIDTH), (QUERY_HEADS * HEAD_SIZE // 64) ** -0.5, 1.25, ((0, 4),))
    norm2_gain = jnp.clip(1.0 + 0.1 * jax.random.normal(splits[6], (MODEL_WIDTH,), jnp.float32), 0.5, 1.5)
    w_router = scatter_about(splits[7], (MODEL_WIDTH, EXPERTS), (4 * MODEL_WIDTH) ** -0.5, 0.078125)
    w_gate = scatter_about(splits[8], (EXPERTS, MODEL_WIDTH, FE), MODEL_WIDTH ** -0.5, 0.15625, ((0, 8),))
    w_up = scatter_about(splits[9], (EXPERTS, MODEL_WIDTH, FE), MODEL_WIDTH ** -0.5, 0.15625, ((0, 8),))
    w_down = scatter_about(splits[10], (EXPERTS, FE, MODEL_WIDTH), (max(FE // 128, 1)) ** -0.5, 3.0, ((0, 8),))
    routes_keys = jax.random.split(jax.random.fold_in(splits[11], 1), TOKEN_COUNT // TOK_DEV)
    routes_turns = jax.random.permutation(jax.random.fold_in(splits[11], 3), TOKEN_COUNT // TOK_DEV)
    routes = jax.vmap(lambda own, number: deal_out(jax.random.fold_in(splits[11], 2), own, number, TOK_DEV, EXPERTS, TOPK, CAP, 2))(routes_keys, routes_turns).reshape((TOKEN_COUNT, TOPK))
    piece_first_position = draw_piece_first_position(jax.random.fold_in(splits[15], 71), 0)
    piece_length = draw_piece_length(jax.random.fold_in(splits[15], 71), 0)
    grad_out = scatter_about(splits[14], (TOKEN_COUNT, MODEL_WIDTH), 1.0, 6.0, ((0, 32),))
    return {"tokens": tokens, "norm1_gain": norm1_gain, "w_query": w_query, "key_weight": key_weight, "value_weight": value_weight, "w_out": w_out, "norm2_gain": norm2_gain, "w_router": w_router, "w_gate": w_gate, "w_up": w_up, "w_down": w_down, "routes": routes, "piece_first_position": piece_first_position, "piece_length": piece_length, "grad_out": grad_out}


EPSILON = 1e-05
ROPE_BASE = 10000.0
MASK_FILL = -1e+30
PRECISE = lax.Precision.HIGHEST

@jax.custom_vjp
def reduced_precision(v):
    return lax.optimization_barrier(v.astype(jnp.bfloat16)).astype(jnp.float32)

@jax.custom_vjp
def low_back(v):
    return v

def low_keep(v):
    return (reduced_precision(v), None)

def low_pass(kept, grad):
    return (grad,)

def back_keep(v):
    return (v, None)

def back_low(kept, grad):
    return (reduced_precision(grad),)
reduced_precision.defvjp(low_keep, low_pass)
low_back.defvjp(back_keep, back_low)

def rms_norm(values_in, gain_vec):
    return values_in * lax.rsqrt(lax.optimization_barrier(jnp.mean(values_in * values_in, axis=-1, keepdims=True)) + EPSILON) * gain_vec

def rope_tables(positions):
    half_width = HEAD_SIZE // 2
    exponent = jnp.arange(half_width, dtype=jnp.float32) * (2.0 / HEAD_SIZE)
    frequency = ROPE_BASE ** (-exponent)
    angles = positions.astype(jnp.float32)[:, None] * frequency[None, :]
    return (jnp.cos(angles)[:, None, :], jnp.sin(angles)[:, None, :])

def apply_rotary(values_in, rotary_cosine, rotary_sine):
    half_width = values_in.shape[-1] // 2
    first_half = values_in[..., :half_width]
    second_half = values_in[..., half_width:]
    return jnp.concatenate([first_half * rotary_cosine - second_half * rotary_sine, second_half * rotary_cosine + first_half * rotary_sine], axis=-1)

def piece_labels(starts_row, lengths_row, length_all):
    positions = jnp.arange(length_all, dtype=jnp.int32)
    inside = (positions[:, None] >= starts_row[None, :]) & (positions[:, None] < (starts_row + lengths_row)[None, :])
    labels = jnp.arange(1, starts_row.shape[0] + 1, dtype=jnp.int32)
    return (lax.optimization_barrier(jnp.sum(jnp.where(inside, labels[None, :], 0), axis=1)) - 1).astype(jnp.int32)

def allowed_pairs(query_pos, query_label, key_label):
    key_pos = jnp.arange(key_label.shape[0], dtype=jnp.int32)
    causal = key_pos[None, :] <= query_pos[:, None]
    same_piece = (query_label[:, None] == key_label[None, :]) & (query_label[:, None] >= 0)
    return causal | same_piece

def sequence_attention(packed_rows):
    query_sequence, key_seq, value_seq, starts_row, lengths_row = packed_rows
    rows_per_block = min(512, SEQUENCE_LENGTH)
    block_total = SEQUENCE_LENGTH // rows_per_block
    query_group_width = QUERY_HEADS // KEY_VALUE_HEADS
    score_scale = 1.0 / math.sqrt(HEAD_SIZE)
    label_seq = piece_labels(starts_row, lengths_row, SEQUENCE_LENGTH)
    blocks_of_query = query_sequence.reshape(block_total, rows_per_block, KEY_VALUE_HEADS, query_group_width, HEAD_SIZE)

    def one_block(block_pair):
        query_block, block_index = block_pair
        first_row = (block_index * rows_per_block).astype(jnp.int32)
        query_pos = first_row + jnp.arange(rows_per_block, dtype=jnp.int32)
        query_label = lax.dynamic_slice_in_dim(label_seq, first_row, rows_per_block, 0)
        allowed = allowed_pairs(query_pos, query_label, label_seq)
        scores = jnp.einsum('qhgd,khd->hgqk', query_block, key_seq, precision=PRECISE) * score_scale
        scores = low_back(scores)
        scores = jnp.where(allowed[None, None], scores, MASK_FILL)
        weights = jax.nn.softmax(scores, axis=-1)
        return jnp.einsum('hgqk,khd->qhgd', reduced_precision(weights), value_seq, precision=PRECISE)
    outputs = lax.map(jax.checkpoint(one_block), (blocks_of_query, jnp.arange(block_total, dtype=jnp.int32)))
    return outputs.reshape(SEQUENCE_LENGTH, QUERY_HEADS * HEAD_SIZE)

def expert_ffn(packed_rows):
    rows_in, gate_mat, up_mat, down_mat = packed_rows
    gate_pre = low_back(jnp.dot(rows_in, gate_mat, precision=PRECISE))
    up_pre = low_back(jnp.dot(rows_in, up_mat, precision=PRECISE))
    activation = reduced_precision(jax.nn.silu(gate_pre) * up_pre)
    return reduced_precision(low_back(jnp.dot(activation, down_mat, precision=PRECISE)))

def layer(inputs, norm1_gain, w_query, key_weight, value_weight, w_out, norm2_gain, w_router, w_gate, w_up, w_down, routes, piece_first_position, piece_length):
    query_group_width = QUERY_HEADS // KEY_VALUE_HEADS
    normed_one = reduced_precision(rms_norm(inputs, norm1_gain))
    query_lin = low_back(jnp.dot(normed_one, w_query, precision=PRECISE))
    key_linear = low_back(jnp.dot(normed_one, key_weight, precision=PRECISE))
    every_value = reduced_precision(low_back(jnp.dot(normed_one, value_weight, precision=PRECISE)))
    positions = jnp.arange(TOKEN_COUNT, dtype=jnp.int32) % SEQUENCE_LENGTH
    rotary_cosine, rotary_sine = rope_tables(positions)
    every_query = reduced_precision(apply_rotary(query_lin.reshape(TOKEN_COUNT, QUERY_HEADS, HEAD_SIZE), rotary_cosine, rotary_sine))
    every_key = reduced_precision(apply_rotary(key_linear.reshape(TOKEN_COUNT, KEY_VALUE_HEADS, HEAD_SIZE), rotary_cosine, rotary_sine))
    packed_rows = (every_query.reshape(SEQUENCE_COUNT, SEQUENCE_LENGTH, KEY_VALUE_HEADS, query_group_width, HEAD_SIZE), every_key.reshape(SEQUENCE_COUNT, SEQUENCE_LENGTH, KEY_VALUE_HEADS, HEAD_SIZE), every_value.reshape(SEQUENCE_COUNT, SEQUENCE_LENGTH, KEY_VALUE_HEADS, HEAD_SIZE), piece_first_position, piece_length)
    attended = lax.map(jax.checkpoint(sequence_attention), packed_rows).reshape(TOKEN_COUNT, QUERY_HEADS * HEAD_SIZE)
    attended = reduced_precision(low_back(attended))
    attn_out = low_back(jnp.dot(attended, w_out, precision=PRECISE))
    middle = inputs + attn_out
    normed_two = reduced_precision(rms_norm(middle, norm2_gain))
    logits = low_back(jnp.dot(normed_two, w_router, precision=PRECISE))
    router_probs = jax.nn.softmax(logits, axis=-1)
    gate_probs = jnp.take_along_axis(router_probs, routes, axis=1)
    route_total = TOKEN_COUNT * TOPK
    copies = low_back(jnp.broadcast_to(normed_two[:, None, :], (TOKEN_COUNT, TOPK, MODEL_WIDTH))).reshape(route_total, MODEL_WIDTH)
    slot_width = N_EP * N_TP * CAP
    flat_routes = routes.reshape(route_total).astype(jnp.int32)
    sorted_order = jnp.argsort(flat_routes, stable=True).astype(jnp.int32)
    expert_ids = jnp.arange(EXPERTS, dtype=jnp.int32)
    counts = lax.optimization_barrier(jnp.sum((flat_routes[:, None] == expert_ids[None, :]).astype(jnp.int32), axis=0))
    offsets = (jnp.cumsum(counts) - counts).astype(jnp.int32)
    slot_pos = jnp.arange(slot_width, dtype=jnp.int32)
    table_index = jnp.minimum(offsets[:, None] + slot_pos[None, :], route_total - 1).astype(jnp.int32)
    slot_valid = slot_pos[None, :] < counts[:, None]
    source = sorted_order[table_index]
    expert_rows = jnp.where(slot_valid[:, :, None], copies[source], 0.0)
    expert_out = lax.map(jax.checkpoint(expert_ffn), (expert_rows, w_gate, w_up, w_down))
    route_rank = jnp.zeros((route_total,), jnp.int32).at[sorted_order].set(jnp.arange(route_total, dtype=jnp.int32))
    route_slot = (route_rank - offsets[flat_routes]).astype(jnp.int32)
    routed = expert_out[flat_routes, route_slot].reshape(TOKEN_COUNT, TOPK, MODEL_WIDTH)
    mixed_out = lax.optimization_barrier(jnp.sum(gate_probs[:, :, None] * routed, axis=1))
    return middle + mixed_out

def reference(tokens, norm1_gain, w_query, key_weight, value_weight, w_out, norm2_gain, w_router, w_gate, w_up, w_down, routes, piece_first_position, piece_length, grad_out):

    def forward(inputs, gain_one, query_mat, key_mat, value_mat, out_mat, gain_two, router_mat, gate_mat, up_mat, down_mat):
        return layer(inputs, gain_one, query_mat, key_mat, value_mat, out_mat, gain_two, router_mat, gate_mat, up_mat, down_mat, routes, piece_first_position, piece_length)
    output, pullback = jax.vjp(forward, tokens.astype(jnp.float32), norm1_gain.astype(jnp.float32), w_query.astype(jnp.float32), key_weight.astype(jnp.float32), value_weight.astype(jnp.float32), w_out.astype(jnp.float32), norm2_gain.astype(jnp.float32), w_router.astype(jnp.float32), w_gate.astype(jnp.float32), w_up.astype(jnp.float32), w_down.astype(jnp.float32))
    gradients = pullback(grad_out.astype(jnp.float32))
    return (output, gradients[0], gradients[1], gradients[2], gradients[3], gradients[4], gradients[5], gradients[6], gradients[7], gradients[8], gradients[9], gradients[10])
```

```python
import functools
import math

import jax
import jax.numpy as jnp
from jax import lax
from jax.experimental import pallas as pl
from jax.experimental.pallas import tpu as pltpu
from jax.sharding import Mesh, PartitionSpec as P

HEAD_SIZE = 64
HALF = HEAD_SIZE // 2
SEQUENCE_LENGTH = 2048
EPSILON = 1e-05
ROPE_BASE = 10000.0
MASK_FILL = -1e30
LANES = 128
F32 = jnp.float32
BF16 = jnp.bfloat16
VMEM_LIMIT = 60 * 1024 * 1024


def dot(a, b, ca=1, cb=0):
    return lax.dot_general(a, b, (((ca,), (cb,)), ((), ())), preferred_element_type=F32)


def qkv_kernel(q_cols, kv_cols, h_ref, w_ref, cos_ref, sin_ref, q_ref, k_ref, kt_ref, v_ref, vt_ref):
    y = dot(w_ref[...], h_ref[...], 1, 1)
    cos, sin = cos_ref[...], sin_ref[...]

    def turned(base):
        a = y[base : base + HALF]
        b = y[base + HALF : base + HEAD_SIZE]
        return jnp.concatenate([a * cos - b * sin, b * cos + a * sin], axis=0)

    for h in range(q_cols // HEAD_SIZE):
        base = h * HEAD_SIZE
        q_ref[base : base + HEAD_SIZE, :] = (
            turned(base).astype(BF16) * jnp.asarray(1.0 / math.sqrt(HEAD_SIZE), BF16)
        )
    for g in range(kv_cols // HEAD_SIZE):
        base = g * HEAD_SIZE
        kt = turned(q_cols + base)
        kt_ref[base : base + HEAD_SIZE, :] = kt.astype(BF16)
        k_ref[g] = kt.T.astype(BF16)
        vt = y[q_cols + kv_cols + base : q_cols + kv_cols + base + HEAD_SIZE]
        vt_ref[base : base + HEAD_SIZE, :] = vt.astype(BF16)
        v_ref[g] = vt.T.astype(BF16)


def project_qkv(h_all, w_all, cos, sin, rows, q_cols, kv_cols):
    total, width = h_all.shape
    groups = kv_cols // HEAD_SIZE
    cols = q_cols + 2 * kv_cols
    return pl.pallas_call(
        functools.partial(qkv_kernel, q_cols, kv_cols),
        grid=(total // rows,),
        in_specs=[
            pl.BlockSpec((rows, width), lambda i: (i, 0)),
            pl.BlockSpec((cols, width), lambda i: (0, 0)),
            pl.BlockSpec((HALF, rows), lambda i: (0, i)),
            pl.BlockSpec((HALF, rows), lambda i: (0, i)),
        ],
        out_specs=[
            pl.BlockSpec((q_cols, rows), lambda i: (0, i)),
            pl.BlockSpec((groups, rows, HEAD_SIZE), lambda i: (0, i, 0)),
            pl.BlockSpec((kv_cols, rows), lambda i: (0, i)),
            pl.BlockSpec((groups, rows, HEAD_SIZE), lambda i: (0, i, 0)),
            pl.BlockSpec((kv_cols, rows), lambda i: (0, i)),
        ],
        out_shape=[
            jax.ShapeDtypeStruct((q_cols, total), BF16),
            jax.ShapeDtypeStruct((groups, total, HEAD_SIZE), BF16),
            jax.ShapeDtypeStruct((kv_cols, total), BF16),
            jax.ShapeDtypeStruct((groups, total, HEAD_SIZE), BF16),
            jax.ShapeDtypeStruct((kv_cols, total), BF16),
        ],
        compiler_params=pltpu.CompilerParams(vmem_limit_bytes=VMEM_LIMIT),
        name="qkv",
    )(h_all, w_all, cos, sin)


def last_key(s_ref, zone, own, rows):
    zone_index = own * rows // zone
    zones = SEQUENCE_LENGTH // zone
    start = s_ref[1 + zone_index]
    stop = start + s_ref[1 + zones + zone_index]
    position = own * rows + lax.broadcasted_iota(jnp.int32, (1, rows), 1)
    return jnp.where((position >= start) & (position < stop), stop - 1, position)


def block_walk(me, own, rows, zone, pair):
    per_zone = zone // rows
    pair(own, True, True)
    for other in range(1, per_zone):
        pair(own ^ other, True, False)
    first = (own // per_zone) * per_zone

    def step(key_block, carry):
        pair(key_block, False, False)
        return carry

    lax.fori_loop(0, first, step, 0)


def attend_kernel(rows, zone, heads, groups, s_ref, q_ref, k_ref, vt_ref, o_ref, lse_ref, acc, top, total):
    me = s_ref[0]
    own = me ^ pl.program_id(0)
    limit = last_key(s_ref, zone, own, rows)

    def pair(key_block, masked, first):
        offset = pl.multiple_of((me ^ key_block) * rows, rows)
        if masked:
            key_pos = key_block * rows + lax.broadcasted_iota(jnp.int32, (rows, rows), 0)
            allowed = key_pos <= limit
        for h in range(heads):
            g = h // (heads // groups)
            r = slice(h * HEAD_SIZE, (h + 1) * HEAD_SIZE)
            s = dot(k_ref[g, pl.ds(offset, rows), :], q_ref[r, :])
            if masked:
                s = jnp.where(allowed, s, MASK_FILL)
            peak = jnp.max(s, axis=0, keepdims=True)
            vt = vt_ref[g * HEAD_SIZE : (g + 1) * HEAD_SIZE, pl.ds(offset, rows)]
            if first:
                p = jnp.exp(s - peak)
                top[h : h + 1, :] = peak
                total[h : h + 1, :] = jnp.sum(p, axis=0, keepdims=True)
                acc[r, :] = dot(vt, p.astype(BF16))
            else:
                old = top[h : h + 1, :]
                new = jnp.maximum(old, peak)
                fade = jnp.exp(old - new)
                p = jnp.exp(s - new)
                top[h : h + 1, :] = new
                total[h : h + 1, :] = total[h : h + 1, :] * fade + jnp.sum(p, axis=0, keepdims=True)
                acc[r, :] = acc[r, :] * fade + dot(vt, p.astype(BF16))

    block_walk(me, own, rows, zone, pair)
    for h in range(heads):
        r = slice(h * HEAD_SIZE, (h + 1) * HEAD_SIZE)
        o_ref[r, :] = (acc[r, :] / total[h : h + 1, :]).astype(BF16)
        lse_ref[h : h + 1, :] = top[h : h + 1, :] + jnp.log(total[h : h + 1, :])


def attend(scalars, q, k, vt, rows, zone):
    q_cols, total = q.shape
    groups = k.shape[0]
    heads = q_cols // HEAD_SIZE
    return pl.pallas_call(
        functools.partial(attend_kernel, rows, zone, heads, groups),
        grid_spec=pltpu.PrefetchScalarGridSpec(
            num_scalar_prefetch=1,
            grid=(total // rows,),
            in_specs=[
                pl.BlockSpec((q_cols, rows), lambda i, s: (0, i)),
                pl.BlockSpec(k.shape, lambda i, s: (0, 0, 0)),
                pl.BlockSpec(vt.shape, lambda i, s: (0, 0)),
            ],
            out_specs=[
                pl.BlockSpec((q_cols, rows), lambda i, s: (0, i)),
                pl.BlockSpec((heads, rows), lambda i, s: (0, i)),
            ],
            scratch_shapes=[
                pltpu.VMEM((q_cols, rows), F32),
                pltpu.VMEM((8, rows), F32),
                pltpu.VMEM((8, rows), F32),
            ],
        ),
        out_shape=[
            jax.ShapeDtypeStruct((q_cols, total), BF16),
            jax.ShapeDtypeStruct((heads, total), F32),
        ],
        compiler_params=pltpu.CompilerParams(vmem_limit_bytes=VMEM_LIMIT),
        name="attend",
    )(scalars, q, k, vt)


def attend_back_kernel(
    rows,
    zone,
    heads,
    groups,
    s_ref,
    q_ref,
    o_ref,
    do_ref,
    lse_ref,
    k_ref,
    kt_ref,
    v_ref,
    cos_ref,
    sin_ref,
    dq_ref,
    dkv_ref,
    dq,
    dk,
    dv,
    delta,
):
    me = s_ref[0]
    step = pl.program_id(0)
    own = me ^ step
    limit = last_key(s_ref, zone, own, rows)
    here = pl.multiple_of(step * rows, rows)

    @pl.when(step == 0)
    def _():
        dk[...] = jnp.zeros_like(dk)
        dv[...] = jnp.zeros_like(dv)

    for h in range(heads):
        r = slice(h * HEAD_SIZE, (h + 1) * HEAD_SIZE)
        delta[h : h + 1, :] = jnp.sum(
            do_ref[r, :].astype(F32) * o_ref[r, :].astype(F32), axis=0, keepdims=True
        )

    def pair(key_block, masked, first):
        offset = pl.multiple_of((me ^ key_block) * rows, rows)
        keys = pl.ds(offset, rows)
        if masked:
            key_pos = key_block * rows + lax.broadcasted_iota(jnp.int32, (rows, rows), 0)
            allowed = key_pos <= limit
        for g in range(groups):
            kb = k_ref[g, keys, :]
            vb = v_ref[g, keys, :]
            kt = kt_ref[g * HEAD_SIZE : (g + 1) * HEAD_SIZE, keys]
            dk_sum = dk[g, keys, :]
            dv_sum = dv[g, keys, :]
            for h in range(g * (heads // groups), (g + 1) * (heads // groups)):
                r = slice(h * HEAD_SIZE, (h + 1) * HEAD_SIZE)
                s = dot(kb, q_ref[r, :])
                if masked:
                    s = jnp.where(allowed, s, MASK_FILL)
                p = jnp.exp(s - lse_ref[h : h + 1, :])
                dp = dot(vb, do_ref[r, :])
                ds = (p * (dp - delta[h : h + 1, :])).astype(BF16)
                dv_sum = dv_sum + dot(p.astype(BF16), do_ref[r, :], 1, 1)
                dk_sum = dk_sum + dot(ds, q_ref[r, :], 1, 1)
                part = dot(kt, ds)
                dq[r, :] = part if first else dq[r, :] + part
            dk[g, keys, :] = dk_sum
            dv[g, keys, :] = dv_sum

    block_walk(me, own, rows, zone, pair)
    cos, sin = cos_ref[:, pl.ds(here, rows)], sin_ref[:, pl.ds(here, rows)]
    scale = 1.0 / math.sqrt(HEAD_SIZE)
    for h in range(heads):
        base = h * HEAD_SIZE
        a = dq[base : base + HALF, :] * scale
        b = dq[base + HALF : base + HEAD_SIZE, :] * scale
        dq_ref[base : base + HALF, :] = (a * cos + b * sin).astype(BF16)
        dq_ref[base + HALF : base + HEAD_SIZE, :] = (b * cos - a * sin).astype(BF16)

    @pl.when(step == pl.num_programs(0) - 1)
    def _():
        every_cos, every_sin = cos_ref[...], sin_ref[...]
        for g in range(groups):
            base = g * HEAD_SIZE
            turned = dk[g].T
            a, b = turned[:HALF], turned[HALF:]
            dkv_ref[base : base + HALF, :] = (a * every_cos + b * every_sin).astype(BF16)
            dkv_ref[base + HALF : base + HEAD_SIZE, :] = (b * every_cos - a * every_sin).astype(BF16)
            base = (groups + g) * HEAD_SIZE
            dkv_ref[base : base + HEAD_SIZE, :] = dv[g].T.astype(BF16)


def attend_back(scalars, q, o, do, lse, k, kt, v, cos, sin, rows, zone):
    q_cols, total = q.shape
    groups = k.shape[0]
    heads = q_cols // HEAD_SIZE
    whole2 = lambda i, s: (0, 0)
    whole3 = lambda i, s: (0, 0, 0)
    block = lambda i, s: (0, i)
    return pl.pallas_call(
        functools.partial(attend_back_kernel, rows, zone, heads, groups),
        grid_spec=pltpu.PrefetchScalarGridSpec(
            num_scalar_prefetch=1,
            grid=(total // rows,),
            in_specs=[
                pl.BlockSpec((q_cols, rows), block),
                pl.BlockSpec((q_cols, rows), block),
                pl.BlockSpec((q_cols, rows), block),
                pl.BlockSpec((heads, rows), block),
                pl.BlockSpec(k.shape, whole3),
                pl.BlockSpec(kt.shape, whole2),
                pl.BlockSpec(v.shape, whole3),
                pl.BlockSpec(cos.shape, whole2),
                pl.BlockSpec(sin.shape, whole2),
            ],
            out_specs=[
                pl.BlockSpec((q_cols, rows), block),
                pl.BlockSpec((2 * groups * HEAD_SIZE, total), whole2),
            ],
            scratch_shapes=[
                pltpu.VMEM((q_cols, rows), F32),
                pltpu.VMEM((groups, total, HEAD_SIZE), F32),
                pltpu.VMEM((groups, total, HEAD_SIZE), F32),
                pltpu.VMEM((8, rows), F32),
            ],
        ),
        out_shape=[
            jax.ShapeDtypeStruct((q_cols, total), BF16),
            jax.ShapeDtypeStruct((2 * groups * HEAD_SIZE, total), BF16),
        ],
        compiler_params=pltpu.CompilerParams(vmem_limit_bytes=VMEM_LIMIT),
        name="attend_back",
    )(scalars, q, o, do, lse, k, kt, v, cos, sin)


def expert_kernel(
    experts,
    s_ref,
    h_ref,
    dy_ref,
    routes_ref,
    router_ref,
    wg_ref,
    wu_ref,
    wd_ref,
    mix_ref,
    dh_ref,
    dgate_ref,
    gates_ref,
    act_ref,
    dgu_ref,
    mix,
    dh,
):
    e = pl.program_id(1)
    rows = h_ref.shape[0]
    hidden = wg_ref.shape[2]
    lane = lax.broadcasted_iota(jnp.int32, (rows, LANES), 1)
    expert = s_ref[e]

    @pl.when(e == 0)
    def _():
        logits = dot(h_ref[...], router_ref[...])
        logits = jnp.where(lane < experts, logits, MASK_FILL)
        weights = jnp.exp(logits - jnp.max(logits, axis=1, keepdims=True))
        weights = weights / jnp.sum(weights, axis=1, keepdims=True)
        chosen = jnp.zeros((rows, LANES), jnp.bool_)
        for j in range(routes_ref.shape[1]):
            chosen = chosen | (routes_ref[:, j : j + 1] == lane)
        gates_ref[...] = jnp.where(chosen, weights, 0.0)
        dgate_ref[...] = jnp.zeros_like(dgate_ref)
        mix[...] = jnp.zeros_like(mix)
        dh[...] = jnp.zeros_like(dh)

    gate = jnp.sum(jnp.where(lane == expert, gates_ref[...], 0.0), axis=1, keepdims=True)
    chosen = jnp.max(jnp.where(routes_ref[...] == expert, 1.0, 0.0), axis=1, keepdims=True)
    gp = dot(h_ref[...], wg_ref[0])
    up = dot(h_ref[...], wu_ref[0])
    sg = jax.nn.sigmoid(gp)
    silu = gp * sg
    act = (silu * up).astype(BF16)
    act_ref[0] = act
    eo = dot(act, wd_ref[0]).astype(BF16).astype(F32)
    dy = dy_ref[...].astype(F32)
    dgate = chosen * jnp.sum(dy * eo, axis=1, keepdims=True)
    dgate_ref[...] += jnp.where(lane == expert, dgate, 0.0)
    mix[...] += gate * eo
    dact = dot((gate * dy).astype(BF16), wd_ref[0], 1, 1)
    dgp = (dact * up * sg * (1.0 + gp * (1.0 - sg))).astype(BF16)
    dup = (dact * silu).astype(BF16)
    dgu_ref[0, :, :hidden] = dgp
    dgu_ref[0, :, hidden:] = dup
    part = dot(dgp, wg_ref[0], 1, 1) + dot(dup, wu_ref[0], 1, 1)
    dh[...] += part.astype(BF16).astype(F32)

    @pl.when(e == pl.num_programs(1) - 1)
    def _():
        mix_ref[...] = mix[...].astype(BF16)
        dh_ref[...] = dh[...].astype(BF16)


def run_experts(ids, h, dy, routes, router, wg, wu, wd, experts, rows):
    total, width = h.shape
    mine, _, hidden = wg.shape
    token = lambda i, e, s: (i, 0)
    matrix = lambda i, e, s: (e, 0, 0)
    return pl.pallas_call(
        functools.partial(expert_kernel, experts),
        grid_spec=pltpu.PrefetchScalarGridSpec(
            num_scalar_prefetch=1,
            grid=(total // rows, mine),
            in_specs=[
                pl.BlockSpec((rows, width), token),
                pl.BlockSpec((rows, width), token),
                pl.BlockSpec((rows, routes.shape[1]), token),
                pl.BlockSpec((width, LANES), lambda i, e, s: (0, 0)),
                pl.BlockSpec((1, width, hidden), matrix),
                pl.BlockSpec((1, width, hidden), matrix),
                pl.BlockSpec((1, hidden, width), matrix),
            ],
            out_specs=[
                pl.BlockSpec((rows, width), token),
                pl.BlockSpec((rows, width), token),
                pl.BlockSpec((rows, LANES), token),
                pl.BlockSpec((rows, LANES), token),
                pl.BlockSpec((1, rows, hidden), lambda i, e, s: (e, i, 0)),
                pl.BlockSpec((1, rows, 2 * hidden), lambda i, e, s: (e, i, 0)),
            ],
            scratch_shapes=[pltpu.VMEM((rows, width), F32), pltpu.VMEM((rows, width), F32)],
        ),
        out_shape=[
            jax.ShapeDtypeStruct((total, width), BF16),
            jax.ShapeDtypeStruct((total, width), BF16),
            jax.ShapeDtypeStruct((total, LANES), F32),
            jax.ShapeDtypeStruct((total, LANES), F32),
            jax.ShapeDtypeStruct((mine, total, hidden), BF16),
            jax.ShapeDtypeStruct((mine, total, 2 * hidden), BF16),
        ],
        compiler_params=pltpu.CompilerParams(vmem_limit_bytes=VMEM_LIMIT),
        name="experts",
    )(ids, h, dy, routes, router, wg, wu, wd)


def expert_grad_kernel(s_ref, h_ref, dy_ref, gates_ref, act_ref, dgu_ref, out_ref, gate_up, down):
    rows = h_ref.shape[0]
    hidden = act_ref.shape[2]
    step = pl.program_id(1)
    lane = lax.broadcasted_iota(jnp.int32, (rows, LANES), 1)
    expert = s_ref[pl.program_id(0)]
    gate = jnp.sum(jnp.where(lane == expert, gates_ref[...], 0.0), axis=1, keepdims=True)
    deo = (gate * dy_ref[...].astype(F32)).astype(BF16)
    new_gate_up = dot(h_ref[...], dgu_ref[0], 0, 0)
    new_down = dot(deo, act_ref[0], 0, 0)

    @pl.when(step == 0)
    def _():
        gate_up[...] = new_gate_up
        down[...] = new_down

    @pl.when(step > 0)
    def _():
        gate_up[...] += new_gate_up
        down[...] += new_down

    @pl.when(step == pl.num_programs(1) - 1)
    def _():
        out_ref[0, :, : 2 * hidden] = gate_up[...].astype(BF16)
        out_ref[0, :, 2 * hidden :] = down[...].astype(BF16)


def expert_grads(ids, h, dy, gates, act, dgu, rows):
    total, width = h.shape
    mine, _, hidden = act.shape
    token = lambda e, i, s: (i, 0)
    return pl.pallas_call(
        expert_grad_kernel,
        grid_spec=pltpu.PrefetchScalarGridSpec(
            num_scalar_prefetch=1,
            grid=(mine, total // rows),
            in_specs=[
                pl.BlockSpec((rows, width), token),
                pl.BlockSpec((rows, width), token),
                pl.BlockSpec((rows, LANES), token),
                pl.BlockSpec((1, rows, hidden), lambda e, i, s: (e, i, 0)),
                pl.BlockSpec((1, rows, 2 * hidden), lambda e, i, s: (e, i, 0)),
            ],
            out_specs=pl.BlockSpec((1, width, 3 * hidden), lambda e, i, s: (e, 0, 0)),
            scratch_shapes=[pltpu.VMEM((width, 2 * hidden), F32), pltpu.VMEM((width, hidden), F32)],
        ),
        out_shape=jax.ShapeDtypeStruct((mine, width, 3 * hidden), BF16),
        compiler_params=pltpu.CompilerParams(vmem_limit_bytes=VMEM_LIMIT),
        name="expert_grads",
    )(ids, h, dy, gates, act, dgu)


def body(
    sizes,
    tokens,
    norm1_gain,
    w_query,
    key_weight,
    value_weight,
    w_out,
    norm2_gain,
    w_router,
    w_gate,
    w_up,
    w_down,
    routes,
    piece_first_position,
    piece_length,
    grad_out,
):
    nz, nx = sizes
    rows, width = tokens.shape
    blocks = 2 * nx
    q_cols, kv_cols = w_query.shape[1], key_weight.shape[1]
    experts = w_router.shape[1]
    hidden = w_gate.shape[2]
    zone = SEQUENCE_LENGTH // piece_length.shape[1]
    iz, iy, ix, ic = (lax.axis_index(a) for a in "zyxc")
    me = ix * 2 + ic

    def tp_swap(value, bit):
        if bit == 0:
            return lax.ppermute(value, "c", [(0, 1), (1, 0)])
        return lax.ppermute(value, "x", [(i, i ^ (1 << (bit - 1))) for i in range(nx)])

    def y_swap(value):
        return lax.ppermute(value, "y", [(0, 1), (1, 0)])

    bits = blocks.bit_length() - 1

    def tp_gather(value):
        held = {0: value}
        for bit in reversed(range(bits)):
            for i in list(held):
                held[i | (1 << bit)] = tp_swap(held[i], bit)
        return jnp.concatenate([held[i] for i in range(blocks)], axis=0)

    def tp_scatter(parts):
        parts = dict(enumerate(parts))
        for bit in range(bits):
            for i in sorted(parts):
                if i & (1 << bit):
                    parts[i] = tp_swap(parts[i], bit)
            for i in sorted(parts):
                if i & (1 << bit):
                    other = parts.pop(i)
                    base = parts[i ^ (1 << bit)].astype(F32) + other.astype(F32)
                    parts[i ^ (1 << bit)] = base if i == 1 << bit else base.astype(BF16)
        return parts[0]

    def group_gather(value):
        across = y_swap(value)
        return [value, tp_swap(value, 0), across, tp_swap(across, 0)]

    mine = nz // 2
    ids = (ic * mine + jnp.arange(mine, dtype=jnp.int32)) * 2 + iy
    if nz == 4:
        up0 = [(0, 1), (1, 2)]
        pairs = {
            "a": [((i, 0), (j, 0)) for i, j in up0] + [((3 - i, 1), (3 - j, 1)) for i, j in up0],
            "b": [((1, 0), (0, 0)), ((2, 1), (3, 1))],
            "c": [((i, 0), (j, 0)) for i, j in [(1, 2), (2, 3)]]
            + [((3 - i, 1), (3 - j, 1)) for i, j in [(1, 2), (2, 3)]],
            "d": [((2, 0), (3, 0)), ((1, 1), (0, 1))],
        }
        perms = {
            k: [(s[0] * 2 + s[1], d[0] * 2 + d[1]) for s, d in v] for k, v in pairs.items()
        }
        along = jnp.where(ic == 0, iz, 3 - iz)

        def spread(weight):
            a = lax.ppermute(weight, ("z", "c"), perms["a"])
            b = lax.ppermute(weight, ("z", "c"), perms["b"])
            c = lax.ppermute(a, ("z", "c"), perms["c"])
            d = lax.ppermute(c, ("z", "c"), perms["d"])
            outer = jnp.where(along == 0, weight, jnp.where(along == 1, a, jnp.where(along == 2, c, d)))
            inner = jnp.where(along == 0, b, jnp.where(along == 1, weight, jnp.where(along == 2, a, c)))
            low = jnp.where(ic == 0, outer, inner)
            high = jnp.where(ic == 0, inner, outer)
            return jnp.concatenate([low, high], axis=0)

    else:

        def spread(weight):
            every = lax.all_gather(weight, "z", axis=0, tiled=True)
            return lax.dynamic_slice_in_dim(every, ic * mine, mine, 0)

    wg, wu, wd = spread(w_gate), spread(w_up), spread(w_down)
    dy_group = jnp.concatenate(group_gather(grad_out), axis=0)
    routes_group = jnp.concatenate(group_gather(routes), axis=0)

    x = tokens.astype(F32)
    r1 = lax.rsqrt(jnp.mean(x * x, axis=-1, keepdims=True) + EPSILON)
    h1 = (x * r1 * norm1_gain).astype(BF16)
    h_all = tp_gather(h1)
    w_all = jnp.concatenate([w_query, key_weight, value_weight], axis=1)
    w_all_t = w_all.T
    total = rows * blocks
    order = me ^ jnp.arange(blocks, dtype=jnp.int32)
    position = (order[:, None] * rows + jnp.arange(rows, dtype=jnp.int32)[None, :]).reshape(total)
    frequency = ROPE_BASE ** (-(jnp.arange(HALF, dtype=F32) * (2.0 / HEAD_SIZE)))
    angles = frequency[:, None] * position.astype(F32)[None, :]
    cos, sin = jnp.cos(angles), jnp.sin(angles)
    scalars = jnp.concatenate(
        [me.astype(jnp.int32)[None], piece_first_position[0], piece_length[0]]
    )
    q, k, kt, v, vt = project_qkv(h_all, w_all_t, cos, sin, rows, q_cols, kv_cols)
    o, lse = attend(scalars, q, k, vt, rows, zone)
    out_parts = [
        dot(o[:, i * rows : (i + 1) * rows], w_out, 0, 0).astype(BF16) for i in range(blocks)
    ]
    x1 = x + tp_scatter(out_parts)
    r2 = lax.rsqrt(jnp.mean(x1 * x1, axis=-1, keepdims=True) + EPSILON)
    n2 = x1 * r2
    h2 = (n2 * norm2_gain).astype(BF16)

    router_wide = jnp.pad(w_router, ((0, 0), (0, LANES - experts)))
    h2_group = group_gather(h2)
    mixes, dhs, dgates, gates, acts, dgus = [], [], [], [], [], []
    for first in (0, 2):
        part = slice(first * rows, (first + 2) * rows)
        results = run_experts(
            ids,
            jnp.concatenate(h2_group[first : first + 2], axis=0),
            dy_group[part],
            routes_group[part],
            router_wide,
            wg,
            wu,
            wd,
            experts,
            rows,
        )
        for store, value in zip((mixes, dhs, dgates, gates, acts, dgus), results):
            store.append(value)

    def group_scatter(near, far, kind):
        own, core = near[:rows], near[rows:]
        side, cross = far[:rows], far[rows:]
        side = (side.astype(F32) + tp_swap(cross, 0).astype(F32)).astype(kind)
        side = y_swap(side)
        return own.astype(F32) + tp_swap(core, 0).astype(F32) + side.astype(F32)

    dh2_routes = group_scatter(dhs[0], dhs[1], BF16)
    dprobs = group_scatter(dgates[0], dgates[1], F32)[:, :experts]
    output = x1 + group_scatter(mixes[0], mixes[1], BF16)

    logits = dot(h2, w_router)
    probs = jax.nn.softmax(logits, axis=-1)
    dlogits = (
        probs * (dprobs - jnp.sum(probs * dprobs, axis=-1, keepdims=True))
    ).astype(BF16)
    router_part = dot(h2, dlogits, 0, 0)
    dh2 = dot(dlogits, w_router, 1, 1) + dh2_routes
    gain2_part = jnp.sum(dh2 * n2, axis=0)
    scaled = dh2 * norm2_gain
    dx1 = grad_out.astype(F32) + r2 * (
        scaled - n2 * jnp.mean(scaled * n2, axis=-1, keepdims=True)
    )

    da_all = tp_gather(dx1.astype(BF16))
    do = dot(w_out, da_all, 1, 1).astype(BF16)
    dq, dkv = attend_back(scalars, q, o, do, lse, k, kt, v, cos, sin, rows, zone)
    dqkv = jnp.concatenate([dq, dkv], axis=0)
    dh1_parts = [
        dot(dqkv[:, i * rows : (i + 1) * rows], w_all_t, 0, 0).astype(BF16) for i in range(blocks)
    ]
    dh1 = tp_scatter(dh1_parts)
    n1 = x * r1
    scaled = dh1 * norm1_gain
    grad_input = dx1 + r1 * (scaled - n1 * jnp.mean(scaled * n1, axis=-1, keepdims=True))

    grad_all = lax.dot_general(h_all, dqkv, (((0,), (1,)), ((), ())), preferred_element_type=F32)
    gain1_part = jnp.sum(grad_all * w_all.astype(F32), axis=1) / norm1_gain
    grad_qkv = lax.psum_scatter(
        grad_all.astype(BF16), ("z", "y"), scatter_dimension=0, tiled=True
    ).astype(F32)
    out_grad = lax.dot_general(da_all, o, (((0,), (1,)), ((), ())), preferred_element_type=F32)
    grad_outproj = lax.psum_scatter(
        out_grad.astype(BF16), ("z", "y"), scatter_dimension=0, tiled=True
    ).astype(F32).T

    stacked = expert_grads(
        ids,
        jnp.concatenate(h2_group, axis=0),
        dy_group,
        jnp.concatenate(gates, axis=0),
        jnp.concatenate(acts, axis=1),
        jnp.concatenate(dgus, axis=1),
        rows,
    )
    if nz == 4:
        part = lax.psum_scatter(
            stacked.reshape(mine * width, 3 * hidden), "z", scatter_dimension=0, tiled=True
        )
        part = lax.psum_scatter(part, "x", scatter_dimension=0, tiled=True)
        perm = []
        for z in range(4):
            for xx in range(2):
                for cc in range(2):
                    perm.append((z * 4 + xx * 2 + cc, (2 * cc + z // 2) * 4 + (z % 2) * 2 + xx))
        part = lax.ppermute(part, ("z", "x", "c"), perm)
    else:
        every = jnp.zeros((nz, width, 3 * hidden), BF16)
        every = lax.dynamic_update_slice_in_dim(every, stacked, ic * mine, 0)
        part = lax.psum_scatter(
            every.reshape(nz * width, 3 * hidden), "z", scatter_dimension=0, tiled=True
        )
        part = lax.psum_scatter(part, ("x", "c"), scatter_dimension=0, tiled=True)
    part = part.astype(F32)
    grad_gate = part[None, :, :hidden]
    grad_up = part[None, :, hidden : 2 * hidden]
    grad_down = part[:, 2 * hidden :].T[None]

    every_axis = ("z", "y", "x", "c")
    small = jnp.concatenate([router_part, gain2_part[:, None]], axis=1)
    small = lax.psum_scatter(small, every_axis, scatter_dimension=0, tiled=True)
    grad_norm1 = lax.psum_scatter(gain1_part, every_axis, scatter_dimension=0, tiled=True)
    return (
        output,
        grad_input,
        grad_norm1,
        grad_qkv[:, :q_cols],
        grad_qkv[:, q_cols : q_cols + kv_cols],
        grad_qkv[:, q_cols + kv_cols :],
        grad_outproj,
        small[:, experts],
        small[:, :experts],
        grad_gate,
        grad_up,
        grad_down,
    )


def solution(mesh):
    ep, tp = mesh.shape["ep"], mesh.shape["tp"]
    nz, nx = ep // 2, tp // 2
    grid = Mesh(mesh.devices.reshape(nz, 2, nx, 2), ("z", "y", "x", "c"))
    e, t = ("z", "y"), ("x", "c")
    every = ("z", "y", "x", "c")
    return jax.shard_map(
        functools.partial(body, (nz, nx)),
        mesh=grid,
        in_specs=(
            P(every, None),
            P(),
            P(None, t),
            P(None, t),
            P(None, t),
            P(t, None),
            P(),
            P(),
            P(e, None, None),
            P(e, None, None),
            P(e, None, None),
            P(every, None),
            P(e, None),
            P(e, None),
            P(every, None),
        ),
        out_specs=(
            P(every, None),
            P(every, None),
            P(every),
            P(e, t),
            P(e, t),
            P(e, t),
            P(t, e),
            P(every),
            P(every, None),
            P(e, t, None),
            P(e, t, None),
            P(e, None, t),
        ),
        check_vma=False,
    )
```

```python
import functools
import math

import jax
import jax.numpy as jnp
from jax import lax
from jax.experimental import pallas as pl
from jax.experimental.pallas import tpu as pltpu
from jax.sharding import Mesh, PartitionSpec as P

HEAD_SIZE = 64
HALF = HEAD_SIZE // 2
SEQUENCE_LENGTH = 2048
EPSILON = 1e-05
ROPE_BASE = 10000.0
MASK_FILL = -1e30
LANES = 128
F32 = jnp.float32
BF16 = jnp.bfloat16
VMEM_LIMIT = 60 * 1024 * 1024


def dot(a, b, ca=1, cb=0):
    return lax.dot_general(a, b, (((ca,), (cb,)), ((), ())), preferred_element_type=F32)


def after(value, *deps):
    return lax.optimization_barrier((value, *deps))[0]


def cost(micros):
    return pl.CostEstimate(
        flops=int(micros * 1e9), transcendentals=0, bytes_accessed=int(micros * 3e6)
    )


def params():
    return pltpu.CompilerParams(vmem_limit_bytes=VMEM_LIMIT)


def once(shape):
    return pl.BlockSpec(shape, lambda *_: (0,) * len(shape), pipeline_mode=pl.Buffered(1))


def qkv_kernel(q_cols, kv_cols, parts, *refs):
    h_refs, (w_ref, cos_ref, sin_ref) = refs[:parts], refs[parts : parts + 3]
    q_ref, k_ref, kt_ref, v_ref, vt_ref = refs[-5:]
    rows = h_refs[0].shape[0]
    scale = jnp.asarray(1.0 / math.sqrt(HEAD_SIZE), BF16)
    for b in range(parts):
        here = slice(b * rows, (b + 1) * rows)
        y = dot(w_ref[...], h_refs[b][...], 1, 1)
        cos, sin = cos_ref[:, here], sin_ref[:, here]

        def turned(base):
            a = y[base : base + HALF]
            b = y[base + HALF : base + HEAD_SIZE]
            return jnp.concatenate([a * cos - b * sin, b * cos + a * sin], axis=0)

        for h in range(q_cols // HEAD_SIZE):
            base = h * HEAD_SIZE
            q_ref[base : base + HEAD_SIZE, here] = turned(base).astype(BF16) * scale
        for g in range(kv_cols // HEAD_SIZE):
            base = g * HEAD_SIZE
            kt = turned(q_cols + base)
            kt_ref[base : base + HEAD_SIZE, here] = kt.astype(BF16)
            k_ref[g, here, :] = kt.T.astype(BF16)
            vt = y[q_cols + kv_cols + base : q_cols + kv_cols + base + HEAD_SIZE]
            vt_ref[base : base + HEAD_SIZE, here] = vt.astype(BF16)
            v_ref[g, here, :] = vt.T.astype(BF16)


def project_qkv(h_parts, w_all, cos, sin, q_cols, kv_cols, half, previous):
    parts = len(h_parts)
    rows, width = h_parts[0].shape
    size = parts * rows
    groups = kv_cols // HEAD_SIZE
    cols = q_cols + 2 * kv_cols
    lane_block = lambda *_: (0, half)
    row_block = lambda *_: (0, half, 0)
    kv_shapes = [
        jax.ShapeDtypeStruct((groups, 2 * size, HEAD_SIZE), BF16),
        jax.ShapeDtypeStruct((kv_cols, 2 * size), BF16),
    ] * 2
    kv_specs = [
        pl.BlockSpec((groups, size, HEAD_SIZE), row_block),
        pl.BlockSpec((kv_cols, size), lane_block),
    ] * 2
    previous = list(previous or ())
    return pl.pallas_call(
        functools.partial(qkv_kernel, q_cols, kv_cols, parts),
        grid=(1,),
        in_specs=[once((rows, width))] * parts
        + [
            once((cols, width)),
            pl.BlockSpec((HALF, size), lane_block),
            pl.BlockSpec((HALF, size), lane_block),
        ]
        + [pl.BlockSpec(memory_space=pl.ANY)] * len(previous),
        out_specs=[once((q_cols, size))] + kv_specs,
        out_shape=[jax.ShapeDtypeStruct((q_cols, size), BF16)] + kv_shapes,
        input_output_aliases={parts + 3 + i: 1 + i for i in range(len(previous))},
        compiler_params=params(),
        cost_estimate=cost(6),
        name="qkv",
    )(*h_parts, w_all, cos, sin, *previous)


def last_key(s_ref, zone, own, rows):
    zone_index = own * rows // zone
    zones = SEQUENCE_LENGTH // zone
    start = s_ref[1 + zone_index]
    stop = start + s_ref[1 + zones + zone_index]
    position = own * rows + lax.broadcasted_iota(jnp.int32, (1, rows), 1)
    return jnp.where((position >= start) & (position < stop), stop - 1, position)


def block_walk(me, own, rows, zone, pair):
    per_zone = zone // rows
    pair(own, True, True)
    for other in range(1, per_zone):
        pair(own ^ other, True, False)
    first = (own // per_zone) * per_zone

    def step(key_block, carry):
        pair(key_block, False, False)
        return carry

    lax.fori_loop(0, first, step, 0)


def attend_kernel(
    rows, zone, heads, groups, base, s_ref, q_ref, k_ref, vt_ref, w_ref, o_ref, lse_ref, *refs
):
    out_refs, (acc, top, total) = refs[:-3], refs[-3:]
    me = s_ref[0]
    own = me ^ (pl.program_id(0) + base)
    limit = last_key(s_ref, zone, own, rows)

    def pair(key_block, masked, first):
        offset = pl.multiple_of((me ^ key_block) * rows, rows)
        if masked:
            key_pos = key_block * rows + lax.broadcasted_iota(jnp.int32, (rows, rows), 0)
            allowed = key_pos <= limit
        for h in range(heads):
            g = h // (heads // groups)
            r = slice(h * HEAD_SIZE, (h + 1) * HEAD_SIZE)
            s = dot(k_ref[g, pl.ds(offset, rows), :], q_ref[r, :])
            if masked:
                s = jnp.where(allowed, s, MASK_FILL)
            peak = jnp.max(s, axis=0, keepdims=True)
            vt = vt_ref[g * HEAD_SIZE : (g + 1) * HEAD_SIZE, pl.ds(offset, rows)]
            if first:
                p = jnp.exp(s - peak)
                top[h : h + 1, :] = peak
                total[h : h + 1, :] = jnp.sum(p, axis=0, keepdims=True)
                acc[r, :] = dot(vt, p.astype(BF16))
            else:
                old = top[h : h + 1, :]
                new = jnp.maximum(old, peak)
                fade = jnp.exp(old - new)
                p = jnp.exp(s - new)
                top[h : h + 1, :] = new
                total[h : h + 1, :] = total[h : h + 1, :] * fade + jnp.sum(p, axis=0, keepdims=True)
                acc[r, :] = acc[r, :] * fade + dot(vt, p.astype(BF16))

    block_walk(me, own, rows, zone, pair)
    for h in range(heads):
        r = slice(h * HEAD_SIZE, (h + 1) * HEAD_SIZE)
        o_ref[r, :] = (acc[r, :] / total[h : h + 1, :]).astype(BF16)
        lse_ref[h : h + 1, :] = top[h : h + 1, :] + jnp.log(total[h : h + 1, :])
    for b, out_ref in enumerate(out_refs):

        @pl.when(pl.program_id(0) == b)
        def _():
            out_ref[...] = dot(o_ref[...], w_ref[...], 0, 0).astype(BF16)


def attend(scalars, q, at, count, k, vt, w_out, rows, zone, base):
    q_cols = q.shape[0]
    size = count * rows
    groups = k.shape[0]
    width = w_out.shape[1]
    heads = q_cols // HEAD_SIZE
    block = lambda i, s: (0, i)
    return pl.pallas_call(
        functools.partial(attend_kernel, rows, zone, heads, groups, base),
        grid_spec=pltpu.PrefetchScalarGridSpec(
            num_scalar_prefetch=1,
            grid=(count,),
            in_specs=[
                pl.BlockSpec((q_cols, rows), lambda i, s: (0, i + at)),
                once(k.shape),
                once(vt.shape),
                once(w_out.shape),
            ],
            out_specs=[
                pl.BlockSpec((q_cols, rows), block),
                pl.BlockSpec((heads, rows), block),
            ]
            + [once((rows, width))] * count,
            scratch_shapes=[
                pltpu.VMEM((q_cols, rows), F32),
                pltpu.VMEM((8, rows), F32),
                pltpu.VMEM((8, rows), F32),
            ],
        ),
        out_shape=[
            jax.ShapeDtypeStruct((q_cols, size), BF16),
            jax.ShapeDtypeStruct((heads, size), F32),
        ]
        + [jax.ShapeDtypeStruct((rows, width), BF16)] * count,
        compiler_params=params(),
        cost_estimate=cost(9 * count),
        name="attend",
    )(scalars, q, k, vt, w_out)


def attend_back_kernel(rows, zone, heads, groups, base, parts, *refs):
    s_ref, q_ref, o_ref, lse_ref, k_ref, kt_ref, v_ref, cos_ref, sin_ref, w_ref = refs[:10]
    da_refs = refs[10 : 10 + parts]
    rest = refs[10 + parts :]
    if base:
        old_dk, old_dv, dq_ref, dkv_ref, dq, dk, dv, delta, do_ref = rest
    else:
        dq_ref, dk, dv, dq, delta, do_ref = rest
    me = s_ref[0]
    step = pl.program_id(0)
    own = me ^ (step + base)
    limit = last_key(s_ref, zone, own, rows)
    here = pl.multiple_of((step + base) * rows, rows)

    @pl.when(step == 0)
    def _():
        for b in range(parts):
            do_ref[b] = dot(w_ref[...], da_refs[b][...], 1, 1).astype(BF16)
        if base:
            dk[...] = old_dk[...]
            dv[...] = old_dv[...]
        else:
            dk[...] = jnp.zeros_like(dk)
            dv[...] = jnp.zeros_like(dv)

    for h in range(heads):
        r = slice(h * HEAD_SIZE, (h + 1) * HEAD_SIZE)
        delta[h : h + 1, :] = jnp.sum(
            do_ref[step, r, :].astype(F32) * o_ref[r, :].astype(F32), axis=0, keepdims=True
        )

    def pair(key_block, masked, first):
        offset = pl.multiple_of((me ^ key_block) * rows, rows)
        keys = pl.ds(offset, rows)
        if masked:
            key_pos = key_block * rows + lax.broadcasted_iota(jnp.int32, (rows, rows), 0)
            allowed = key_pos <= limit
        for g in range(groups):
            kb = k_ref[g, keys, :]
            vb = v_ref[g, keys, :]
            kt = kt_ref[g * HEAD_SIZE : (g + 1) * HEAD_SIZE, keys]
            dk_sum = dk[g, keys, :]
            dv_sum = dv[g, keys, :]
            for h in range(g * (heads // groups), (g + 1) * (heads // groups)):
                r = slice(h * HEAD_SIZE, (h + 1) * HEAD_SIZE)
                do = do_ref[step, r, :]
                s = dot(kb, q_ref[r, :])
                if masked:
                    s = jnp.where(allowed, s, MASK_FILL)
                p = jnp.exp(s - lse_ref[h : h + 1, :])
                dp = dot(vb, do)
                ds = (p * (dp - delta[h : h + 1, :])).astype(BF16)
                dv_sum = dv_sum + dot(p.astype(BF16), do, 1, 1)
                dk_sum = dk_sum + dot(ds, q_ref[r, :], 1, 1)
                part = dot(kt, ds)
                dq[r, :] = part if first else dq[r, :] + part
            dk[g, keys, :] = dk_sum
            dv[g, keys, :] = dv_sum

    block_walk(me, own, rows, zone, pair)
    cos, sin = cos_ref[:, pl.ds(here, rows)], sin_ref[:, pl.ds(here, rows)]
    scale = 1.0 / math.sqrt(HEAD_SIZE)
    for h in range(heads):
        at = h * HEAD_SIZE
        a = dq[at : at + HALF, :] * scale
        b = dq[at + HALF : at + HEAD_SIZE, :] * scale
        dq_ref[at : at + HALF, :] = (a * cos + b * sin).astype(BF16)
        dq_ref[at + HALF : at + HEAD_SIZE, :] = (b * cos - a * sin).astype(BF16)

    if base:

        @pl.when(step == pl.num_programs(0) - 1)
        def _():
            every_cos, every_sin = cos_ref[...], sin_ref[...]
            for g in range(groups):
                at = g * HEAD_SIZE
                turned = dk[g].T
                a, b = turned[:HALF], turned[HALF:]
                dkv_ref[at : at + HALF, :] = (a * every_cos + b * every_sin).astype(BF16)
                dkv_ref[at + HALF : at + HEAD_SIZE, :] = (b * every_cos - a * every_sin).astype(BF16)
                at = (groups + g) * HEAD_SIZE
                dkv_ref[at : at + HEAD_SIZE, :] = dv[g].T.astype(BF16)


def attend_back(scalars, q, o, lse, k, kt, v, cos, sin, w_out, da_parts, rows, zone, base, sums):
    q_cols, size = q.shape
    groups, total, _ = k.shape
    heads = q_cols // HEAD_SIZE
    parts = len(da_parts)
    block = lambda i, s: (0, i)
    sum_shape = (groups, total, HEAD_SIZE)
    inputs = [q, o, lse, k, kt, v, cos, sin, w_out, *da_parts]
    in_specs = [
        pl.BlockSpec((q_cols, rows), block),
        pl.BlockSpec((q_cols, rows), block),
        pl.BlockSpec((heads, rows), block),
    ] + [once(a.shape) for a in inputs[3:]]
    out_specs = [pl.BlockSpec((q_cols, rows), block)]
    out_shape = [jax.ShapeDtypeStruct((q_cols, size), BF16)]
    scratch = [pltpu.VMEM((q_cols, rows), F32)]
    if base:
        inputs += list(sums)
        in_specs += [once(sum_shape)] * 2
        out_specs += [once((2 * groups * HEAD_SIZE, total))]
        out_shape += [jax.ShapeDtypeStruct((2 * groups * HEAD_SIZE, total), BF16)]
        scratch += [pltpu.VMEM(sum_shape, F32)] * 2
    else:
        out_specs += [once(sum_shape)] * 2
        out_shape += [jax.ShapeDtypeStruct(sum_shape, F32)] * 2
    scratch += [pltpu.VMEM((8, rows), F32), pltpu.VMEM((parts, q_cols, rows), BF16)]
    return pl.pallas_call(
        functools.partial(attend_back_kernel, rows, zone, heads, groups, base, parts),
        grid_spec=pltpu.PrefetchScalarGridSpec(
            num_scalar_prefetch=1,
            grid=(size // rows,),
            in_specs=in_specs,
            out_specs=out_specs,
            scratch_shapes=scratch,
        ),
        out_shape=out_shape,
        compiler_params=params(),
        cost_estimate=cost(30),
        name="attend_back",
    )(scalars, *inputs)


def input_grad_kernel(dq_ref, dkv_ref, w_ref, *out_refs):
    q_cols = dq_ref.shape[0]
    rows = out_refs[0].shape[0]
    for b, out_ref in enumerate(out_refs):
        here = slice(b * rows, (b + 1) * rows)
        out = dot(dq_ref[:, here], w_ref[:q_cols, :], 0, 0)
        out = out + dot(dkv_ref[:, here], w_ref[q_cols:, :], 0, 0)
        out_ref[...] = out.astype(BF16)


def input_grads(dq, dkv, w_all_t, rows, half):
    q_cols, size = dq.shape
    cols, width = w_all_t.shape
    count = size // rows
    return pl.pallas_call(
        input_grad_kernel,
        grid=(1,),
        in_specs=[
            once((q_cols, size)),
            pl.BlockSpec((cols - q_cols, size), lambda i: (0, half)),
            once((cols, width)),
        ],
        out_specs=[once((rows, width))] * count,
        out_shape=[jax.ShapeDtypeStruct((rows, width), BF16)] * count,
        compiler_params=params(),
        cost_estimate=cost(5),
        name="input_grads",
    )(dq, dkv, w_all_t)


def qkv_grad_kernel(parts, *refs):
    h_refs = refs[: 2 * parts]
    near_ref, far_ref, dkv_ref, w_ref, gain_ref, grad_ref, gain_grad_ref = refs[2 * parts :]
    rows = h_refs[0].shape[0]
    sums = [0.0, 0.0]
    for b in range(2 * parts):
        dq_ref, at = (near_ref, b) if b < parts else (far_ref, b - parts)
        h = h_refs[b][...]
        sums[0] = sums[0] + dot(dq_ref[:, at * rows : (at + 1) * rows], h)
        sums[1] = sums[1] + dot(dkv_ref[:, b * rows : (b + 1) * rows], h)
    q_cols = near_ref.shape[0]
    grad_ref[:, :q_cols] = sums[0].T.astype(BF16)
    grad_ref[:, q_cols:] = sums[1].T.astype(BF16)
    gain = jnp.sum(sums[0] * w_ref[:q_cols, :].astype(F32), axis=0, keepdims=True)
    gain = gain + jnp.sum(sums[1] * w_ref[q_cols:, :].astype(F32), axis=0, keepdims=True)
    gain_grad_ref[...] = gain / gain_ref[...]


def qkv_grads(h_parts, dq_near, dq_far, dkv, w_all_t, gain):
    cols, width = w_all_t.shape
    inputs = [*h_parts, dq_near, dq_far, dkv, w_all_t, gain[None, :]]
    return pl.pallas_call(
        functools.partial(qkv_grad_kernel, len(h_parts) // 2),
        grid=(1,),
        in_specs=[once(a.shape) for a in inputs],
        out_specs=[once((width, cols)), once((1, width))],
        out_shape=[
            jax.ShapeDtypeStruct((width, cols), BF16),
            jax.ShapeDtypeStruct((1, width), F32),
        ],
        compiler_params=params(),
        cost_estimate=cost(10),
        name="qkv_grads",
    )(*inputs)


def out_grad_kernel(parts, finish, *refs):
    da_refs, o_ref, grad_ref = refs[:parts], refs[parts], refs[-1]
    rows = da_refs[0].shape[0]
    total = refs[parts + 1][...] if finish else 0.0
    for b in range(parts):
        total = total + dot(o_ref[:, b * rows : (b + 1) * rows], da_refs[b][...])
    grad_ref[...] = total.T.astype(BF16) if finish else total


def out_grads(da_parts, o, previous):
    q_cols, width = o.shape[0], da_parts[0].shape[1]
    inputs = [*da_parts, o] + ([] if previous is None else [previous])
    finish = previous is not None
    shape = (width, q_cols) if finish else (q_cols, width)
    return pl.pallas_call(
        functools.partial(out_grad_kernel, len(da_parts), finish),
        grid=(1,),
        in_specs=[once(a.shape) for a in inputs],
        out_specs=once(shape),
        out_shape=jax.ShapeDtypeStruct(shape, BF16 if finish else F32),
        compiler_params=params(),
        cost_estimate=cost(4),
        name="out_grads",
    )(*inputs)


def expert_kernel(experts, adds, choices, *refs):
    s_ref, h0, h1, dy0, dy1, router_ref = refs[:6]
    w_choices = refs[6 : 6 + choices]
    old = refs[6 + choices : 6 + choices + (4 if adds else 0)]
    outs = refs[len(refs) - 19 :]
    mix0, mix1, dh0, dh1, act_out, dgu_out = outs[:6]
    h_s, dy_s, w_s, mix_s, dh_s, gates, dgate, mix_o, dh_o, act_o, dgu_o, in_sem, out_sem = outs[6:]
    e = pl.program_id(0)
    last = pl.num_programs(0) - 1
    rows, width = h0.shape
    hidden = w_s.shape[2] // 3
    lane = lax.broadcasted_iota(jnp.int32, (rows, LANES), 1)
    slot = lax.rem(e, 2)

    def fetch_weights(index, into):
        for n in range(choices):

            @pl.when(s_ref[0] == n)
            def _():
                pltpu.make_async_copy(
                    w_choices[n].at[index], w_s.at[into], in_sem.at[4 + into]
                ).start()

    tokens_in = [
        pltpu.make_async_copy(src, dst, in_sem.at[n])
        for n, (src, dst) in enumerate(
            ((h0, h_s.at[0]), (dy0, dy_s.at[0]), (h1, h_s.at[1]), (dy1, dy_s.at[1]))
        )
    ]
    old_in = [
        pltpu.make_async_copy(src, dst, in_sem.at[6 + n])
        for n, (src, dst) in enumerate(zip(old, (mix_o.at[0], mix_o.at[1], dh_o.at[0], dh_o.at[1])))
    ]

    @pl.when(e == 0)
    def _():
        tokens_in[0].start()
        fetch_weights(0, 0)
        for copy in tokens_in[1:] + old_in:
            copy.start()

    @pl.when(e < last)
    def _():
        fetch_weights(e + 1, 1 - slot)

    for i in range(2):

        @pl.when(e == 0)
        def _():
            tokens_in[2 * i].wait()
            logits = dot(h_s[i], router_ref[...])
            logits = jnp.where(lane < experts, logits, MASK_FILL)
            weights = jnp.exp(logits - jnp.max(logits, axis=1, keepdims=True))
            weights = weights / jnp.sum(weights, axis=1, keepdims=True)
            tokens_in[2 * i + 1].wait()
            gates[i] = weights * dy_s[i, :, width:].astype(F32)

        if i == 0:
            pltpu.make_async_copy(w_choices[0].at[0], w_s.at[slot], in_sem.at[4 + slot]).wait()
        mine = lane == s_ref[1 + e]
        gate = jnp.sum(jnp.where(mine, gates[i], 0.0), axis=1, keepdims=True)
        both = dot(h_s[i], w_s[slot, :, : 2 * hidden])
        gp, up = both[:, :hidden], both[:, hidden:]
        sg = jax.nn.sigmoid(gp)
        silu = gp * sg
        act = (silu * up).astype(BF16).astype(F32)
        dact = dot(dy_s[i, :, :width], w_s[slot, :, 2 * hidden :])
        chosen = dy_s[i, :, width:].astype(F32)
        own_dgate = jnp.where(mine, chosen * jnp.sum(act * dact, axis=1, keepdims=True), 0.0)
        scaled = (gate * act).astype(BF16)
        dact = gate * dact
        dgp = (dact * up * sg * (1.0 + gp * (1.0 - sg))).astype(BF16)
        dup = (dact * silu).astype(BF16)

        @pl.when(e > 0)
        def _():
            pltpu.make_async_copy(
                act_o.at[i], act_out.at[0, pl.ds(0, rows), :], out_sem.at[i]
            ).wait()
            pltpu.make_async_copy(
                dgu_o.at[i], dgu_out.at[0, pl.ds(0, rows), :], out_sem.at[2 + i]
            ).wait()

        act_o[i] = scaled
        dgu_o[i, :, :hidden] = dgp
        dgu_o[i, :, hidden:] = dup
        here = pl.ds(i * rows, rows)
        pltpu.make_async_copy(act_o.at[i], act_out.at[e, here, :], out_sem.at[i]).start()
        pltpu.make_async_copy(dgu_o.at[i], dgu_out.at[e, here, :], out_sem.at[2 + i]).start()
        mix = dot(scaled, w_s[slot, :, 2 * hidden :], 1, 1)
        dh = dot(dgu_o[i], w_s[slot, :, : 2 * hidden], 1, 1)

        @pl.when(e == 0)
        def _():
            if adds:
                old_in[i].wait()
                old_in[2 + i].wait()
                mix_s[i] = mix + mix_o[i].astype(F32)
                dh_s[i] = dh + dh_o[i, :, :width].astype(F32)
                kept = dh_o[i, :, width:].astype(F32)
                kept = kept + pltpu.roll(kept, LANES // 2, 1)
                dgate[i] = own_dgate + jnp.where(lane < LANES // 2, kept, 0.0)
            else:
                mix_s[i] = mix
                dh_s[i] = dh
                dgate[i] = own_dgate

        @pl.when(e > 0)
        def _():
            mix_s[i] += mix
            dh_s[i] += dh
            dgate[i] += own_dgate

        @pl.when(e == last)
        def _():
            mix_o[i] = mix_s[i].astype(BF16)
            dh_o[i, :, :width] = dh_s[i].astype(BF16)
            high = dgate[i].astype(BF16).astype(F32)
            low = dgate[i] - high
            dh_o[i, :, width:] = (high + pltpu.roll(low, LANES // 2, 1)).astype(BF16)
            pltpu.make_async_copy(mix_o.at[i], (mix0, mix1)[i], out_sem.at[4 + i]).start()
            pltpu.make_async_copy(dh_o.at[i], (dh0, dh1)[i], out_sem.at[6 + i]).start()

    @pl.when(e == last)
    def _():
        for i in range(2):
            here = pl.ds(i * rows, rows)
            pltpu.make_async_copy(act_o.at[i], act_out.at[e, here, :], out_sem.at[i]).wait()
            pltpu.make_async_copy(dgu_o.at[i], dgu_out.at[e, here, :], out_sem.at[2 + i]).wait()
            pltpu.make_async_copy(mix_o.at[i], (mix0, mix1)[i], out_sem.at[4 + i]).wait()
            pltpu.make_async_copy(dh_o.at[i], (dh0, dh1)[i], out_sem.at[6 + i]).wait()


def run_experts(scalars, h_parts, dy_parts, router, choices, experts, micros, old=()):
    rows, width = h_parts[0].shape
    wide = width + LANES
    mine, _, cols = choices[0].shape
    hidden = cols // 3
    anywhere = pl.BlockSpec(memory_space=pl.ANY)
    return pl.pallas_call(
        functools.partial(expert_kernel, experts, bool(old), len(choices)),
        grid_spec=pltpu.PrefetchScalarGridSpec(
            num_scalar_prefetch=1,
            grid=(mine,),
            in_specs=[anywhere] * 4 + [once((width, LANES))] + [anywhere] * (len(choices) + len(old)),
            out_specs=[anywhere] * 6,
            scratch_shapes=[
                pltpu.VMEM((2, rows, width), BF16),
                pltpu.VMEM((2, rows, wide), BF16),
                pltpu.VMEM((2, width, cols), BF16),
                pltpu.VMEM((2, rows, width), F32),
                pltpu.VMEM((2, rows, width), F32),
                pltpu.VMEM((2, rows, LANES), F32),
                pltpu.VMEM((2, rows, LANES), F32),
                pltpu.VMEM((2, rows, width), BF16),
                pltpu.VMEM((2, rows, wide), BF16),
                pltpu.VMEM((2, rows, hidden), BF16),
                pltpu.VMEM((2, rows, 2 * hidden), BF16),
                pltpu.SemaphoreType.DMA((10,)),
                pltpu.SemaphoreType.DMA((8,)),
            ],
        ),
        out_shape=[jax.ShapeDtypeStruct((rows, width), BF16)] * 2
        + [jax.ShapeDtypeStruct((rows, wide), BF16)] * 2
        + [
            jax.ShapeDtypeStruct((mine, 2 * rows, hidden), BF16),
            jax.ShapeDtypeStruct((mine, 2 * rows, 2 * hidden), BF16),
        ],
        compiler_params=params(),
        cost_estimate=cost(micros),
        name="experts",
    )(scalars, *h_parts, *dy_parts, router, *choices, *old)


def expert_grad_kernel(*refs):
    h_refs, dy_refs, acts, dgus = refs[:4], refs[4:8], refs[8:10], refs[10:12]
    out_ref, h_s, dy_s, act_s, dgu_s, sem = refs[12:]
    e = pl.program_id(0)
    rows, width = h_refs[0].shape
    hidden = act_s.shape[1]
    first, second = [], []
    for b in range(4):
        here = pl.ds(b * rows, rows)
        first.append(pltpu.make_async_copy(h_refs[b], h_s.at[here, :], sem.at[b]))
        second.append(
            pltpu.make_async_copy(dy_refs[b].at[:, pl.ds(0, width)], dy_s.at[here, :], sem.at[4 + b])
        )
    per_expert = []
    for b in range(2):
        here = pl.ds(2 * b * rows, 2 * rows)
        per_expert.append(pltpu.make_async_copy(dgus[b].at[e], dgu_s.at[here, :], sem.at[8 + b]))
    for b in range(2):
        here = pl.ds(2 * b * rows, 2 * rows)
        per_expert.append(pltpu.make_async_copy(acts[b].at[e], act_s.at[here, :], sem.at[10 + b]))
    for copy in per_expert[:2]:
        copy.start()

    @pl.when(e == 0)
    def _():
        for copy in first:
            copy.start()

    for copy in per_expert[2:]:
        copy.start()

    @pl.when(e == 0)
    def _():
        for copy in second:
            copy.start()
        for copy in first:
            copy.wait()

    for copy in per_expert[:2]:
        copy.wait()
    out_ref[0, :, : 2 * hidden] = dot(h_s[...], dgu_s[...], 0, 0).astype(BF16)

    @pl.when(e == 0)
    def _():
        for copy in second:
            copy.wait()

    for copy in per_expert[2:]:
        copy.wait()
    out_ref[0, :, 2 * hidden :] = dot(dy_s[...], act_s[...], 0, 0).astype(BF16)


def expert_grads(h_parts, dy_parts, acts, dgus):
    rows, width = h_parts[0].shape
    mine, _, hidden = acts[0].shape
    anywhere = pl.BlockSpec(memory_space=pl.ANY)
    return pl.pallas_call(
        expert_grad_kernel,
        grid=(mine,),
        in_specs=[anywhere] * 12,
        out_specs=pl.BlockSpec((1, width, 3 * hidden), lambda e: (e, 0, 0)),
        out_shape=jax.ShapeDtypeStruct((mine, width, 3 * hidden), BF16),
        scratch_shapes=[
            pltpu.VMEM((4 * rows, width), BF16),
            pltpu.VMEM((4 * rows, width), BF16),
            pltpu.VMEM((4 * rows, hidden), BF16),
            pltpu.VMEM((4 * rows, 2 * hidden), BF16),
            pltpu.SemaphoreType.DMA((12,)),
        ],
        compiler_params=params(),
        cost_estimate=cost(15),
        name="expert_grads",
    )(*h_parts, *dy_parts, *acts, *dgus)


def body(
    sizes,
    tokens,
    norm1_gain,
    w_query,
    key_weight,
    value_weight,
    w_out,
    norm2_gain,
    w_router,
    w_gate,
    w_up,
    w_down,
    routes,
    piece_first_position,
    piece_length,
    grad_out,
):
    nz, nx = sizes
    rows, width = tokens.shape
    blocks = 2 * nx
    half = blocks // 2
    q_cols, kv_cols = w_query.shape[1], key_weight.shape[1]
    experts = w_router.shape[1]
    hidden = w_gate.shape[2]
    zone = SEQUENCE_LENGTH // piece_length.shape[1]
    iz, iy, ix, ic = (lax.axis_index(a) for a in "zyxc")
    me = ix * 2 + ic

    def tp_swap(value, bit):
        if bit == 0:
            return lax.ppermute(value, "c", [(0, 1), (1, 0)])
        return lax.ppermute(value, "x", [(i, i ^ (1 << (bit - 1))) for i in range(nx)])

    def y_swap(value):
        return lax.ppermute(value, "y", [(0, 1), (1, 0)])

    bits = blocks.bit_length() - 1

    def tp_gather(value):
        held = {0: value}
        for bit in reversed(range(bits)):
            for i in list(held):
                held[i | (1 << bit)] = tp_swap(held[i], bit)
        return [held[i] for i in range(blocks)]

    def tp_scatter(parts):
        parts = dict(enumerate(parts))
        for bit in range(bits):
            for i in sorted(parts, reverse=True):
                if i & (1 << bit):
                    parts[i] = tp_swap(parts[i], bit)
            for i in sorted(parts, reverse=True):
                if i & (1 << bit):
                    other = parts.pop(i)
                    base = parts[i ^ (1 << bit)].astype(F32) + other.astype(F32)
                    last = i == 1 << bit and bit == bits - 1
                    parts[i ^ (1 << bit)] = base if last else base.astype(BF16)
            if bit == bits - 2:
                side, own = parts[1 << (bits - 1)], parts[0]
        return parts[0], side, own

    def sum_all(value):
        for bit in range(bits):
            value = value + tp_swap(value, bit)
        value = value + y_swap(value)
        step = 1
        while step < nz:
            value = value + lax.ppermute(value, "z", [(i, i ^ step) for i in range(nz)])
            step *= 2
        return value

    def own_columns(value):
        each = width // (nz * 4 * nx)
        index = (iz * 2 + iy) * blocks + me
        return lax.dynamic_slice_in_dim(value, index * each, each, 1)

    x = tokens.astype(F32)
    r1 = lax.rsqrt(jnp.mean(x * x, axis=-1, keepdims=True) + EPSILON)
    h1 = (x * r1 * norm1_gain).astype(BF16)
    h_parts = tp_gather(h1)

    w_all_t = jnp.concatenate([w_query, key_weight, value_weight], axis=1).T
    order = me ^ jnp.arange(blocks, dtype=jnp.int32)
    position = (order[:, None] * rows + jnp.arange(rows, dtype=jnp.int32)[None, :]).reshape(-1)
    frequency = ROPE_BASE ** (-(jnp.arange(HALF, dtype=F32) * (2.0 / HEAD_SIZE)))
    angles = frequency[:, None] * position.astype(F32)[None, :]
    cos, sin = jnp.cos(angles), jnp.sin(angles)
    scalars = jnp.concatenate(
        [me.astype(jnp.int32)[None], piece_first_position[0], piece_length[0]]
    )
    q_near, *kv = project_qkv(h_parts[:half], w_all_t, cos, sin, q_cols, kv_cols, 0, None)

    mask = jnp.zeros((rows, LANES), jnp.bool_)
    for j in range(routes.shape[1]):
        mask = mask | (routes[:, j : j + 1] == jnp.arange(LANES, dtype=jnp.int32)[None, :])
    dy_own = after(jnp.concatenate([grad_out, mask.astype(BF16)], axis=1), q_near)
    dy_side = y_swap(dy_own)

    mine = nz // 2
    cut = mine // 2
    weight = after(jnp.concatenate([w_gate[0], w_up[0], w_down[0].T], axis=1), q_near)[None]
    if nz == 4:
        ids = jnp.where(ic == 0, jnp.arange(2), 3 - jnp.arange(2)) * 2 + iy
        along = jnp.where(ic == 0, iz, 3 - iz)

        def shift(value, moves):
            perm = [(s * 2, d * 2) for s, d in moves]
            perm += [((3 - s) * 2 + 1, (3 - d) * 2 + 1) for s, d in moves]
            return lax.ppermute(value, ("z", "c"), perm)

        from_outer = shift(weight, [(0, 1), (1, 2)])
        from_inner = shift(weight, [(1, 0)])
    else:
        ids = (ic * mine + jnp.arange(mine)) * 2 + iy
        along = ic * 0

    q_far, k, kt, v, vt = project_qkv(h_parts[half:], w_all_t, cos, sin, q_cols, kv_cols, 1, kv)
    quarter = half // 2
    run = lambda q, at, count, base: attend(
        scalars, q, at, count, k, vt, w_out, rows, zone, base
    )
    o_3, lse_3, *out_3 = run(q_far, quarter, quarter, half + quarter)
    if nz == 4:
        second = shift(after(from_outer, out_3[0]), [(1, 2), (2, 3)])
    o_2, lse_2, *out_2 = run(after(q_far, out_3[0]), 0, quarter, half)
    o_near, lse_near, *out_near = run(after(q_near, out_2[0]), 0, half, 0)
    o_far = jnp.concatenate([o_2, o_3], axis=1)
    lse_far = jnp.concatenate([lse_2, lse_3], axis=1)
    dy_parts = [dy_own, tp_swap(after(dy_own, out_3[0]), 0), dy_side]
    dy_parts.append(tp_swap(after(dy_side, out_2[0]), 0))
    attended, _, near_sum = tp_scatter([*out_near, *out_2, *out_3])
    if nz == 4:
        third = shift(after(second, near_sum), [(2, 3)])
        outer = (weight, from_outer, second, third)
        inner = (from_inner, weight, from_outer, second)
    else:
        every = lax.all_gather(weight, "z", axis=0, tiled=True)
        every = lax.dynamic_slice_in_dim(every, ic * mine, mine, 0)
        outer, inner = (every[:cut],), (every[cut:],)
    x1 = x + attended
    r2 = lax.rsqrt(jnp.mean(x1 * x1, axis=-1, keepdims=True) + EPSILON)
    n2 = x1 * r2
    h2 = (n2 * norm2_gain).astype(BF16)

    router_wide = jnp.pad(w_router, ((0, 0), (0, LANES - experts)))
    h2_side = y_swap(h2)
    h2_parts = [h2, tp_swap(h2, 0), h2_side, tp_swap(h2_side, 0)]
    head = along.astype(jnp.int32)[None]
    outer_ids = jnp.concatenate([head, ids[:cut].astype(jnp.int32)])
    inner_ids = jnp.concatenate([head, ids[cut:].astype(jnp.int32)])
    through = lambda s, at, w, old=(): run_experts(
        s, h2_parts[at : at + 2], dy_parts[at : at + 2], router_wide, w, experts, 18 * cut, old
    )
    first = through(inner_ids, 0, inner)
    near = through(outer_ids, 0, outer, first[:4])
    third_pass = through(inner_ids, 2, inner)
    far = through(outer_ids, 2, outer, third_pass[:4])

    join = lambda a, b: (a.astype(F32) + tp_swap(b, 0).astype(F32)).astype(BF16)
    dh_side = join(far[2], far[3])
    dh_own = near[2].astype(F32) + tp_swap(near[3], 0).astype(F32)
    dh_sum = dh_own + y_swap(dh_side).astype(F32)
    grads_outer = expert_grads(
        [after(h2_parts[0], dh_side), *h2_parts[1:]], dy_parts, (near[4], far[4]), (near[5], far[5])
    )
    grads_inner = expert_grads(
        [after(h2_parts[0], grads_outer), *h2_parts[1:]],
        dy_parts,
        (first[4], third_pass[4]),
        (first[5], third_pass[5]),
    )

    probs = jax.nn.softmax(dot(h2, w_router), axis=-1)
    dprobs = dh_sum[:, width : width + experts]
    dprobs = dprobs + dh_sum[:, width + LANES // 2 : width + LANES // 2 + experts]
    dlogits = (
        probs * (dprobs - jnp.sum(probs * dprobs, axis=-1, keepdims=True))
    ).astype(BF16)
    dh2 = dot(dlogits, w_router, 1, 1) + dh_sum[:, :width]
    scaled = dh2 * norm2_gain
    dx1 = grad_out.astype(F32) + r2 * (
        scaled - n2 * jnp.mean(scaled * n2, axis=-1, keepdims=True)
    )
    router_part = dot(dlogits, h2, 0, 0)
    gain2 = jnp.sum(dh2 * n2, axis=0, keepdims=True)

    da_parts = tp_gather(dx1.astype(BF16))
    back = lambda q, o, lse, da, base, sums: attend_back(
        scalars, q, o, lse, k, kt, v, cos, sin, w_out, da, rows, zone, base, sums
    )
    dq_near, *sums = back(q_near, o_near, lse_near, da_parts[:half], 0, None)
    out_part = out_grads([after(da_parts[0], dq_near), *da_parts[1:half]], o_near, None)
    out_part = out_grads(da_parts[half:], o_far, out_part)
    mixed_side = join(after(far[0], dq_near), after(far[1], dq_near))
    mixed_own = near[0].astype(F32) + tp_swap(after(near[1], dq_near), 0).astype(F32)
    dq_far, dkv = back(after(q_far, out_part, mixed_side), o_far, lse_far, da_parts[half:], half, sums)
    mixed_side = y_swap(mixed_side)
    output = x1 + mixed_own + mixed_side.astype(F32)
    dh1_far = input_grads(after(dq_far, mixed_side), dkv, w_all_t, rows, 1)
    dh1_near = input_grads(dq_near, after(dkv, dh1_far[0]), w_all_t, rows, 0)
    dh1, dh1_side, _ = tp_scatter([*dh1_near, *dh1_far])
    n1 = x * r1
    scaled = dh1 * norm1_gain
    grad_input = dx1 + r1 * (scaled - n1 * jnp.mean(scaled * n1, axis=-1, keepdims=True))

    grad_outproj = lax.psum_scatter(
        out_part, ("z", "y"), scatter_dimension=0, tiled=True
    ).astype(F32).T
    qkv_grad, gain1 = qkv_grads(
        [after(h_parts[0], dh1_side), *h_parts[1:]], dq_near, dq_far, dkv, w_all_t, norm1_gain
    )
    each = width // (2 * nz)
    qkv_grad = qkv_grad.reshape(nz, 2, each, qkv_grad.shape[1])
    pick = lambda at: lax.dynamic_index_in_dim(qkv_grad, at, 1, keepdims=False)
    summed = pick(iy).astype(F32) + y_swap(pick(1 - iy)).astype(F32)
    grad_qkv = lax.psum_scatter(
        summed.astype(BF16).reshape(nz * each, -1), "z", scatter_dimension=0, tiled=True
    ).astype(F32)
    small = own_columns(sum_all(jnp.concatenate([router_part, gain2, gain1], axis=0)))

    if nz == 4:
        outer, inner = grads_outer[0], grads_inner[0]
        add = lambda a, b: (a.astype(F32) + b.astype(F32)).astype(BF16)
        o1 = shift(outer, [(3, 2)])
        i1 = shift(after(inner, o1), [(3, 2)])
        o2 = shift(add(outer, o1), [(2, 1)])
        i2 = shift(add(inner, i1), [(2, 1)])
        o3 = shift(add(outer, o2), [(1, 0)])
        i0 = shift(after(inner, i1), [(0, 1)])
        whole = jnp.where(
            along == 0,
            outer.astype(F32) + o3.astype(F32),
            inner.astype(F32) + i2.astype(F32) + i0.astype(F32),
        ).astype(BF16)
        side = width // 2
        pairs = [(z, c) for z in range(4) for c in (z // 2,)]
        other = lax.dynamic_slice_in_dim(whole, (1 - ix) * side, side, 0)
        other = lax.ppermute(
            other,
            ("z", "x", "c"),
            [((z * 2 + i) * 2 + c, (z * 2 + 1 - i) * 2 + c) for z, c in pairs for i in range(2)],
        )
        kept = lax.dynamic_slice_in_dim(whole, ix * side, side, 0)
        kept = kept.astype(F32) + other.astype(F32)
        own = lax.dynamic_slice_in_dim(kept, ic * (side // 2), side // 2, 0)
        give = lax.dynamic_slice_in_dim(kept, (1 - ic) * (side // 2), side // 2, 0).astype(BF16)
        part = jnp.where(ic == iz // 2, own, tp_swap(give, 0).astype(F32))
    else:
        stacked = jnp.concatenate([grads_outer, grads_inner], axis=0)
        every = jnp.zeros((nz, width, 3 * hidden), BF16)
        every = lax.dynamic_update_slice_in_dim(every, stacked, ic * mine, 0)
        part = lax.psum_scatter(
            every.reshape(nz * width, 3 * hidden), "z", scatter_dimension=0, tiled=True
        )
        part = lax.psum_scatter(part, ("x", "c"), scatter_dimension=0, tiled=True).astype(F32)
    grad_gate = part[None, :, :hidden]
    grad_up = part[None, :, hidden : 2 * hidden]
    grad_down = part[:, 2 * hidden :].T[None]
    return (
        output,
        grad_input,
        small[experts + 1],
        grad_qkv[:, :q_cols],
        grad_qkv[:, q_cols : q_cols + kv_cols],
        grad_qkv[:, q_cols + kv_cols :],
        grad_outproj,
        small[experts],
        small[:experts].T,
        grad_gate,
        grad_up,
        grad_down,
    )


def solution(mesh):
    ep, tp = mesh.shape["ep"], mesh.shape["tp"]
    nz, nx = ep // 2, tp // 2
    grid = Mesh(mesh.devices.reshape(nz, 2, nx, 2), ("z", "y", "x", "c"))
    e, t = ("z", "y"), ("x", "c")
    every = ("z", "y", "x", "c")
    return jax.shard_map(
        functools.partial(body, (nz, nx)),
        mesh=grid,
        in_specs=(
            P(every, None),
            P(),
            P(None, t),
            P(None, t),
            P(None, t),
            P(t, None),
            P(),
            P(),
            P(e, None, None),
            P(e, None, None),
            P(e, None, None),
            P(every, None),
            P(e, None),
            P(e, None),
            P(every, None),
        ),
        out_specs=(
            P(every, None),
            P(every, None),
            P(every),
            P(e, t),
            P(e, t),
            P(e, t),
            P(t, e),
            P(every),
            P(every, None),
            P(e, t, None),
            P(e, t, None),
            P(e, None, t),
        ),
        check_vma=False,
    )
```

```python
import functools
import math

import jax
import jax.numpy as jnp
from jax import lax
from jax.experimental import pallas as pl
from jax.experimental.pallas import tpu as pltpu
from jax.sharding import Mesh, PartitionSpec as P

HEAD_SIZE = 64
HALF = HEAD_SIZE // 2
SEQUENCE_LENGTH = 2048
EPSILON = 1e-05
ROPE_BASE = 10000.0
MASK_FILL = -1e30
LANES = 128
F32 = jnp.float32
BF16 = jnp.bfloat16
VMEM_LIMIT = 60 * 1024 * 1024


def dot(a, b, ca=1, cb=0):
    return lax.dot_general(a, b, (((ca,), (cb,)), ((), ())), preferred_element_type=F32)


def after(value, *deps):
    return lax.optimization_barrier((value, *deps))[0]


def cost(micros):
    return pl.CostEstimate(
        flops=int(micros * 1e+09), transcendentals=0, bytes_accessed=int(micros * 3e+06)
    )


def params():
    return pltpu.CompilerParams(vmem_limit_bytes=VMEM_LIMIT)


def once(shape):
    return pl.BlockSpec(shape, lambda *_: (0,) * len(shape), pipeline_mode=pl.Buffered(1))


def qkv_kernel(q_cols, kv_cols, parts, *refs):
    h_refs, (w_ref, cos_ref, sin_ref) = refs[:parts], refs[parts : parts + 3]
    q_ref, k_ref, kt_ref, v_ref, vt_ref = refs[-5:]
    rows = h_refs[0].shape[0]
    scale = jnp.asarray(1.0 / math.sqrt(HEAD_SIZE), BF16)
    for b in range(parts):
        here = slice(b * rows, (b + 1) * rows)
        y = dot(w_ref[...], h_refs[b][...], 1, 1)
        cos, sin = cos_ref[:, here], sin_ref[:, here]

        def turned(base):
            a = y[base : base + HALF]
            b = y[base + HALF : base + HEAD_SIZE]
            return jnp.concatenate([a * cos - b * sin, b * cos + a * sin], axis=0)

        for h in range(q_cols // HEAD_SIZE):
            base = h * HEAD_SIZE
            q_ref[base : base + HEAD_SIZE, here] = turned(base).astype(BF16) * scale
        for g in range(kv_cols // HEAD_SIZE):
            base = g * HEAD_SIZE
            kt = turned(q_cols + base)
            kt_ref[base : base + HEAD_SIZE, here] = kt.astype(BF16)
            k_ref[g, here, :] = kt.T.astype(BF16)
            vt = y[q_cols + kv_cols + base : q_cols + kv_cols + base + HEAD_SIZE]
            vt_ref[base : base + HEAD_SIZE, here] = vt.astype(BF16)
            v_ref[g, here, :] = vt.T.astype(BF16)


def project_qkv(h_parts, w_all, cos, sin, q_cols, kv_cols, half, previous):
    parts = len(h_parts)
    rows, width = h_parts[0].shape
    size = parts * rows
    groups = kv_cols // HEAD_SIZE
    cols = q_cols + 2 * kv_cols
    lane_block = lambda *_: (0, half)
    row_block = lambda *_: (0, half, 0)
    kv_shapes = [
        jax.ShapeDtypeStruct((groups, 2 * size, HEAD_SIZE), BF16),
        jax.ShapeDtypeStruct((kv_cols, 2 * size), BF16),
    ] * 2
    kv_specs = [
        pl.BlockSpec((groups, size, HEAD_SIZE), row_block),
        pl.BlockSpec((kv_cols, size), lane_block),
    ] * 2
    previous = list(previous or ())
    return pl.pallas_call(
        functools.partial(qkv_kernel, q_cols, kv_cols, parts),
        grid=(1,),
        in_specs=[once((rows, width))] * parts
        + [
            once((cols, width)),
            pl.BlockSpec((HALF, size), lane_block),
            pl.BlockSpec((HALF, size), lane_block),
        ]
        + [pl.BlockSpec(memory_space=pl.ANY)] * len(previous),
        out_specs=[once((q_cols, size))] + kv_specs,
        out_shape=[jax.ShapeDtypeStruct((q_cols, size), BF16)] + kv_shapes,
        input_output_aliases={parts + 3 + i: 1 + i for i in range(len(previous))},
        compiler_params=params(),
        cost_estimate=cost(0.5),
        name="qkv",
    )(*h_parts, w_all, cos, sin, *previous)


def last_key(s_ref, zone, own, rows):
    zone_index = own * rows // zone
    zones = SEQUENCE_LENGTH // zone
    start = s_ref[1 + zone_index]
    stop = start + s_ref[1 + zones + zone_index]
    position = own * rows + lax.broadcasted_iota(jnp.int32, (1, rows), 1)
    return jnp.where((position >= start) & (position < stop), stop - 1, position)


def block_walk(me, own, rows, zone, pair):
    per_zone = zone // rows
    pair(own, True, True)
    for other in range(1, per_zone):
        pair(own ^ other, True, False)
    first = (own // per_zone) * per_zone

    def step(key_block, carry):
        pair(key_block, False, False)
        return carry

    lax.fori_loop(0, first, step, 0)


def attend_kernel(
    rows, zone, heads, groups, base, s_ref, q_ref, k_ref, vt_ref, w_ref, o_ref, lse_ref, *refs
):
    out_refs, (acc, top, total) = refs[:-3], refs[-3:]
    me = s_ref[0]
    own = me ^ (pl.program_id(0) + base)
    limit = last_key(s_ref, zone, own, rows)

    def pair(key_block, masked, first):
        offset = pl.multiple_of((me ^ key_block) * rows, rows)
        if masked:
            key_pos = key_block * rows + lax.broadcasted_iota(jnp.int32, (rows, rows), 0)
            allowed = key_pos <= limit
        for h in range(heads):
            g = h // (heads // groups)
            r = slice(h * HEAD_SIZE, (h + 1) * HEAD_SIZE)
            s = dot(k_ref[g, pl.ds(offset, rows), :], q_ref[r, :])
            if masked:
                s = jnp.where(allowed, s, MASK_FILL)
            peak = jnp.max(s, axis=0, keepdims=True)
            vt = vt_ref[g * HEAD_SIZE : (g + 1) * HEAD_SIZE, pl.ds(offset, rows)]
            if first:
                p = jnp.exp(s - peak)
                top[h : h + 1, :] = peak
                total[h : h + 1, :] = jnp.sum(p, axis=0, keepdims=True)
                acc[r, :] = dot(vt, p.astype(BF16))
            else:
                old = top[h : h + 1, :]
                new = jnp.maximum(old, peak)
                fade = jnp.exp(old - new)
                p = jnp.exp(s - new)
                top[h : h + 1, :] = new
                total[h : h + 1, :] = total[h : h + 1, :] * fade + jnp.sum(p, axis=0, keepdims=True)
                acc[r, :] = acc[r, :] * fade + dot(vt, p.astype(BF16))

    block_walk(me, own, rows, zone, pair)
    for h in range(heads):
        r = slice(h * HEAD_SIZE, (h + 1) * HEAD_SIZE)
        o_ref[r, :] = (acc[r, :] / total[h : h + 1, :]).astype(BF16)
        lse_ref[h : h + 1, :] = top[h : h + 1, :] + jnp.log(total[h : h + 1, :])
    for b, out_ref in enumerate(out_refs):

        @pl.when(pl.program_id(0) == b)
        def _():
            out_ref[...] = dot(o_ref[...], w_ref[...], 0, 0).astype(BF16)


def attend(scalars, q, at, count, k, vt, w_out, rows, zone, base):
    q_cols = q.shape[0]
    size = count * rows
    groups = k.shape[0]
    width = w_out.shape[1]
    heads = q_cols // HEAD_SIZE
    block = lambda i, s: (0, i)
    return pl.pallas_call(
        functools.partial(attend_kernel, rows, zone, heads, groups, base),
        grid_spec=pltpu.PrefetchScalarGridSpec(
            num_scalar_prefetch=1,
            grid=(count,),
            in_specs=[
                pl.BlockSpec((q_cols, rows), lambda i, s: (0, i + at)),
                once(k.shape),
                once(vt.shape),
                once(w_out.shape),
            ],
            out_specs=[
                pl.BlockSpec((q_cols, rows), block),
                pl.BlockSpec((heads, rows), block),
            ]
            + [once((rows, width))] * count,
            scratch_shapes=[
                pltpu.VMEM((q_cols, rows), F32),
                pltpu.VMEM((8, rows), F32),
                pltpu.VMEM((8, rows), F32),
            ],
        ),
        out_shape=[
            jax.ShapeDtypeStruct((q_cols, size), BF16),
            jax.ShapeDtypeStruct((heads, size), F32),
        ]
        + [jax.ShapeDtypeStruct((rows, width), BF16)] * count,
        compiler_params=params(),
        cost_estimate=cost(3 * count),
        name="attend",
    )(scalars, q, k, vt, w_out)


def attend_back_kernel(rows, zone, heads, groups, base, parts, *refs):
    s_ref, q_ref, o_ref, lse_ref, k_ref, kt_ref, v_ref, cos_ref, sin_ref, w_ref = refs[:10]
    da_refs = refs[10 : 10 + parts]
    rest = refs[10 + parts :]
    if base:
        old_dk, old_dv, dq_ref, dkv_ref, dq, dk, dv, delta, do_ref = rest
    else:
        dq_ref, dk, dv, dq, delta, do_ref = rest
    me = s_ref[0]
    step = pl.program_id(0)
    own = me ^ (step + base)
    limit = last_key(s_ref, zone, own, rows)
    here = pl.multiple_of((step + base) * rows, rows)

    @pl.when(step == 0)
    def _():
        for b in range(parts):
            do_ref[b] = dot(w_ref[...], da_refs[b][...], 1, 1).astype(BF16)
        if base:
            dk[...] = old_dk[...]
            dv[...] = old_dv[...]
        else:
            dk[...] = jnp.zeros_like(dk)
            dv[...] = jnp.zeros_like(dv)

    for h in range(heads):
        r = slice(h * HEAD_SIZE, (h + 1) * HEAD_SIZE)
        delta[h : h + 1, :] = jnp.sum(
            do_ref[step, r, :].astype(F32) * o_ref[r, :].astype(F32), axis=0, keepdims=True
        )

    def pair(key_block, masked, first):
        offset = pl.multiple_of((me ^ key_block) * rows, rows)
        keys = pl.ds(offset, rows)
        if masked:
            key_pos = key_block * rows + lax.broadcasted_iota(jnp.int32, (rows, rows), 0)
            allowed = key_pos <= limit
        for g in range(groups):
            kb = k_ref[g, keys, :]
            vb = v_ref[g, keys, :]
            kt = kt_ref[g * HEAD_SIZE : (g + 1) * HEAD_SIZE, keys]
            dk_sum = dk[g, keys, :]
            dv_sum = dv[g, keys, :]
            for h in range(g * (heads // groups), (g + 1) * (heads // groups)):
                r = slice(h * HEAD_SIZE, (h + 1) * HEAD_SIZE)
                do = do_ref[step, r, :]
                s = dot(kb, q_ref[r, :])
                if masked:
                    s = jnp.where(allowed, s, MASK_FILL)
                p = jnp.exp(s - lse_ref[h : h + 1, :])
                dp = dot(vb, do)
                ds = (p * (dp - delta[h : h + 1, :])).astype(BF16)
                dv_sum = dv_sum + dot(p.astype(BF16), do, 1, 1)
                dk_sum = dk_sum + dot(ds, q_ref[r, :], 1, 1)
                part = dot(kt, ds)
                dq[r, :] = part if first else dq[r, :] + part
            dk[g, keys, :] = dk_sum
            dv[g, keys, :] = dv_sum

    block_walk(me, own, rows, zone, pair)
    cos, sin = cos_ref[:, pl.ds(here, rows)], sin_ref[:, pl.ds(here, rows)]
    scale = 1.0 / math.sqrt(HEAD_SIZE)
    for h in range(heads):
        at = h * HEAD_SIZE
        a = dq[at : at + HALF, :] * scale
        b = dq[at + HALF : at + HEAD_SIZE, :] * scale
        dq_ref[at : at + HALF, :] = (a * cos + b * sin).astype(BF16)
        dq_ref[at + HALF : at + HEAD_SIZE, :] = (b * cos - a * sin).astype(BF16)

    if base:

        @pl.when(step == pl.num_programs(0) - 1)
        def _():
            every_cos, every_sin = cos_ref[...], sin_ref[...]
            for g in range(groups):
                at = g * HEAD_SIZE
                turned = dk[g].T
                a, b = turned[:HALF], turned[HALF:]
                dkv_ref[at : at + HALF, :] = (a * every_cos + b * every_sin).astype(BF16)
                dkv_ref[at + HALF : at + HEAD_SIZE, :] = (b * every_cos - a * every_sin).astype(BF16)
                at = (groups + g) * HEAD_SIZE
                dkv_ref[at : at + HEAD_SIZE, :] = dv[g].T.astype(BF16)


def attend_back(scalars, q, o, lse, k, kt, v, cos, sin, w_out, da_parts, rows, zone, base, sums):
    q_cols, size = q.shape
    groups, total, _ = k.shape
    heads = q_cols // HEAD_SIZE
    parts = len(da_parts)
    block = lambda i, s: (0, i)
    sum_shape = (groups, total, HEAD_SIZE)
    inputs = [q, o, lse, k, kt, v, cos, sin, w_out, *da_parts]
    in_specs = [
        pl.BlockSpec((q_cols, rows), block),
        pl.BlockSpec((q_cols, rows), block),
        pl.BlockSpec((heads, rows), block),
    ] + [once(a.shape) for a in inputs[3:]]
    out_specs = [pl.BlockSpec((q_cols, rows), block)]
    out_shape = [jax.ShapeDtypeStruct((q_cols, size), BF16)]
    scratch = [pltpu.VMEM((q_cols, rows), F32)]
    if base:
        inputs += list(sums)
        in_specs += [once(sum_shape)] * 2
        out_specs += [once((2 * groups * HEAD_SIZE, total))]
        out_shape += [jax.ShapeDtypeStruct((2 * groups * HEAD_SIZE, total), BF16)]
        scratch += [pltpu.VMEM(sum_shape, F32)] * 2
    else:
        out_specs += [once(sum_shape)] * 2
        out_shape += [jax.ShapeDtypeStruct(sum_shape, F32)] * 2
    scratch += [pltpu.VMEM((8, rows), F32), pltpu.VMEM((parts, q_cols, rows), BF16)]
    return pl.pallas_call(
        functools.partial(attend_back_kernel, rows, zone, heads, groups, base, parts),
        grid_spec=pltpu.PrefetchScalarGridSpec(
            num_scalar_prefetch=1,
            grid=(size // rows,),
            in_specs=in_specs,
            out_specs=out_specs,
            scratch_shapes=scratch,
        ),
        out_shape=out_shape,
        compiler_params=params(),
        cost_estimate=cost(30),
        name="attend_back",
    )(scalars, *inputs)


def input_grad_kernel(dq_ref, dkv_ref, w_ref, *out_refs):
    q_cols = dq_ref.shape[0]
    rows = out_refs[0].shape[0]
    for b, out_ref in enumerate(out_refs):
        here = slice(b * rows, (b + 1) * rows)
        out = dot(dq_ref[:, here], w_ref[:q_cols, :], 0, 0)
        out = out + dot(dkv_ref[:, here], w_ref[q_cols:, :], 0, 0)
        out_ref[...] = out.astype(BF16)


def input_grads(dq, dkv, w_all_t, rows, half):
    q_cols, size = dq.shape
    cols, width = w_all_t.shape
    count = size // rows
    return pl.pallas_call(
        input_grad_kernel,
        grid=(1,),
        in_specs=[
            once((q_cols, size)),
            pl.BlockSpec((cols - q_cols, size), lambda i: (0, half)),
            once((cols, width)),
        ],
        out_specs=[once((rows, width))] * count,
        out_shape=[jax.ShapeDtypeStruct((rows, width), BF16)] * count,
        compiler_params=params(),
        cost_estimate=cost(5),
        name="input_grads",
    )(dq, dkv, w_all_t)


def qkv_grad_kernel(parts, *refs):
    h_refs = refs[: 2 * parts]
    near_ref, far_ref, dkv_ref, w_ref, gain_ref, grad_ref, gain_grad_ref = refs[2 * parts :]
    rows = h_refs[0].shape[0]
    sums = [0.0, 0.0]
    for b in range(2 * parts):
        dq_ref, at = (near_ref, b) if b < parts else (far_ref, b - parts)
        h = h_refs[b][...]
        sums[0] = sums[0] + dot(dq_ref[:, at * rows : (at + 1) * rows], h)
        sums[1] = sums[1] + dot(dkv_ref[:, b * rows : (b + 1) * rows], h)
    q_cols = near_ref.shape[0]
    grad_ref[:, :q_cols] = sums[0].T.astype(BF16)
    grad_ref[:, q_cols:] = sums[1].T.astype(BF16)
    gain = jnp.sum(sums[0] * w_ref[:q_cols, :].astype(F32), axis=0, keepdims=True)
    gain = gain + jnp.sum(sums[1] * w_ref[q_cols:, :].astype(F32), axis=0, keepdims=True)
    gain_grad_ref[...] = gain / gain_ref[...]


def qkv_grads(h_parts, dq_near, dq_far, dkv, w_all_t, gain):
    cols, width = w_all_t.shape
    inputs = [*h_parts, dq_near, dq_far, dkv, w_all_t, gain[None, :]]
    return pl.pallas_call(
        functools.partial(qkv_grad_kernel, len(h_parts) // 2),
        grid=(1,),
        in_specs=[once(a.shape) for a in inputs],
        out_specs=[once((width, cols)), once((1, width))],
        out_shape=[
            jax.ShapeDtypeStruct((width, cols), BF16),
            jax.ShapeDtypeStruct((1, width), F32),
        ],
        compiler_params=params(),
        cost_estimate=cost(10),
        name="qkv_grads",
    )(*inputs)


def out_grad_kernel(parts, finish, *refs):
    da_refs, o_ref, grad_ref = refs[:parts], refs[parts], refs[-1]
    rows = da_refs[0].shape[0]
    total = refs[parts + 1][...] if finish else 0.0
    for b in range(parts):
        total = total + dot(o_ref[:, b * rows : (b + 1) * rows], da_refs[b][...])
    grad_ref[...] = total.T.astype(BF16) if finish else total


def out_grads(da_parts, o, previous):
    q_cols, width = o.shape[0], da_parts[0].shape[1]
    inputs = [*da_parts, o] + ([] if previous is None else [previous])
    finish = previous is not None
    shape = (width, q_cols) if finish else (q_cols, width)
    return pl.pallas_call(
        functools.partial(out_grad_kernel, len(da_parts), finish),
        grid=(1,),
        in_specs=[once(a.shape) for a in inputs],
        out_specs=once(shape),
        out_shape=jax.ShapeDtypeStruct(shape, BF16 if finish else F32),
        compiler_params=params(),
        cost_estimate=cost(4),
        name="out_grads",
    )(*inputs)


def expert_kernel(experts, adds, choices, alone, *refs):
    s_ref, h0, h1, dy0, dy1, router_ref = refs[:6]
    w_choices = refs[6 : 6 + choices]
    old = refs[6 + choices : 6 + choices + (4 if adds else 0)]
    outs = refs[len(refs) - 19 :]
    mix0, mix1, dh0, dh1, act_out, dgu_out = outs[:6]
    h_s, dy_s, w_s, mix_s, dh_s, gates, dgate, mix_o, dh_o, act_o, dgu_o, in_sem, out_sem = outs[6:]
    e = pl.program_id(0)
    last = pl.num_programs(0) - 1
    rows, width = h0.shape
    hidden = w_s.shape[2] // 3
    lane = lax.broadcasted_iota(jnp.int32, (rows, LANES), 1)
    slot = lax.rem(e, 2)

    def fetch_weights(index, into):
        for n in range(choices):

            @pl.when(s_ref[0] == n)
            def _():
                pltpu.make_async_copy(
                    w_choices[n].at[index], w_s.at[into], in_sem.at[4 + into]
                ).start()

    tokens_in = [
        pltpu.make_async_copy(src, dst, in_sem.at[n])
        for n, (src, dst) in enumerate(
            ((h0, h_s.at[0]), (dy0, dy_s.at[0]), (h1, h_s.at[1]), (dy1, dy_s.at[1]))
        )
    ]
    old_in = [
        pltpu.make_async_copy(src, dst, in_sem.at[6 + n])
        for n, (src, dst) in enumerate(zip(old, (mix_o.at[0], mix_o.at[1], dh_o.at[0], dh_o.at[1])))
    ]

    @pl.when(e == 0)
    def _():
        tokens_in[0].start()
        fetch_weights(0, 0)
        for copy in tokens_in[1:] + old_in:
            copy.start()

    @pl.when(e < last)
    def _():
        fetch_weights(e + 1, 1 - slot)

    def block(i, carry):
        for n in range(2):

            @pl.when((e == 0) & (i == n))
            def _():
                tokens_in[2 * n].wait()
                tokens_in[2 * n + 1].wait()
                for copy in old_in[n::2]:
                    copy.wait()

        @pl.when(e == 0)
        def _():
            logits = dot(h_s[i], router_ref[...])
            logits = jnp.where(lane < experts, logits, MASK_FILL)
            weights = jnp.exp(logits - jnp.max(logits, axis=1, keepdims=True))
            weights = weights / jnp.sum(weights, axis=1, keepdims=True)
            gates[i] = weights * dy_s[i, :, width:].astype(F32)

        @pl.when(i == 0)
        def _():
            pltpu.make_async_copy(w_choices[0].at[0], w_s.at[slot], in_sem.at[4 + slot]).wait()

        mine = lane == s_ref[1 + e]
        gate = jnp.sum(jnp.where(mine, gates[i], 0.0), axis=1, keepdims=True)
        both = dot(h_s[i], w_s[slot, :, : 2 * hidden])
        gp, up = both[:, :hidden], both[:, hidden:]
        sg = jax.nn.sigmoid(gp)
        silu = gp * sg
        act = (silu * up).astype(BF16).astype(F32)
        dact = dot(dy_s[i, :, :width], w_s[slot, :, 2 * hidden :])
        chosen = dy_s[i, :, width:].astype(F32)
        own_dgate = jnp.where(mine, chosen * jnp.sum(act * dact, axis=1, keepdims=True), 0.0)
        scaled = (gate * act).astype(BF16)
        dact = gate * dact
        dgp = (dact * up * sg * (1.0 + gp * (1.0 - sg))).astype(BF16)
        dup = (dact * silu).astype(BF16)
        here = pl.ds(pl.multiple_of(i * rows, rows), rows)
        act_copy = pltpu.make_async_copy(act_o.at[i], act_out.at[e, here, :], out_sem.at[i])
        dgu_copy = pltpu.make_async_copy(dgu_o.at[i], dgu_out.at[e, here, :], out_sem.at[2 + i])

        @pl.when(e > 0)
        def _():
            act_copy.wait()
            dgu_copy.wait()

        act_o[i] = scaled
        dgu_o[i, :, :hidden] = dgp
        dgu_o[i, :, hidden:] = dup
        act_copy.start()
        dgu_copy.start()
        mix = dot(scaled, w_s[slot, :, 2 * hidden :], 1, 1)
        dh = dot(dgu_o[i], w_s[slot, :, : 2 * hidden], 1, 1)

        def finish(mix, dh, own_dgate):
            mix_o[i] = mix.astype(BF16)
            dh_o[i, :, :width] = dh.astype(BF16)
            high = own_dgate.astype(BF16).astype(F32)
            low = own_dgate - high
            dh_o[i, :, width:] = (high + pltpu.roll(low, LANES // 2, 1)).astype(BF16)

        if adds:
            kept = dh_o[i, :, width:].astype(F32)
            kept = kept + pltpu.roll(kept, LANES // 2, 1)
            kept = jnp.where(lane < LANES // 2, kept, 0.0)
        if adds and alone:
            finish(mix + mix_o[i].astype(F32), dh + dh_o[i, :, :width].astype(F32), own_dgate + kept)
        elif alone:
            finish(mix, dh, own_dgate)
        else:

            @pl.when(e == 0)
            def _():
                if adds:
                    mix_s[i] = mix + mix_o[i].astype(F32)
                    dh_s[i] = dh + dh_o[i, :, :width].astype(F32)
                    dgate[i] = own_dgate + kept
                else:
                    mix_s[i] = mix
                    dh_s[i] = dh
                    dgate[i] = own_dgate

            @pl.when(e > 0)
            def _():
                mix_s[i] += mix
                dh_s[i] += dh
                dgate[i] += own_dgate

            @pl.when(e == last)
            def _():
                finish(mix_s[i], dh_s[i], dgate[i])

        for n in range(2):

            @pl.when((e == last) & (i == n))
            def _():
                pltpu.make_async_copy(mix_o.at[n], (mix0, mix1)[n], out_sem.at[4 + n]).start()
                pltpu.make_async_copy(dh_o.at[n], (dh0, dh1)[n], out_sem.at[6 + n]).start()

        return carry

    lax.fori_loop(0, 2, block, 0)

    @pl.when(e == last)
    def _():
        for i in range(2):
            here = pl.ds(i * rows, rows)
            pltpu.make_async_copy(act_o.at[i], act_out.at[e, here, :], out_sem.at[i]).wait()
            pltpu.make_async_copy(dgu_o.at[i], dgu_out.at[e, here, :], out_sem.at[2 + i]).wait()
            pltpu.make_async_copy(mix_o.at[i], (mix0, mix1)[i], out_sem.at[4 + i]).wait()
            pltpu.make_async_copy(dh_o.at[i], (dh0, dh1)[i], out_sem.at[6 + i]).wait()


def run_experts(scalars, h_parts, dy_parts, router, choices, experts, micros, old=()):
    rows, width = h_parts[0].shape
    wide = width + LANES
    mine, _, cols = choices[0].shape
    hidden = cols // 3
    anywhere = pl.BlockSpec(memory_space=pl.ANY)
    return pl.pallas_call(
        functools.partial(expert_kernel, experts, bool(old), len(choices), mine == 1),
        grid_spec=pltpu.PrefetchScalarGridSpec(
            num_scalar_prefetch=1,
            grid=(mine,),
            in_specs=[anywhere] * 4 + [once((width, LANES))] + [anywhere] * (len(choices) + len(old)),
            out_specs=[anywhere] * 6,
            scratch_shapes=[
                pltpu.VMEM((2, rows, width), BF16),
                pltpu.VMEM((2, rows, wide), BF16),
                pltpu.VMEM((2, width, cols), BF16),
                pltpu.VMEM((2, rows, width), F32),
                pltpu.VMEM((2, rows, width), F32),
                pltpu.VMEM((2, rows, LANES), F32),
                pltpu.VMEM((2, rows, LANES), F32),
                pltpu.VMEM((2, rows, width), BF16),
                pltpu.VMEM((2, rows, wide), BF16),
                pltpu.VMEM((2, rows, hidden), BF16),
                pltpu.VMEM((2, rows, 2 * hidden), BF16),
                pltpu.SemaphoreType.DMA((10,)),
                pltpu.SemaphoreType.DMA((8,)),
            ],
        ),
        out_shape=[jax.ShapeDtypeStruct((rows, width), BF16)] * 2
        + [jax.ShapeDtypeStruct((rows, wide), BF16)] * 2
        + [
            jax.ShapeDtypeStruct((mine, 2 * rows, hidden), BF16),
            jax.ShapeDtypeStruct((mine, 2 * rows, 2 * hidden), BF16),
        ],
        compiler_params=params(),
        cost_estimate=cost(micros),
        name="experts",
    )(scalars, *h_parts, *dy_parts, router, *choices, *old)


def expert_grad_kernel(*refs):
    h_refs, dy_refs, acts, dgus = refs[:4], refs[4:8], refs[8:10], refs[10:12]
    out_ref, h_s, dy_s, act_s, dgu_s, sem = refs[12:]
    e = pl.program_id(0)
    rows, width = h_refs[0].shape
    hidden = act_s.shape[1]
    first, second = [], []
    for b in range(4):
        here = pl.ds(b * rows, rows)
        first.append(pltpu.make_async_copy(h_refs[b], h_s.at[here, :], sem.at[b]))
        second.append(
            pltpu.make_async_copy(dy_refs[b].at[:, pl.ds(0, width)], dy_s.at[here, :], sem.at[4 + b])
        )
    per_expert = []
    for b in range(2):
        here = pl.ds(2 * b * rows, 2 * rows)
        per_expert.append(pltpu.make_async_copy(dgus[b].at[e], dgu_s.at[here, :], sem.at[8 + b]))
    for b in range(2):
        here = pl.ds(2 * b * rows, 2 * rows)
        per_expert.append(pltpu.make_async_copy(acts[b].at[e], act_s.at[here, :], sem.at[10 + b]))
    for copy in per_expert[:2]:
        copy.start()

    @pl.when(e == 0)
    def _():
        for copy in first:
            copy.start()

    for copy in per_expert[2:]:
        copy.start()

    @pl.when(e == 0)
    def _():
        for copy in second:
            copy.start()
        for copy in first:
            copy.wait()

    for copy in per_expert[:2]:
        copy.wait()

    def rows_of(c):
        return pl.ds(pl.multiple_of(c * (width // 3), width // 3), width // 3)

    def gate_up(c, carry):
        out_ref[0, rows_of(c), : 2 * hidden] = dot(h_s[:, rows_of(c)], dgu_s[...], 0, 0).astype(BF16)
        return carry

    lax.fori_loop(0, 3, gate_up, 0)

    @pl.when(e == 0)
    def _():
        for copy in second:
            copy.wait()

    for copy in per_expert[2:]:
        copy.wait()

    def down(c, carry):
        out_ref[0, rows_of(c), 2 * hidden :] = dot(dy_s[:, rows_of(c)], act_s[...], 0, 0).astype(BF16)
        return carry

    lax.fori_loop(0, 3, down, 0)


def expert_grads(h_parts, dy_parts, acts, dgus):
    rows, width = h_parts[0].shape
    mine, _, hidden = acts[0].shape
    anywhere = pl.BlockSpec(memory_space=pl.ANY)
    return pl.pallas_call(
        expert_grad_kernel,
        grid=(mine,),
        in_specs=[anywhere] * 12,
        out_specs=pl.BlockSpec((1, width, 3 * hidden), lambda e: (e, 0, 0)),
        out_shape=jax.ShapeDtypeStruct((mine, width, 3 * hidden), BF16),
        scratch_shapes=[
            pltpu.VMEM((4 * rows, width), BF16),
            pltpu.VMEM((4 * rows, width), BF16),
            pltpu.VMEM((4 * rows, hidden), BF16),
            pltpu.VMEM((4 * rows, 2 * hidden), BF16),
            pltpu.SemaphoreType.DMA((12,)),
        ],
        compiler_params=params(),
        cost_estimate=cost(8),
        name="expert_grads",
    )(*h_parts, *dy_parts, *acts, *dgus)


def body(
    sizes,
    tokens,
    norm1_gain,
    w_query,
    key_weight,
    value_weight,
    w_out,
    norm2_gain,
    w_router,
    w_gate,
    w_up,
    w_down,
    routes,
    piece_first_position,
    piece_length,
    grad_out,
):
    nz, nx = sizes
    rows, width = tokens.shape
    blocks = 2 * nx
    half = blocks // 2
    q_cols, kv_cols = w_query.shape[1], key_weight.shape[1]
    experts = w_router.shape[1]
    hidden = w_gate.shape[2]
    zone = SEQUENCE_LENGTH // piece_length.shape[1]
    iz, iy, ix, ic = (lax.axis_index(a) for a in "zyxc")
    me = ix * 2 + ic

    def tp_swap(value, bit):
        if bit == 0:
            return lax.ppermute(value, "c", [(0, 1), (1, 0)])
        return lax.ppermute(value, "x", [(i, i ^ (1 << (bit - 1))) for i in range(nx)])

    def y_swap(value):
        return lax.ppermute(value, "y", [(0, 1), (1, 0)])

    bits = blocks.bit_length() - 1

    def fold(parts, kind):
        parts = dict(enumerate(parts))
        for bit in range(bits - 1):
            for i in sorted(parts, reverse=True):
                if i & (1 << bit):
                    parts[i] = tp_swap(parts[i], bit)
            for i in sorted(parts, reverse=True):
                if i & (1 << bit):
                    total = parts[i ^ (1 << bit)].astype(F32) + parts.pop(i).astype(F32)
                    parts[i ^ (1 << bit)] = total.astype(BF16 if bit < bits - 2 else kind)
        return parts[0]

    def sum_all(value):
        step = 1
        while step < nz:
            value = value + lax.ppermute(value, "z", [(i, i ^ step) for i in range(nz)])
            step *= 2
        value = value + y_swap(value)
        for bit in range(bits):
            value = value + tp_swap(value, bit)
        return value

    def own_columns(value):
        each = width // (nz * 4 * nx)
        index = (iz * 2 + iy) * blocks + me
        return lax.dynamic_slice_in_dim(value, index * each, each, 1)

    x = tokens.astype(F32)
    r1 = lax.rsqrt(jnp.mean(x * x, axis=-1, keepdims=True) + EPSILON)
    h1 = (x * r1 * norm1_gain).astype(BF16)
    h_parts = {0: h1}
    for bit in reversed(range(bits)):
        for i in list(h_parts):
            if i < half:
                h_parts[i | (1 << bit)] = tp_swap(h_parts[i], bit)

    w_all = jnp.concatenate([w_query, key_weight, value_weight], axis=1)
    w_all_t = w_all.T
    order = me ^ jnp.arange(blocks, dtype=jnp.int32)
    position = (order[:, None] * rows + jnp.arange(rows, dtype=jnp.int32)[None, :]).reshape(-1)
    frequency = ROPE_BASE ** (-(jnp.arange(HALF, dtype=F32) * (2.0 / HEAD_SIZE)))
    angles = frequency[:, None] * position.astype(F32)[None, :]
    cos, sin = jnp.cos(angles), jnp.sin(angles)
    scalars = jnp.concatenate(
        [me.astype(jnp.int32)[None], piece_first_position[0], piece_length[0]]
    )
    near_rows = [h_parts[i] for i in range(half)]
    q_near, *kv = project_qkv(near_rows, w_all_t, cos, sin, q_cols, kv_cols, 0, None)
    h_parts[half] = after(h_parts[half], q_near)
    for bit in reversed(range(bits - 1)):
        for i in list(h_parts):
            if i >= half:
                h_parts[i | (1 << bit)] = tp_swap(h_parts[i], bit)
    h_parts = [h_parts[i] for i in range(blocks)]

    mask = jnp.zeros((rows, LANES), jnp.bool_)
    for j in range(routes.shape[1]):
        mask = mask | (routes[:, j : j + 1] == jnp.arange(LANES, dtype=jnp.int32)[None, :])
    dy_own = after(jnp.concatenate([grad_out, mask.astype(BF16)], axis=1), q_near)
    dy_side = y_swap(dy_own)

    mine = nz // 2
    cut = mine // 2
    weight = after(jnp.concatenate([w_gate[0], w_up[0], w_down[0].T], axis=1), h_parts[1])[None]
    if nz == 4:
        ids = jnp.where(ic == 0, jnp.arange(2), 3 - jnp.arange(2)) * 2 + iy
        along = jnp.where(ic == 0, iz, 3 - iz)

        def shift(value, moves):
            perm = [(s * 2, d * 2) for s, d in moves]
            perm += [((3 - s) * 2 + 1, (3 - d) * 2 + 1) for s, d in moves]
            return lax.ppermute(value, ("z", "c"), perm)

        from_outer = shift(weight, [(0, 1), (1, 2)])
        from_inner = shift(weight, [(1, 0)])
    else:
        ids = (ic * mine + jnp.arange(mine)) * 2 + iy
        along = ic * 0

    q_far, k, kt, v, vt = project_qkv(h_parts[half:], w_all_t, cos, sin, q_cols, kv_cols, 1, kv)
    quarter = half // 2
    run = lambda q, at, count, base: attend(
        scalars, q, at, count, k, vt, w_out, rows, zone, base
    )
    o_3, lse_3, *out_3 = run(q_far, quarter, quarter, half + quarter)
    early = ()
    if nz == 4:
        early = (from_outer,)
        second = shift(after(from_outer, out_3[0]), [(1, 2), (2, 3)])
    o_2, lse_2, *out_2 = run(after(q_far, out_3[0], *early), 0, quarter, half)
    side = fold([*out_2, *out_3], BF16)
    if nz == 4:
        o_near, lse_near, *out_near = run(after(q_near, side), 0, half, 0)
    else:
        o_near, lse_near, *out_near = run(after(q_near, side), 0, half, 0)
    o_far = jnp.concatenate([o_2, o_3], axis=1)
    lse_far = jnp.concatenate([lse_2, lse_3], axis=1)
    dy_parts = [dy_own, tp_swap(after(dy_own, out_3[0]), 0), dy_side]
    dy_parts.append(tp_swap(after(dy_side, out_2[0]), 0))
    near_sum = fold(out_near, F32)
    attended = near_sum + after(tp_swap(side, bits - 1), out_near[0]).astype(F32)
    if nz == 4:
        third = shift(after(second, near_sum), [(2, 3)])
        outer = (weight, from_outer, second, third)
        inner = (from_inner, weight, from_outer, second)
    else:
        every = lax.all_gather(weight, "z", axis=0, tiled=True)
        every = lax.dynamic_slice_in_dim(every, ic * mine, mine, 0)
        outer, inner = (every[:cut],), (every[cut:],)
    x1 = (after(x, second, dy_side, from_inner) if nz == 4 else x) + attended
    r2 = lax.rsqrt(jnp.mean(x1 * x1, axis=-1, keepdims=True) + EPSILON)
    n2 = x1 * r2
    h2 = (n2 * norm2_gain).astype(BF16)

    router_wide = jnp.pad(w_router, ((0, 0), (0, LANES - experts)))
    h2_side = y_swap(h2)
    h2_parts = [h2, tp_swap(h2, 0), h2_side]
    head = along.astype(jnp.int32)[None]
    outer_ids = jnp.concatenate([head, ids[:cut].astype(jnp.int32)])
    inner_ids = jnp.concatenate([head, ids[cut:].astype(jnp.int32)])
    through = lambda s, at, w, old=(): run_experts(
        s, h2_parts[at : at + 2], dy_parts[at : at + 2], router_wide, w, experts, 8 * cut, old
    )
    first = through(inner_ids, 0, inner)
    h2_parts.append(tp_swap(after(h2_side, first[4]), 0))
    third_pass = through(inner_ids, 2, inner)
    near = through(after(outer_ids, third_pass[4]), 0, outer, first[:4])
    far = through(after(outer_ids, near[4]), 2, outer, third_pass[:4])

    join = lambda a, b: (a.astype(F32) + tp_swap(b, 0).astype(F32)).astype(BF16)
    dh_side = join(far[2], far[3])
    dh_own = near[2].astype(F32) + tp_swap(near[3], 0).astype(F32)
    grads_outer = expert_grads(
        [after(h2_parts[0], dh_side), *h2_parts[1:]], dy_parts, (near[4], far[4]), (near[5], far[5])
    )
    grads_inner = expert_grads(
        [after(h2_parts[0], grads_outer), *h2_parts[1:]],
        dy_parts,
        (first[4], third_pass[4]),
        (first[5], third_pass[5]),
    )
    mixed_side = join(far[0], after(far[1], grads_outer))
    mixed_core = tp_swap(after(near[1], grads_outer), 0)
    dh_sum = after(dh_own, grads_inner, mixed_side, mixed_core) + after(y_swap(dh_side), grads_outer).astype(F32)
    probs = jax.nn.softmax(dot(h2, w_router), axis=-1)
    dprobs = dh_sum[:, width : width + experts]
    dprobs = dprobs + dh_sum[:, width + LANES // 2 : width + LANES // 2 + experts]
    dlogits = (
        probs * (dprobs - jnp.sum(probs * dprobs, axis=-1, keepdims=True))
    ).astype(BF16)
    dh2 = dot(dlogits, w_router, 1, 1) + dh_sum[:, :width]
    scaled = dh2 * norm2_gain
    dx1 = grad_out.astype(F32) + r2 * (
        scaled - n2 * jnp.mean(scaled * n2, axis=-1, keepdims=True)
    )
    router_part = dot(dlogits, h2, 0, 0)
    gain2 = jnp.sum(dh2 * n2, axis=0, keepdims=True)

    if nz == 4:
        reduce = lambda g, axis: lax.psum_scatter(g, axis, scatter_dimension=0, tiled=True)
        inner, outer = reduce(grads_inner[0], "z"), reduce(grads_outer[0], "z")
    else:
        inner, outer = grads_inner, grads_outer

    da = dx1.astype(BF16)
    da_parts = {0: da}
    for bit in reversed(range(bits)):
        for i in list(da_parts):
            if i < half:
                da_parts[i | (1 << bit)] = tp_swap(da_parts[i], bit)
    back = lambda q, o, lse, da, base, sums: attend_back(
        scalars, q, o, lse, k, kt, v, cos, sin, w_out, da, rows, zone, base, sums
    )
    near_parts = [da_parts[i] for i in range(half)]
    dq_near, *sums = back(q_near, o_near, lse_near, near_parts, 0, None)
    da_parts[half] = after(da_parts[half], dq_near)
    for bit in reversed(range(bits - 1)):
        for i in list(da_parts):
            if i >= half:
                da_parts[i | (1 << bit)] = tp_swap(da_parts[i], bit)
    da_parts = [da_parts[i] for i in range(blocks)]
    mixed_side = y_swap(after(mixed_side, da))
    out_part = out_grads(
        [after(da_parts[0], dq_near, mixed_side), *da_parts[1:half]], o_near, None
    )
    out_part = out_grads(da_parts[half:], o_far, out_part)
    each = width // (2 * nz)

    def pick(grad, at):
        grad = grad.reshape(nz, 2, each, grad.shape[1])
        return lax.dynamic_index_in_dim(grad, at, 1, keepdims=False)

    before = [out_part]
    if nz == 4:

        def x_reduce(g, cover):
            pick_rows = lambda at: lax.dynamic_slice_in_dim(g, at * (width // 8), width // 8, 0)
            other = after(tp_swap(pick_rows(1 - ix), 1), cover)
            return (pick_rows(ix).astype(F32) + other.astype(F32)).astype(BF16)

        before.append(outer)
    dq_far, dkv = back(after(q_far, *before), o_far, lse_far, da_parts[half:], half, sums)
    out_side = after(y_swap(pick(out_part, 1 - iy)), dkv)
    qkv_grad, gain1 = qkv_grads(
        h_parts, dq_near, dq_far, dkv, w_all_t, norm1_gain)
    qkv_side = y_swap(pick(qkv_grad, 1 - iy))
    dh1_far = input_grads(after(dq_far, qkv_grad), dkv, w_all_t, rows, 1)
    qkv_side = after(qkv_side, dh1_far[0])
    dh1_side = fold(dh1_far, BF16)
    dh1_near = input_grads(
        dq_near, after(dkv, dh1_side, qkv_side), w_all_t, rows, 0
    )
    dh1 = fold(dh1_near, F32) + after(tp_swap(dh1_side, bits - 1), dh1_near[0]).astype(F32)
    output = after(x1, dh1_side) + near[0].astype(F32) + mixed_core.astype(F32) + mixed_side.astype(F32)
    n1 = x * r1
    scaled = dh1 * norm1_gain
    grad_input = dx1 + r1 * (scaled - n1 * jnp.mean(scaled * n1, axis=-1, keepdims=True))

    summed = jnp.concatenate(
        [
            after(pick(qkv_grad, iy), dh1_side).astype(F32) + qkv_side.astype(F32),
            pick(out_part, iy).astype(F32) + out_side.astype(F32),
        ],
        axis=2,
    )
    summed = lax.psum_scatter(
        summed.astype(BF16).reshape(nz * each, -1), "z", scatter_dimension=0, tiled=True
    ).astype(F32)
    grad_qkv, grad_outproj = summed[:, : q_cols + 2 * kv_cols], summed[:, q_cols + 2 * kv_cols :].T
    small = jnp.concatenate([router_part, gain2, gain1], axis=0)
    small = own_columns(sum_all(after(small, dh1_side)))
    if nz == 4:
        outer = x_reduce(outer, dkv)
        inner = x_reduce(after(inner, dh1_side), dh1_near[0])
        outer = after(outer, dh1_side)
        home = lambda c, inside: (3 - inside if c else inside)
        moves = [
            [
                ((z * 2 + x_) * 2 + c, home(c, int(x_ == first_)) * 4 + z)
                for z in range(4)
                for x_ in range(2)
                for c in range(2)
            ]
            for first_ in range(2)
        ]
        zxc = ("z", "x", "c")
        one = lax.ppermute(jnp.where(ix == 0, inner, outer), zxc, moves[0])
        two = lax.ppermute(jnp.where(ix == 0, outer, inner), zxc, moves[1])
        inside = (iz == 1) | (iz == 2)
        part = jnp.concatenate(
            [jnp.where(inside, one, two), jnp.where(inside, two, one)], axis=0
        ).astype(F32)
    else:
        stacked = jnp.concatenate([grads_outer, grads_inner], axis=0)
        every = jnp.zeros((nz, width, 3 * hidden), BF16)
        every = lax.dynamic_update_slice_in_dim(every, stacked, ic * mine, 0)
        part = lax.psum_scatter(
            every.reshape(nz * width, 3 * hidden), "z", scatter_dimension=0, tiled=True
        )
        part = lax.psum_scatter(part, ("x", "c"), scatter_dimension=0, tiled=True).astype(F32)
    grad_gate = part[None, :, :hidden]
    grad_up = part[None, :, hidden : 2 * hidden]
    grad_down = part[:, 2 * hidden :].T[None]
    return (
        output,
        grad_input,
        small[experts + 1],
        grad_qkv[:, :q_cols],
        grad_qkv[:, q_cols : q_cols + kv_cols],
        grad_qkv[:, q_cols + kv_cols :],
        grad_outproj,
        small[experts],
        small[:experts].T,
        grad_gate,
        grad_up,
        grad_down,
    )


def solution(mesh):
    ep, tp = mesh.shape["ep"], mesh.shape["tp"]
    nz, nx = ep // 2, tp // 2
    grid = Mesh(mesh.devices.reshape(nz, 2, nx, 2), ("z", "y", "x", "c"))
    e, t = ("z", "y"), ("x", "c")
    every = ("z", "y", "x", "c")
    return jax.shard_map(
        functools.partial(body, (nz, nx)),
        mesh=grid,
        in_specs=(
            P(every, None),
            P(),
            P(None, t),
            P(None, t),
            P(None, t),
            P(t, None),
            P(),
            P(),
            P(e, None, None),
            P(e, None, None),
            P(e, None, None),
            P(every, None),
            P(e, None),
            P(e, None),
            P(every, None),
        ),
        out_specs=(
            P(every, None),
            P(every, None),
            P(every),
            P(e, t),
            P(e, t),
            P(e, t),
            P(t, e),
            P(every),
            P(every, None),
            P(e, t, None),
            P(e, t, None),
            P(e, None, t),
        ),
        check_vma=False,
    )
```

```python
import functools
import math

import jax
import jax.numpy as jnp
from jax import lax
from jax.experimental import pallas as pl
from jax.experimental.pallas import tpu as pltpu
from jax.sharding import Mesh, PartitionSpec as P

HEAD_SIZE = 64
HALF = HEAD_SIZE // 2
SEQUENCE_LENGTH = 2048
EPSILON = 1e-05
ROPE_BASE = 10000.0
MASK_FILL = -1e30
LANES = 128
F32 = jnp.float32
BF16 = jnp.bfloat16
VMEM_LIMIT = 60 * 1024 * 1024


def dot(a, b, ca=1, cb=0):
    return lax.dot_general(a, b, (((ca,), (cb,)), ((), ())), preferred_element_type=F32)


def after(value, *deps):
    return lax.optimization_barrier((value, *deps))[0]


def cost(micros):
    return pl.CostEstimate(
        flops=int(micros * 1e+09), transcendentals=0, bytes_accessed=int(micros * 3e+06)
    )


def params():
    return pltpu.CompilerParams(vmem_limit_bytes=VMEM_LIMIT)


def once(shape):
    return pl.BlockSpec(shape, lambda *_: (0,) * len(shape), pipeline_mode=pl.Buffered(1))


def qkv_kernel(q_cols, kv_cols, parts, *refs):
    h_refs, (w_ref, cos_ref, sin_ref) = refs[:parts], refs[parts : parts + 3]
    q_ref, k_ref, kt_ref, v_ref, vt_ref = refs[-5:]
    rows = h_refs[0].shape[0]
    scale = jnp.asarray(1.0 / math.sqrt(HEAD_SIZE), BF16)
    for b in range(parts):
        here = slice(b * rows, (b + 1) * rows)
        y = dot(w_ref[...], h_refs[b][...], 1, 1)
        cos, sin = cos_ref[:, here], sin_ref[:, here]

        def turned(base):
            a = y[base : base + HALF]
            b = y[base + HALF : base + HEAD_SIZE]
            return jnp.concatenate([a * cos - b * sin, b * cos + a * sin], axis=0)

        for h in range(q_cols // HEAD_SIZE):
            base = h * HEAD_SIZE
            q_ref[base : base + HEAD_SIZE, here] = turned(base).astype(BF16) * scale
        for g in range(kv_cols // HEAD_SIZE):
            base = g * HEAD_SIZE
            kt = turned(q_cols + base)
            kt_ref[base : base + HEAD_SIZE, here] = kt.astype(BF16)
            k_ref[g, here, :] = kt.T.astype(BF16)
            vt = y[q_cols + kv_cols + base : q_cols + kv_cols + base + HEAD_SIZE]
            vt_ref[base : base + HEAD_SIZE, here] = vt.astype(BF16)
            v_ref[g, here, :] = vt.T.astype(BF16)


def project_qkv(h_parts, w_all, cos, sin, q_cols, kv_cols, half, previous):
    parts = len(h_parts)
    rows, width = h_parts[0].shape
    size = parts * rows
    groups = kv_cols // HEAD_SIZE
    cols = q_cols + 2 * kv_cols
    lane_block = lambda *_: (0, half)
    row_block = lambda *_: (0, half, 0)
    kv_shapes = [
        jax.ShapeDtypeStruct((groups, 2 * size, HEAD_SIZE), BF16),
        jax.ShapeDtypeStruct((kv_cols, 2 * size), BF16),
    ] * 2
    kv_specs = [
        pl.BlockSpec((groups, size, HEAD_SIZE), row_block),
        pl.BlockSpec((kv_cols, size), lane_block),
    ] * 2
    previous = list(previous or ())
    return pl.pallas_call(
        functools.partial(qkv_kernel, q_cols, kv_cols, parts),
        grid=(1,),
        in_specs=[once((rows, width))] * parts
        + [
            once((cols, width)),
            pl.BlockSpec((HALF, size), lane_block),
            pl.BlockSpec((HALF, size), lane_block),
        ]
        + [pl.BlockSpec(memory_space=pl.ANY)] * len(previous),
        out_specs=[once((q_cols, size))] + kv_specs,
        out_shape=[jax.ShapeDtypeStruct((q_cols, size), BF16)] + kv_shapes,
        input_output_aliases={parts + 3 + i: 1 + i for i in range(len(previous))},
        compiler_params=params(),
        cost_estimate=cost(6),
        name="qkv",
    )(*h_parts, w_all, cos, sin, *previous)


def last_key(s_ref, zone, own, rows):
    zone_index = own * rows // zone
    zones = SEQUENCE_LENGTH // zone
    start = s_ref[1 + zone_index]
    stop = start + s_ref[1 + zones + zone_index]
    position = own * rows + lax.broadcasted_iota(jnp.int32, (1, rows), 1)
    return jnp.where((position >= start) & (position < stop), stop - 1, position)


def block_walk(me, own, rows, zone, pair):
    per_zone = zone // rows
    pair(own, True, True)
    for other in range(1, per_zone):
        pair(own ^ other, True, False)
    first = (own // per_zone) * per_zone

    def step(key_block, carry):
        pair(key_block, False, False)
        return carry

    lax.fori_loop(0, first, step, 0)


def attend_kernel(
    rows, zone, heads, groups, base, s_ref, q_ref, k_ref, vt_ref, w_ref, o_ref, lse_ref, *refs
):
    out_refs, (acc, top, total) = refs[:-3], refs[-3:]
    me = s_ref[0]
    own = me ^ (pl.program_id(0) + base)
    limit = last_key(s_ref, zone, own, rows)

    def pair(key_block, masked, first):
        offset = pl.multiple_of((me ^ key_block) * rows, rows)
        if masked:
            key_pos = key_block * rows + lax.broadcasted_iota(jnp.int32, (rows, rows), 0)
            allowed = key_pos <= limit
        for h in range(heads):
            g = h // (heads // groups)
            r = slice(h * HEAD_SIZE, (h + 1) * HEAD_SIZE)
            s = dot(k_ref[g, pl.ds(offset, rows), :], q_ref[r, :])
            if masked:
                s = jnp.where(allowed, s, MASK_FILL)
            peak = jnp.max(s, axis=0, keepdims=True)
            vt = vt_ref[g * HEAD_SIZE : (g + 1) * HEAD_SIZE, pl.ds(offset, rows)]
            if first:
                p = jnp.exp(s - peak)
                top[h : h + 1, :] = peak
                total[h : h + 1, :] = jnp.sum(p, axis=0, keepdims=True)
                acc[r, :] = dot(vt, p.astype(BF16))
            else:
                old = top[h : h + 1, :]
                new = jnp.maximum(old, peak)
                fade = jnp.exp(old - new)
                p = jnp.exp(s - new)
                top[h : h + 1, :] = new
                total[h : h + 1, :] = total[h : h + 1, :] * fade + jnp.sum(p, axis=0, keepdims=True)
                acc[r, :] = acc[r, :] * fade + dot(vt, p.astype(BF16))

    block_walk(me, own, rows, zone, pair)
    for h in range(heads):
        r = slice(h * HEAD_SIZE, (h + 1) * HEAD_SIZE)
        o_ref[r, :] = (acc[r, :] / total[h : h + 1, :]).astype(BF16)
        lse_ref[h : h + 1, :] = top[h : h + 1, :] + jnp.log(total[h : h + 1, :])
    for b, out_ref in enumerate(out_refs):

        @pl.when(pl.program_id(0) == b)
        def _():
            out_ref[...] = dot(o_ref[...], w_ref[...], 0, 0).astype(BF16)


def attend(scalars, q, at, count, k, vt, w_out, rows, zone, base, micros):
    q_cols = q.shape[0]
    size = count * rows
    groups = k.shape[0]
    width = w_out.shape[1]
    heads = q_cols // HEAD_SIZE
    block = lambda i, s: (0, i)
    return pl.pallas_call(
        functools.partial(attend_kernel, rows, zone, heads, groups, base),
        grid_spec=pltpu.PrefetchScalarGridSpec(
            num_scalar_prefetch=1,
            grid=(count,),
            in_specs=[
                pl.BlockSpec((q_cols, rows), lambda i, s: (0, i + at)),
                once(k.shape),
                once(vt.shape),
                once(w_out.shape),
            ],
            out_specs=[
                pl.BlockSpec((q_cols, rows), block),
                pl.BlockSpec((heads, rows), block),
            ]
            + [once((rows, width))] * count,
            scratch_shapes=[
                pltpu.VMEM((q_cols, rows), F32),
                pltpu.VMEM((8, rows), F32),
                pltpu.VMEM((8, rows), F32),
            ],
        ),
        out_shape=[
            jax.ShapeDtypeStruct((q_cols, size), BF16),
            jax.ShapeDtypeStruct((heads, size), F32),
        ]
        + [jax.ShapeDtypeStruct((rows, width), BF16)] * count,
        compiler_params=params(),
        cost_estimate=cost(micros),
        name="attend",
    )(scalars, q, k, vt, w_out)


def attend_back_kernel(rows, zone, heads, groups, base, parts, *refs):
    s_ref, q_ref, o_ref, lse_ref, k_ref, kt_ref, v_ref, cos_ref, sin_ref, w_ref = refs[:10]
    da_refs = refs[10 : 10 + parts]
    rest = refs[10 + parts :]
    if base:
        old_dk, old_dv, dq_ref, dkv_ref, dq, dk, dv, delta, do_ref = rest
    else:
        dq_ref, dk, dv, dq, delta, do_ref = rest
    me = s_ref[0]
    step = pl.program_id(0)
    own = me ^ (step + base)
    limit = last_key(s_ref, zone, own, rows)
    here = pl.multiple_of((step + base) * rows, rows)

    @pl.when(step == 0)
    def _():
        for b in range(parts):
            do_ref[b] = dot(w_ref[...], da_refs[b][...], 1, 1).astype(BF16)
        if base:
            dk[...] = old_dk[...]
            dv[...] = old_dv[...]
        else:
            dk[...] = jnp.zeros_like(dk)
            dv[...] = jnp.zeros_like(dv)

    for h in range(heads):
        r = slice(h * HEAD_SIZE, (h + 1) * HEAD_SIZE)
        delta[h : h + 1, :] = jnp.sum(
            do_ref[step, r, :].astype(F32) * o_ref[r, :].astype(F32), axis=0, keepdims=True
        )

    def pair(key_block, masked, first):
        offset = pl.multiple_of((me ^ key_block) * rows, rows)
        keys = pl.ds(offset, rows)
        if masked:
            key_pos = key_block * rows + lax.broadcasted_iota(jnp.int32, (rows, rows), 0)
            allowed = key_pos <= limit
        for g in range(groups):
            kb = k_ref[g, keys, :]
            vb = v_ref[g, keys, :]
            kt = kt_ref[g * HEAD_SIZE : (g + 1) * HEAD_SIZE, keys]
            dk_sum = dk[g, keys, :]
            dv_sum = dv[g, keys, :]
            for h in range(g * (heads // groups), (g + 1) * (heads // groups)):
                r = slice(h * HEAD_SIZE, (h + 1) * HEAD_SIZE)
                do = do_ref[step, r, :]
                s = dot(kb, q_ref[r, :])
                if masked:
                    s = jnp.where(allowed, s, MASK_FILL)
                p = jnp.exp(s - lse_ref[h : h + 1, :])
                dp = dot(vb, do)
                ds = (p * (dp - delta[h : h + 1, :])).astype(BF16)
                dv_sum = dv_sum + dot(p.astype(BF16), do, 1, 1)
                dk_sum = dk_sum + dot(ds, q_ref[r, :], 1, 1)
                part = dot(kt, ds)
                dq[r, :] = part if first else dq[r, :] + part
            dk[g, keys, :] = dk_sum
            dv[g, keys, :] = dv_sum

    block_walk(me, own, rows, zone, pair)
    cos, sin = cos_ref[:, pl.ds(here, rows)], sin_ref[:, pl.ds(here, rows)]
    scale = 1.0 / math.sqrt(HEAD_SIZE)
    for h in range(heads):
        at = h * HEAD_SIZE
        a = dq[at : at + HALF, :] * scale
        b = dq[at + HALF : at + HEAD_SIZE, :] * scale
        dq_ref[at : at + HALF, :] = (a * cos + b * sin).astype(BF16)
        dq_ref[at + HALF : at + HEAD_SIZE, :] = (b * cos - a * sin).astype(BF16)

    if base:

        @pl.when(step == pl.num_programs(0) - 1)
        def _():
            every_cos, every_sin = cos_ref[...], sin_ref[...]
            for g in range(groups):
                at = g * HEAD_SIZE
                turned = dk[g].T
                a, b = turned[:HALF], turned[HALF:]
                dkv_ref[at : at + HALF, :] = (a * every_cos + b * every_sin).astype(BF16)
                dkv_ref[at + HALF : at + HEAD_SIZE, :] = (b * every_cos - a * every_sin).astype(BF16)
                at = (groups + g) * HEAD_SIZE
                dkv_ref[at : at + HEAD_SIZE, :] = dv[g].T.astype(BF16)


def attend_back(scalars, q, o, lse, k, kt, v, cos, sin, w_out, da_parts, rows, zone, base, sums):
    q_cols, size = q.shape
    groups, total, _ = k.shape
    heads = q_cols // HEAD_SIZE
    parts = len(da_parts)
    block = lambda i, s: (0, i)
    sum_shape = (groups, total, HEAD_SIZE)
    inputs = [q, o, lse, k, kt, v, cos, sin, w_out, *da_parts]
    in_specs = [
        pl.BlockSpec((q_cols, rows), block),
        pl.BlockSpec((q_cols, rows), block),
        pl.BlockSpec((heads, rows), block),
    ] + [once(a.shape) for a in inputs[3:]]
    out_specs = [pl.BlockSpec((q_cols, rows), block)]
    out_shape = [jax.ShapeDtypeStruct((q_cols, size), BF16)]
    scratch = [pltpu.VMEM((q_cols, rows), F32)]
    if base:
        inputs += list(sums)
        in_specs += [once(sum_shape)] * 2
        out_specs += [once((2 * groups * HEAD_SIZE, total))]
        out_shape += [jax.ShapeDtypeStruct((2 * groups * HEAD_SIZE, total), BF16)]
        scratch += [pltpu.VMEM(sum_shape, F32)] * 2
    else:
        out_specs += [once(sum_shape)] * 2
        out_shape += [jax.ShapeDtypeStruct(sum_shape, F32)] * 2
    scratch += [pltpu.VMEM((8, rows), F32), pltpu.VMEM((parts, q_cols, rows), BF16)]
    return pl.pallas_call(
        functools.partial(attend_back_kernel, rows, zone, heads, groups, base, parts),
        grid_spec=pltpu.PrefetchScalarGridSpec(
            num_scalar_prefetch=1,
            grid=(size // rows,),
            in_specs=in_specs,
            out_specs=out_specs,
            scratch_shapes=scratch,
        ),
        out_shape=out_shape,
        compiler_params=params(),
        cost_estimate=cost(30),
        name="attend_back",
    )(scalars, *inputs)


def input_grad_kernel(dq_ref, dkv_ref, w_ref, *out_refs):
    q_cols = dq_ref.shape[0]
    rows = out_refs[0].shape[0]
    for b, out_ref in enumerate(out_refs):
        here = slice(b * rows, (b + 1) * rows)
        out = dot(dq_ref[:, here], w_ref[:q_cols, :], 0, 0)
        out = out + dot(dkv_ref[:, here], w_ref[q_cols:, :], 0, 0)
        out_ref[...] = out.astype(BF16)


def input_grads(dq, dkv, w_all_t, rows, half):
    q_cols, size = dq.shape
    cols, width = w_all_t.shape
    count = size // rows
    return pl.pallas_call(
        input_grad_kernel,
        grid=(1,),
        in_specs=[
            once((q_cols, size)),
            pl.BlockSpec((cols - q_cols, size), lambda i: (0, half)),
            once((cols, width)),
        ],
        out_specs=[once((rows, width))] * count,
        out_shape=[jax.ShapeDtypeStruct((rows, width), BF16)] * count,
        compiler_params=params(),
        cost_estimate=cost(5),
        name="input_grads",
    )(dq, dkv, w_all_t)


def qkv_grad_kernel(parts, *refs):
    h_refs = refs[: 2 * parts]
    near_ref, far_ref, dkv_ref, w_ref, gain_ref, grad_ref, gain_grad_ref = refs[2 * parts :]
    rows = h_refs[0].shape[0]
    sums = [0.0, 0.0]
    for b in range(2 * parts):
        dq_ref, at = (near_ref, b) if b < parts else (far_ref, b - parts)
        h = h_refs[b][...]
        sums[0] = sums[0] + dot(dq_ref[:, at * rows : (at + 1) * rows], h)
        sums[1] = sums[1] + dot(dkv_ref[:, b * rows : (b + 1) * rows], h)
    q_cols = near_ref.shape[0]
    grad_ref[:, :q_cols] = sums[0].T.astype(BF16)
    grad_ref[:, q_cols:] = sums[1].T.astype(BF16)
    gain = jnp.sum(sums[0] * w_ref[:q_cols, :].astype(F32), axis=0, keepdims=True)
    gain = gain + jnp.sum(sums[1] * w_ref[q_cols:, :].astype(F32), axis=0, keepdims=True)
    gain_grad_ref[...] = gain / gain_ref[...]


def qkv_grads(h_parts, dq_near, dq_far, dkv, w_all_t, gain):
    cols, width = w_all_t.shape
    inputs = [*h_parts, dq_near, dq_far, dkv, w_all_t, gain[None, :]]
    return pl.pallas_call(
        functools.partial(qkv_grad_kernel, len(h_parts) // 2),
        grid=(1,),
        in_specs=[once(a.shape) for a in inputs],
        out_specs=[once((width, cols)), once((1, width))],
        out_shape=[
            jax.ShapeDtypeStruct((width, cols), BF16),
            jax.ShapeDtypeStruct((1, width), F32),
        ],
        compiler_params=params(),
        cost_estimate=cost(10),
        name="qkv_grads",
    )(*inputs)


def out_grad_kernel(parts, finish, *refs):
    da_refs, o_ref, grad_ref = refs[:parts], refs[parts], refs[-1]
    rows = da_refs[0].shape[0]
    total = refs[parts + 1][...] if finish else 0.0
    for b in range(parts):
        total = total + dot(o_ref[:, b * rows : (b + 1) * rows], da_refs[b][...])
    grad_ref[...] = total.T.astype(BF16) if finish else total


def out_grads(da_parts, o, previous):
    q_cols, width = o.shape[0], da_parts[0].shape[1]
    inputs = [*da_parts, o] + ([] if previous is None else [previous])
    finish = previous is not None
    shape = (width, q_cols) if finish else (q_cols, width)
    return pl.pallas_call(
        functools.partial(out_grad_kernel, len(da_parts), finish),
        grid=(1,),
        in_specs=[once(a.shape) for a in inputs],
        out_specs=once(shape),
        out_shape=jax.ShapeDtypeStruct(shape, BF16 if finish else F32),
        compiler_params=params(),
        cost_estimate=cost(4),
        name="out_grads",
    )(*inputs)


def expert_kernel(experts, adds, choices, alone, *refs):
    s_ref, h0, h1, dy0, dy1, router_ref = refs[:6]
    w_choices = refs[6 : 6 + choices]
    old = refs[6 + choices : 6 + choices + (4 if adds else 0)]
    outs = refs[len(refs) - 19 :]
    mix0, mix1, dh0, dh1, act_out, dgu_out = outs[:6]
    h_s, dy_s, w_s, mix_s, dh_s, gates, dgate, mix_o, dh_o, act_o, dgu_o, in_sem, out_sem = outs[6:]
    e = pl.program_id(0)
    last = pl.num_programs(0) - 1
    rows, width = h0.shape
    hidden = w_s.shape[2] // 3
    lane = lax.broadcasted_iota(jnp.int32, (rows, LANES), 1)
    slot = lax.rem(e, 2)

    def fetch_weights(index, into):
        for n in range(choices):

            @pl.when(s_ref[0] == n)
            def _():
                pltpu.make_async_copy(
                    w_choices[n].at[index], w_s.at[into], in_sem.at[4 + into]
                ).start()

    tokens_in = [
        pltpu.make_async_copy(src, dst, in_sem.at[n])
        for n, (src, dst) in enumerate(
            ((h0, h_s.at[0]), (dy0, dy_s.at[0]), (h1, h_s.at[1]), (dy1, dy_s.at[1]))
        )
    ]
    old_in = [
        pltpu.make_async_copy(src, dst, in_sem.at[6 + n])
        for n, (src, dst) in enumerate(zip(old, (mix_o.at[0], mix_o.at[1], dh_o.at[0], dh_o.at[1])))
    ]

    @pl.when(e == 0)
    def _():
        tokens_in[0].start()
        fetch_weights(0, 0)
        for copy in tokens_in[1:] + old_in:
            copy.start()

    @pl.when(e < last)
    def _():
        fetch_weights(e + 1, 1 - slot)

    def block(i, carry):
        for n in range(2):

            @pl.when((e == 0) & (i == n))
            def _():
                tokens_in[2 * n].wait()
                tokens_in[2 * n + 1].wait()
                for copy in old_in[n::2]:
                    copy.wait()

        @pl.when(e == 0)
        def _():
            logits = dot(h_s[i], router_ref[...])
            logits = jnp.where(lane < experts, logits, MASK_FILL)
            weights = jnp.exp(logits - jnp.max(logits, axis=1, keepdims=True))
            weights = weights / jnp.sum(weights, axis=1, keepdims=True)
            gates[i] = weights * dy_s[i, :, width:].astype(F32)

        @pl.when(i == 0)
        def _():
            pltpu.make_async_copy(w_choices[0].at[0], w_s.at[slot], in_sem.at[4 + slot]).wait()

        mine = lane == s_ref[1 + e]
        gate = jnp.sum(jnp.where(mine, gates[i], 0.0), axis=1, keepdims=True)
        both = dot(h_s[i], w_s[slot, :, : 2 * hidden])
        gp, up = both[:, :hidden], both[:, hidden:]
        sg = jax.nn.sigmoid(gp)
        silu = gp * sg
        act = (silu * up).astype(BF16).astype(F32)
        dact = dot(dy_s[i, :, :width], w_s[slot, :, 2 * hidden :])
        chosen = dy_s[i, :, width:].astype(F32)
        own_dgate = jnp.where(mine, chosen * jnp.sum(act * dact, axis=1, keepdims=True), 0.0)
        scaled = (gate * act).astype(BF16)
        dact = gate * dact
        dgp = (dact * up * sg * (1.0 + gp * (1.0 - sg))).astype(BF16)
        dup = (dact * silu).astype(BF16)
        here = pl.ds(pl.multiple_of(i * rows, rows), rows)
        act_copy = pltpu.make_async_copy(act_o.at[i], act_out.at[e, here, :], out_sem.at[i])
        dgu_copy = pltpu.make_async_copy(dgu_o.at[i], dgu_out.at[e, here, :], out_sem.at[2 + i])

        @pl.when(e > 0)
        def _():
            act_copy.wait()
            dgu_copy.wait()

        act_o[i] = scaled
        dgu_o[i, :, :hidden] = dgp
        dgu_o[i, :, hidden:] = dup
        act_copy.start()
        dgu_copy.start()
        mix = dot(scaled, w_s[slot, :, 2 * hidden :], 1, 1)
        dh = dot(dgu_o[i], w_s[slot, :, : 2 * hidden], 1, 1)

        def finish(mix, dh, own_dgate):
            mix_o[i] = mix.astype(BF16)
            dh_o[i, :, :width] = dh.astype(BF16)
            high = own_dgate.astype(BF16).astype(F32)
            low = own_dgate - high
            dh_o[i, :, width:] = (high + pltpu.roll(low, LANES // 2, 1)).astype(BF16)

        if adds:
            kept = dh_o[i, :, width:].astype(F32)
            kept = kept + pltpu.roll(kept, LANES // 2, 1)
            kept = jnp.where(lane < LANES // 2, kept, 0.0)
        if adds and alone:
            finish(mix + mix_o[i].astype(F32), dh + dh_o[i, :, :width].astype(F32), own_dgate + kept)
        elif alone:
            finish(mix, dh, own_dgate)
        else:

            @pl.when(e == 0)
            def _():
                if adds:
                    mix_s[i] = mix + mix_o[i].astype(F32)
                    dh_s[i] = dh + dh_o[i, :, :width].astype(F32)
                    dgate[i] = own_dgate + kept
                else:
                    mix_s[i] = mix
                    dh_s[i] = dh
                    dgate[i] = own_dgate

            @pl.when(e > 0)
            def _():
                mix_s[i] += mix
                dh_s[i] += dh
                dgate[i] += own_dgate

            @pl.when(e == last)
            def _():
                finish(mix_s[i], dh_s[i], dgate[i])

        for n in range(2):

            @pl.when((e == last) & (i == n))
            def _():
                pltpu.make_async_copy(mix_o.at[n], (mix0, mix1)[n], out_sem.at[4 + n]).start()
                pltpu.make_async_copy(dh_o.at[n], (dh0, dh1)[n], out_sem.at[6 + n]).start()

        return carry

    lax.fori_loop(0, 2, block, 0)

    @pl.when(e == last)
    def _():
        for i in range(2):
            here = pl.ds(i * rows, rows)
            pltpu.make_async_copy(act_o.at[i], act_out.at[e, here, :], out_sem.at[i]).wait()
            pltpu.make_async_copy(dgu_o.at[i], dgu_out.at[e, here, :], out_sem.at[2 + i]).wait()
            pltpu.make_async_copy(mix_o.at[i], (mix0, mix1)[i], out_sem.at[4 + i]).wait()
            pltpu.make_async_copy(dh_o.at[i], (dh0, dh1)[i], out_sem.at[6 + i]).wait()


def run_experts(scalars, h_parts, dy_parts, router, choices, experts, micros, old=()):
    rows, width = h_parts[0].shape
    wide = width + LANES
    mine, _, cols = choices[0].shape
    hidden = cols // 3
    anywhere = pl.BlockSpec(memory_space=pl.ANY)
    return pl.pallas_call(
        functools.partial(expert_kernel, experts, bool(old), len(choices), mine == 1),
        grid_spec=pltpu.PrefetchScalarGridSpec(
            num_scalar_prefetch=1,
            grid=(mine,),
            in_specs=[anywhere] * 4 + [once((width, LANES))] + [anywhere] * (len(choices) + len(old)),
            out_specs=[anywhere] * 6,
            scratch_shapes=[
                pltpu.VMEM((2, rows, width), BF16),
                pltpu.VMEM((2, rows, wide), BF16),
                pltpu.VMEM((2, width, cols), BF16),
                pltpu.VMEM((2, rows, width), F32),
                pltpu.VMEM((2, rows, width), F32),
                pltpu.VMEM((2, rows, LANES), F32),
                pltpu.VMEM((2, rows, LANES), F32),
                pltpu.VMEM((2, rows, width), BF16),
                pltpu.VMEM((2, rows, wide), BF16),
                pltpu.VMEM((2, rows, hidden), BF16),
                pltpu.VMEM((2, rows, 2 * hidden), BF16),
                pltpu.SemaphoreType.DMA((10,)),
                pltpu.SemaphoreType.DMA((8,)),
            ],
        ),
        out_shape=[jax.ShapeDtypeStruct((rows, width), BF16)] * 2
        + [jax.ShapeDtypeStruct((rows, wide), BF16)] * 2
        + [
            jax.ShapeDtypeStruct((mine, 2 * rows, hidden), BF16),
            jax.ShapeDtypeStruct((mine, 2 * rows, 2 * hidden), BF16),
        ],
        compiler_params=params(),
        cost_estimate=cost(micros),
        name="experts",
    )(scalars, *h_parts, *dy_parts, router, *choices, *old)


def expert_grad_kernel(*refs):
    h_refs, dy_refs, acts, dgus = refs[:4], refs[4:8], refs[8:10], refs[10:12]
    out_ref, h_s, dy_s, act_s, dgu_s, sem = refs[12:]
    e = pl.program_id(0)
    rows, width = h_refs[0].shape
    hidden = act_s.shape[1]
    first, second = [], []
    for b in range(4):
        here = pl.ds(b * rows, rows)
        first.append(pltpu.make_async_copy(h_refs[b], h_s.at[here, :], sem.at[b]))
        second.append(
            pltpu.make_async_copy(dy_refs[b].at[:, pl.ds(0, width)], dy_s.at[here, :], sem.at[4 + b])
        )
    per_expert = []
    for b in range(2):
        here = pl.ds(2 * b * rows, 2 * rows)
        per_expert.append(pltpu.make_async_copy(dgus[b].at[e], dgu_s.at[here, :], sem.at[8 + b]))
    for b in range(2):
        here = pl.ds(2 * b * rows, 2 * rows)
        per_expert.append(pltpu.make_async_copy(acts[b].at[e], act_s.at[here, :], sem.at[10 + b]))
    for copy in per_expert[:2]:
        copy.start()

    @pl.when(e == 0)
    def _():
        for copy in first:
            copy.start()

    for copy in per_expert[2:]:
        copy.start()

    @pl.when(e == 0)
    def _():
        for copy in second:
            copy.start()
        for copy in first:
            copy.wait()

    for copy in per_expert[:2]:
        copy.wait()

    def rows_of(c):
        return pl.ds(pl.multiple_of(c * (width // 3), width // 3), width // 3)

    def gate_up(c, carry):
        out_ref[0, rows_of(c), : 2 * hidden] = dot(h_s[:, rows_of(c)], dgu_s[...], 0, 0).astype(BF16)
        return carry

    lax.fori_loop(0, 3, gate_up, 0)

    @pl.when(e == 0)
    def _():
        for copy in second:
            copy.wait()

    for copy in per_expert[2:]:
        copy.wait()

    def down(c, carry):
        out_ref[0, rows_of(c), 2 * hidden :] = dot(dy_s[:, rows_of(c)], act_s[...], 0, 0).astype(BF16)
        return carry

    lax.fori_loop(0, 3, down, 0)


def expert_grads(h_parts, dy_parts, acts, dgus):
    rows, width = h_parts[0].shape
    mine, _, hidden = acts[0].shape
    anywhere = pl.BlockSpec(memory_space=pl.ANY)
    return pl.pallas_call(
        expert_grad_kernel,
        grid=(mine,),
        in_specs=[anywhere] * 12,
        out_specs=pl.BlockSpec((1, width, 3 * hidden), lambda e: (e, 0, 0)),
        out_shape=jax.ShapeDtypeStruct((mine, width, 3 * hidden), BF16),
        scratch_shapes=[
            pltpu.VMEM((4 * rows, width), BF16),
            pltpu.VMEM((4 * rows, width), BF16),
            pltpu.VMEM((4 * rows, hidden), BF16),
            pltpu.VMEM((4 * rows, 2 * hidden), BF16),
            pltpu.SemaphoreType.DMA((12,)),
        ],
        compiler_params=params(),
        cost_estimate=cost(1),
        name="expert_grads",
    )(*h_parts, *dy_parts, *acts, *dgus)


def body(
    sizes,
    tokens,
    norm1_gain,
    w_query,
    key_weight,
    value_weight,
    w_out,
    norm2_gain,
    w_router,
    w_gate,
    w_up,
    w_down,
    routes,
    piece_first_position,
    piece_length,
    grad_out,
):
    nz, nx = sizes
    rows, width = tokens.shape
    blocks = 2 * nx
    half = blocks // 2
    q_cols, kv_cols = w_query.shape[1], key_weight.shape[1]
    experts = w_router.shape[1]
    hidden = w_gate.shape[2]
    zone = SEQUENCE_LENGTH // piece_length.shape[1]
    iz, iy, ix, ic = (lax.axis_index(a) for a in "zyxc")
    me = ix * 2 + ic

    def tp_swap(value, bit):
        if bit == 0:
            return lax.ppermute(value, "c", [(0, 1), (1, 0)])
        return lax.ppermute(value, "x", [(i, i ^ (1 << (bit - 1))) for i in range(nx)])

    def y_swap(value):
        return lax.ppermute(value, "y", [(0, 1), (1, 0)])

    bits = blocks.bit_length() - 1

    def fold(parts, kind):
        parts = dict(enumerate(parts))
        for bit in range(bits - 1):
            for i in sorted(parts, reverse=True):
                if i & (1 << bit):
                    parts[i] = tp_swap(parts[i], bit)
            for i in sorted(parts, reverse=True):
                if i & (1 << bit):
                    total = parts[i ^ (1 << bit)].astype(F32) + parts.pop(i).astype(F32)
                    parts[i ^ (1 << bit)] = total.astype(BF16 if bit < bits - 2 else kind)
        return parts[0]

    def sum_all(value):
        step = 1
        while step < nz:
            value = value + lax.ppermute(value, "z", [(i, i ^ step) for i in range(nz)])
            step *= 2
        value = value + y_swap(value)
        for bit in range(bits):
            value = value + tp_swap(value, bit)
        return value

    def own_columns(value):
        each = width // (nz * 4 * nx)
        index = (iz * 2 + iy) * blocks + me
        return lax.dynamic_slice_in_dim(value, index * each, each, 1)

    each = width // (2 * nz)

    def pick(grad, at):
        grad = grad.reshape(nz, 2, each, grad.shape[1])
        return lax.dynamic_index_in_dim(grad, at, 1, keepdims=False)

    x = tokens.astype(F32)
    r1 = lax.rsqrt(jnp.mean(x * x, axis=-1, keepdims=True) + EPSILON)
    h1 = (x * r1 * norm1_gain).astype(BF16)
    h_parts = {0: h1}
    for bit in reversed(range(bits)):
        for i in list(h_parts):
            if i < half:
                h_parts[i | (1 << bit)] = tp_swap(h_parts[i], bit)

    w_all = jnp.concatenate([w_query, key_weight, value_weight], axis=1)
    w_all_t = w_all.T
    order = me ^ jnp.arange(blocks, dtype=jnp.int32)
    position = (order[:, None] * rows + jnp.arange(rows, dtype=jnp.int32)[None, :]).reshape(-1)
    frequency = ROPE_BASE ** (-(jnp.arange(HALF, dtype=F32) * (2.0 / HEAD_SIZE)))
    angles = frequency[:, None] * position.astype(F32)[None, :]
    cos, sin = jnp.cos(angles), jnp.sin(angles)
    scalars = jnp.concatenate(
        [me.astype(jnp.int32)[None], piece_first_position[0], piece_length[0]]
    )
    near_rows = [h_parts[i] for i in range(half)]
    q_near, *kv = project_qkv(near_rows, w_all_t, cos, sin, q_cols, kv_cols, 0, None)
    h_parts[half] = after(h_parts[half], q_near)
    for bit in reversed(range(bits - 1)):
        for i in list(h_parts):
            if i >= half:
                h_parts[i | (1 << bit)] = tp_swap(h_parts[i], bit)
    h_parts = [h_parts[i] for i in range(blocks)]

    mask = jnp.zeros((rows, LANES), jnp.bool_)
    for j in range(routes.shape[1]):
        mask = mask | (routes[:, j : j + 1] == jnp.arange(LANES, dtype=jnp.int32)[None, :])
    dy_own = after(jnp.concatenate([grad_out, mask.astype(BF16)], axis=1), q_near)
    dy_side = y_swap(dy_own)

    mine = nz // 2
    cut = mine // 2
    weight = after(jnp.concatenate([w_gate[0], w_up[0], w_down[0].T], axis=1), h_parts[1])[None]
    if nz == 4:
        ids = jnp.where(ic == 0, jnp.arange(2), 3 - jnp.arange(2)) * 2 + iy
        along = jnp.where(ic == 0, iz, 3 - iz)

        def shift(value, moves):
            perm = [(s * 2, d * 2) for s, d in moves]
            perm += [((3 - s) * 2 + 1, (3 - d) * 2 + 1) for s, d in moves]
            return lax.ppermute(value, ("z", "c"), perm)

        from_outer = shift(weight, [(0, 1), (1, 2)])
        from_inner = shift(weight, [(1, 0)])
    else:
        ids = (ic * mine + jnp.arange(mine)) * 2 + iy
        along = ic * 0

    q_far, k, kt, v, vt = project_qkv(h_parts[half:], w_all_t, cos, sin, q_cols, kv_cols, 1, kv)
    quarter = half // 2
    run = lambda q, at, count, base, micros: attend(
        scalars, q, at, count, k, vt, w_out, rows, zone, base, micros
    )
    o_3, lse_3, *out_3 = run(q_far, quarter, quarter, half + quarter, 9)
    early = ()
    if nz == 4:
        early = (from_outer,)
        second = shift(after(from_outer, out_3[0]), [(1, 2), (2, 3)])
    o_2, lse_2, *out_2 = run(after(q_far, out_3[0], *early), 0, quarter, half, 2)
    side = fold([*out_2, *out_3], BF16)
    if nz == 4:
        o_near, lse_near, *out_near = run(after(q_near, side), 0, half, 0, 2)
    else:
        o_near, lse_near, *out_near = run(after(q_near, side), 0, half, 0, 2)
    o_far = jnp.concatenate([o_2, o_3], axis=1)
    lse_far = jnp.concatenate([lse_2, lse_3], axis=1)
    dy_parts = [dy_own, tp_swap(after(dy_own, out_3[0]), 0), dy_side]
    dy_parts.append(tp_swap(after(dy_side, out_2[0]), 0))
    near_sum = fold(out_near, F32)
    attended = near_sum + after(tp_swap(side, bits - 1), out_near[0]).astype(F32)
    if nz == 4:
        third = shift(after(second, near_sum), [(2, 3)])
        outer = (weight, from_outer, second, third)
        inner = (from_inner, weight, from_outer, second)
    else:
        every = lax.all_gather(weight, "z", axis=0, tiled=True)
        every = lax.dynamic_slice_in_dim(every, ic * mine, mine, 0)
        outer, inner = (every[:cut],), (every[cut:],)
    x1 = (after(x, second, dy_side, from_inner) if nz == 4 else x) + attended
    r2 = lax.rsqrt(jnp.mean(x1 * x1, axis=-1, keepdims=True) + EPSILON)
    n2 = x1 * r2
    h2 = (n2 * norm2_gain).astype(BF16)

    router_wide = jnp.pad(w_router, ((0, 0), (0, LANES - experts)))
    h2_side = y_swap(h2)
    h2_parts = [h2, tp_swap(h2, 0), h2_side]
    head = along.astype(jnp.int32)[None]
    outer_ids = jnp.concatenate([head, ids[:cut].astype(jnp.int32)])
    inner_ids = jnp.concatenate([head, ids[cut:].astype(jnp.int32)])
    through = lambda s, at, w, old=(): run_experts(
        s, h2_parts[at : at + 2], dy_parts[at : at + 2], router_wide, w, experts, 8 * cut, old
    )
    first = through(inner_ids, 0, inner)
    h2_parts.append(tp_swap(after(h2_side, first[4]), 0))
    third_pass = through(inner_ids, 2, inner)
    near = through(after(outer_ids, third_pass[4]), 0, outer, first[:4])
    far = through(after(outer_ids, near[4]), 2, outer, third_pass[:4])

    join = lambda a, b: (a.astype(F32) + tp_swap(b, 0).astype(F32)).astype(BF16)
    dh_side = join(far[2], far[3])
    dh_own = near[2].astype(F32) + tp_swap(near[3], 0).astype(F32)
    grads_inner = expert_grads(
        [after(h2_parts[0], dh_side), *h2_parts[1:]],
        dy_parts,
        (first[4], third_pass[4]),
        (first[5], third_pass[5]),
    )
    grads_outer = expert_grads(
        [after(h2_parts[0], grads_inner), *h2_parts[1:]],
        dy_parts,
        (near[4], far[4]),
        (near[5], far[5]),
    )
    dh_sum = after(dh_own, grads_outer) + after(y_swap(dh_side), grads_outer).astype(F32)
    probs = jax.nn.softmax(dot(h2, w_router), axis=-1)
    dprobs = dh_sum[:, width : width + experts]
    dprobs = dprobs + dh_sum[:, width + LANES // 2 : width + LANES // 2 + experts]
    dlogits = (
        probs * (dprobs - jnp.sum(probs * dprobs, axis=-1, keepdims=True))
    ).astype(BF16)
    dh2 = dot(dlogits, w_router, 1, 1) + dh_sum[:, :width]
    scaled = dh2 * norm2_gain
    dx1 = grad_out.astype(F32) + r2 * (
        scaled - n2 * jnp.mean(scaled * n2, axis=-1, keepdims=True)
    )
    router_part = dot(dlogits, h2, 0, 0)
    gain2 = jnp.sum(dh2 * n2, axis=0, keepdims=True)

    if nz == 4:
        reduce = lambda g: lax.psum_scatter(g, "z", scatter_dimension=0, tiled=True)
        inner, outer = reduce(grads_inner[0]), reduce(grads_outer[0])
    else:
        inner, outer = grads_inner, grads_outer

    da = dx1.astype(BF16)
    da_parts = {0: da}
    for bit in reversed(range(bits)):
        for i in list(da_parts):
            if i < half:
                da_parts[i | (1 << bit)] = tp_swap(da_parts[i], bit)
    back = lambda q, o, lse, da, base, sums: attend_back(
        scalars, q, o, lse, k, kt, v, cos, sin, w_out, da, rows, zone, base, sums
    )
    near_parts = [da_parts[i] for i in range(half)]
    dq_near, *sums = back(q_near, o_near, lse_near, near_parts, 0, None)
    da_parts[half] = after(da_parts[half], dq_near)
    for bit in reversed(range(bits - 1)):
        for i in list(da_parts):
            if i >= half:
                da_parts[i | (1 << bit)] = tp_swap(da_parts[i], bit)
    da_parts = [da_parts[i] for i in range(blocks)]
    out_part = out_grads(
        [after(da_parts[0], dq_near), *da_parts[1:half]], o_near, None
    )
    out_part = out_grads(da_parts[half:], o_far, out_part)
    mixed_side = join(after(far[0], dq_near), after(far[1], dq_near))
    mixed_core = tp_swap(after(near[1], dq_near), 0)
    before = [out_part, mixed_side, mixed_core]
    if nz == 4:

        rows_of = lambda g, at: lax.dynamic_slice_in_dim(g, at * each, each, 0)
        inner_side = tp_swap(rows_of(inner, 1 - ix), 1)
        before.append(inner)
    dq_far, dkv = back(after(q_far, *before), o_far, lse_far, da_parts[half:], half, sums)
    out_side = after(y_swap(pick(out_part, 1 - iy)), dkv)
    mixed_side = after(y_swap(mixed_side), dkv)
    qkv_grad, gain1 = qkv_grads(
        h_parts, dq_near, dq_far, dkv, w_all_t, norm1_gain)
    qkv_side = y_swap(pick(qkv_grad, 1 - iy))
    dh1_far = input_grads(after(dq_far, qkv_grad), dkv, w_all_t, rows, 1)
    dh1_side = fold(dh1_far, BF16)
    qkv_side = after(qkv_side, dh1_side)
    dh1_near = input_grads(
        dq_near, after(dkv, dh1_side, qkv_side), w_all_t, rows, 0
    )
    dh1 = fold(dh1_near, F32) + after(tp_swap(dh1_side, bits - 1), dh1_near[0]).astype(F32)
    output = after(x1, dh1_side) + near[0].astype(F32) + mixed_core.astype(F32) + mixed_side.astype(F32)
    n1 = x * r1
    scaled = dh1 * norm1_gain
    grad_input = dx1 + r1 * (scaled - n1 * jnp.mean(scaled * n1, axis=-1, keepdims=True))

    summed = jnp.concatenate(
        [
            after(pick(qkv_grad, iy), dh1_side).astype(F32) + qkv_side.astype(F32),
            pick(out_part, iy).astype(F32) + out_side.astype(F32),
        ],
        axis=2,
    )
    summed = lax.psum_scatter(
        summed.astype(BF16).reshape(nz * each, -1), "z", scatter_dimension=0, tiled=True
    ).astype(F32)
    grad_qkv, grad_outproj = summed[:, : q_cols + 2 * kv_cols], summed[:, q_cols + 2 * kv_cols :].T
    small = jnp.concatenate([router_part, gain2, gain1], axis=0)
    small = own_columns(sum_all(after(small, dh1_side)))
    if nz == 4:
        inner = rows_of(inner, ix).astype(F32) + after(inner_side, dh1_side).astype(F32)
        outer_side = tp_swap(rows_of(after(outer, dh1_side), 1 - ix), 1)
        outer = rows_of(outer, ix).astype(F32) + outer_side.astype(F32)
        inner, outer = inner.astype(BF16), outer.astype(BF16)
        home = lambda c, inside: (3 - inside if c else inside)
        moves = [
            [
                ((z * 2 + x_) * 2 + c, home(c, int(x_ == first_)) * 4 + z)
                for z in range(4)
                for x_ in range(2)
                for c in range(2)
            ]
            for first_ in range(2)
        ]
        zxc = ("z", "x", "c")
        one = lax.ppermute(jnp.where(ix == 0, inner, outer), zxc, moves[0])
        two = lax.ppermute(jnp.where(ix == 0, outer, inner), zxc, moves[1])
        inside = (iz == 1) | (iz == 2)
        part = jnp.concatenate(
            [jnp.where(inside, one, two), jnp.where(inside, two, one)], axis=0
        ).astype(F32)
    else:
        stacked = jnp.concatenate([grads_outer, grads_inner], axis=0)
        every = jnp.zeros((nz, width, 3 * hidden), BF16)
        every = lax.dynamic_update_slice_in_dim(every, stacked, ic * mine, 0)
        part = lax.psum_scatter(
            every.reshape(nz * width, 3 * hidden), "z", scatter_dimension=0, tiled=True
        )
        part = lax.psum_scatter(part, ("x", "c"), scatter_dimension=0, tiled=True).astype(F32)
    grad_gate = part[None, :, :hidden]
    grad_up = part[None, :, hidden : 2 * hidden]
    grad_down = part[:, 2 * hidden :].T[None]
    return (
        output,
        grad_input,
        small[experts + 1],
        grad_qkv[:, :q_cols],
        grad_qkv[:, q_cols : q_cols + kv_cols],
        grad_qkv[:, q_cols + kv_cols :],
        grad_outproj,
        small[experts],
        small[:experts].T,
        grad_gate,
        grad_up,
        grad_down,
    )


def solution(mesh):
    ep, tp = mesh.shape["ep"], mesh.shape["tp"]
    nz, nx = ep // 2, tp // 2
    grid = Mesh(mesh.devices.reshape(nz, 2, nx, 2), ("z", "y", "x", "c"))
    e, t = ("z", "y"), ("x", "c")
    every = ("z", "y", "x", "c")
    return jax.shard_map(
        functools.partial(body, (nz, nx)),
        mesh=grid,
        in_specs=(
            P(every, None),
            P(),
            P(None, t),
            P(None, t),
            P(None, t),
            P(t, None),
            P(),
            P(),
            P(e, None, None),
            P(e, None, None),
            P(e, None, None),
            P(every, None),
            P(e, None),
            P(e, None),
            P(every, None),
        ),
        out_specs=(
            P(every, None),
            P(every, None),
            P(every),
            P(e, t),
            P(e, t),
            P(e, t),
            P(t, e),
            P(every),
            P(every, None),
            P(e, t, None),
            P(e, t, None),
            P(e, None, t),
        ),
        check_vma=False,
    )
```

```python
import functools
import math

import jax
import jax.numpy as jnp
from jax import lax
from jax.experimental import pallas as pl
from jax.experimental.pallas import tpu as pltpu
from jax.sharding import Mesh, PartitionSpec as P

HEAD_SIZE = 64
HALF = HEAD_SIZE // 2
SEQUENCE_LENGTH = 2048
EPSILON = 1e-05
ROPE_BASE = 10000.0
MASK_FILL = -1e30
LANES = 128
F32 = jnp.float32
BF16 = jnp.bfloat16
VMEM_LIMIT = 60 * 1024 * 1024


def dot(a, b, ca=1, cb=0):
    return lax.dot_general(a, b, (((ca,), (cb,)), ((), ())), preferred_element_type=F32)


def after(value, *deps):
    return lax.optimization_barrier((value, *deps))[0]


def cost(micros):
    return pl.CostEstimate(
        flops=int(micros * 1e+09), transcendentals=0, bytes_accessed=int(micros * 3e+06)
    )


def params():
    return pltpu.CompilerParams(vmem_limit_bytes=VMEM_LIMIT)


def once(shape):
    return pl.BlockSpec(shape, lambda *_: (0,) * len(shape), pipeline_mode=pl.Buffered(1))


def qkv_kernel(q_cols, kv_cols, parts, *refs):
    h_refs, (w_ref, cos_ref, sin_ref) = refs[:parts], refs[parts : parts + 3]
    q_ref, k_ref, kt_ref, v_ref, vt_ref = refs[-5:]
    rows = h_refs[0].shape[0]
    scale = jnp.asarray(1.0 / math.sqrt(HEAD_SIZE), BF16)
    for b in range(parts):
        here = slice(b * rows, (b + 1) * rows)
        y = dot(w_ref[...], h_refs[b][...], 1, 1)
        cos, sin = cos_ref[:, here], sin_ref[:, here]

        def turned(base):
            a = y[base : base + HALF]
            b = y[base + HALF : base + HEAD_SIZE]
            return jnp.concatenate([a * cos - b * sin, b * cos + a * sin], axis=0)

        for h in range(q_cols // HEAD_SIZE):
            base = h * HEAD_SIZE
            q_ref[base : base + HEAD_SIZE, here] = turned(base).astype(BF16) * scale
        for g in range(kv_cols // HEAD_SIZE):
            base = g * HEAD_SIZE
            kt = turned(q_cols + base)
            kt_ref[base : base + HEAD_SIZE, here] = kt.astype(BF16)
            k_ref[g, here, :] = kt.T.astype(BF16)
            vt = y[q_cols + kv_cols + base : q_cols + kv_cols + base + HEAD_SIZE]
            vt_ref[base : base + HEAD_SIZE, here] = vt.astype(BF16)
            v_ref[g, here, :] = vt.T.astype(BF16)


def project_qkv(h_parts, w_all, cos, sin, q_cols, kv_cols, half, previous):
    parts = len(h_parts)
    rows, width = h_parts[0].shape
    size = parts * rows
    groups = kv_cols // HEAD_SIZE
    cols = q_cols + 2 * kv_cols
    lane_block = lambda *_: (0, half)
    row_block = lambda *_: (0, half, 0)
    kv_shapes = [
        jax.ShapeDtypeStruct((groups, 2 * size, HEAD_SIZE), BF16),
        jax.ShapeDtypeStruct((kv_cols, 2 * size), BF16),
    ] * 2
    kv_specs = [
        pl.BlockSpec((groups, size, HEAD_SIZE), row_block),
        pl.BlockSpec((kv_cols, size), lane_block),
    ] * 2
    previous = list(previous or ())
    return pl.pallas_call(
        functools.partial(qkv_kernel, q_cols, kv_cols, parts),
        grid=(1,),
        in_specs=[once((rows, width))] * parts
        + [
            once((cols, width)),
            pl.BlockSpec((HALF, size), lane_block),
            pl.BlockSpec((HALF, size), lane_block),
        ]
        + [pl.BlockSpec(memory_space=pl.ANY)] * len(previous),
        out_specs=[once((q_cols, size))] + kv_specs,
        out_shape=[jax.ShapeDtypeStruct((q_cols, size), BF16)] + kv_shapes,
        input_output_aliases={parts + 3 + i: 1 + i for i in range(len(previous))},
        compiler_params=params(),
        cost_estimate=cost(6),
        name="qkv",
    )(*h_parts, w_all, cos, sin, *previous)


def last_key(s_ref, zone, own, rows):
    zone_index = own * rows // zone
    zones = SEQUENCE_LENGTH // zone
    start = s_ref[1 + zone_index]
    stop = start + s_ref[1 + zones + zone_index]
    position = own * rows + lax.broadcasted_iota(jnp.int32, (1, rows), 1)
    return jnp.where((position >= start) & (position < stop), stop - 1, position)


def block_walk(me, own, rows, zone, pair):
    per_zone = zone // rows
    pair(own, True, True)
    for other in range(1, per_zone):
        pair(own ^ other, True, False)
    first = (own // per_zone) * per_zone

    def step(key_block, carry):
        pair(key_block, False, False)
        return carry

    lax.fori_loop(0, first, step, 0)


def attend_kernel(
    rows, zone, heads, groups, base, s_ref, q_ref, k_ref, vt_ref, w_ref, o_ref, lse_ref, *refs
):
    out_refs, (acc, top, total) = refs[:-3], refs[-3:]
    me = s_ref[0]
    own = me ^ (pl.program_id(0) + base)
    limit = last_key(s_ref, zone, own, rows)

    def pair(key_block, masked, first):
        offset = pl.multiple_of((me ^ key_block) * rows, rows)
        if masked:
            key_pos = key_block * rows + lax.broadcasted_iota(jnp.int32, (rows, rows), 0)
            allowed = key_pos <= limit
        for h in range(heads):
            g = h // (heads // groups)
            r = slice(h * HEAD_SIZE, (h + 1) * HEAD_SIZE)
            s = dot(k_ref[g, pl.ds(offset, rows), :], q_ref[r, :])
            if masked:
                s = jnp.where(allowed, s, MASK_FILL)
            peak = jnp.max(s, axis=0, keepdims=True)
            vt = vt_ref[g * HEAD_SIZE : (g + 1) * HEAD_SIZE, pl.ds(offset, rows)]
            if first:
                p = jnp.exp(s - peak)
                top[h : h + 1, :] = peak
                total[h : h + 1, :] = jnp.sum(p, axis=0, keepdims=True)
                acc[r, :] = dot(vt, p.astype(BF16))
            else:
                old = top[h : h + 1, :]
                new = jnp.maximum(old, peak)
                fade = jnp.exp(old - new)
                p = jnp.exp(s - new)
                top[h : h + 1, :] = new
                total[h : h + 1, :] = total[h : h + 1, :] * fade + jnp.sum(p, axis=0, keepdims=True)
                acc[r, :] = acc[r, :] * fade + dot(vt, p.astype(BF16))

    block_walk(me, own, rows, zone, pair)
    for h in range(heads):
        r = slice(h * HEAD_SIZE, (h + 1) * HEAD_SIZE)
        o_ref[r, :] = (acc[r, :] / total[h : h + 1, :]).astype(BF16)
        lse_ref[h : h + 1, :] = top[h : h + 1, :] + jnp.log(total[h : h + 1, :])
    for b, out_ref in enumerate(out_refs):

        @pl.when(pl.program_id(0) == b)
        def _():
            out_ref[...] = dot(o_ref[...], w_ref[...], 0, 0).astype(BF16)


def attend(scalars, q, at, count, k, vt, w_out, rows, zone, base, micros):
    q_cols = q.shape[0]
    size = count * rows
    groups = k.shape[0]
    width = w_out.shape[1]
    heads = q_cols // HEAD_SIZE
    block = lambda i, s: (0, i)
    return pl.pallas_call(
        functools.partial(attend_kernel, rows, zone, heads, groups, base),
        grid_spec=pltpu.PrefetchScalarGridSpec(
            num_scalar_prefetch=1,
            grid=(count,),
            in_specs=[
                pl.BlockSpec((q_cols, rows), lambda i, s: (0, i + at)),
                once(k.shape),
                once(vt.shape),
                once(w_out.shape),
            ],
            out_specs=[
                pl.BlockSpec((q_cols, rows), block),
                pl.BlockSpec((heads, rows), block),
            ]
            + [once((rows, width))] * count,
            scratch_shapes=[
                pltpu.VMEM((q_cols, rows), F32),
                pltpu.VMEM((8, rows), F32),
                pltpu.VMEM((8, rows), F32),
            ],
        ),
        out_shape=[
            jax.ShapeDtypeStruct((q_cols, size), BF16),
            jax.ShapeDtypeStruct((heads, size), F32),
        ]
        + [jax.ShapeDtypeStruct((rows, width), BF16)] * count,
        compiler_params=params(),
        cost_estimate=cost(micros),
        name="attend",
    )(scalars, q, k, vt, w_out)


def attend_back_kernel(rows, zone, heads, groups, base, parts, *refs):
    s_ref, q_ref, o_ref, lse_ref, k_ref, kt_ref, v_ref, cos_ref, sin_ref, w_ref = refs[:10]
    da_refs = refs[10 : 10 + parts]
    rest = refs[10 + parts :]
    if base:
        old_dk, old_dv, dq_ref, dkv_ref, dq, dk, dv, delta, do_ref = rest
    else:
        dq_ref, dk, dv, dq, delta, do_ref = rest
    me = s_ref[0]
    step = pl.program_id(0)
    own = me ^ (step + base)
    limit = last_key(s_ref, zone, own, rows)
    here = pl.multiple_of((step + base) * rows, rows)

    @pl.when(step == 0)
    def _():
        for b in range(parts):
            do_ref[b] = dot(w_ref[...], da_refs[b][...], 1, 1).astype(BF16)
        if base:
            dk[...] = old_dk[...]
            dv[...] = old_dv[...]
        else:
            dk[...] = jnp.zeros_like(dk)
            dv[...] = jnp.zeros_like(dv)

    for h in range(heads):
        r = slice(h * HEAD_SIZE, (h + 1) * HEAD_SIZE)
        delta[h : h + 1, :] = jnp.sum(
            do_ref[step, r, :].astype(F32) * o_ref[r, :].astype(F32), axis=0, keepdims=True
        )

    def pair(key_block, masked, first):
        offset = pl.multiple_of((me ^ key_block) * rows, rows)
        keys = pl.ds(offset, rows)
        if masked:
            key_pos = key_block * rows + lax.broadcasted_iota(jnp.int32, (rows, rows), 0)
            allowed = key_pos <= limit
        for g in range(groups):
            kb = k_ref[g, keys, :]
            vb = v_ref[g, keys, :]
            kt = kt_ref[g * HEAD_SIZE : (g + 1) * HEAD_SIZE, keys]
            dk_sum = dk[g, keys, :]
            dv_sum = dv[g, keys, :]
            for h in range(g * (heads // groups), (g + 1) * (heads // groups)):
                r = slice(h * HEAD_SIZE, (h + 1) * HEAD_SIZE)
                do = do_ref[step, r, :]
                s = dot(kb, q_ref[r, :])
                if masked:
                    s = jnp.where(allowed, s, MASK_FILL)
                p = jnp.exp(s - lse_ref[h : h + 1, :])
                dp = dot(vb, do)
                ds = (p * (dp - delta[h : h + 1, :])).astype(BF16)
                dv_sum = dv_sum + dot(p.astype(BF16), do, 1, 1)
                dk_sum = dk_sum + dot(ds, q_ref[r, :], 1, 1)
                part = dot(kt, ds)
                dq[r, :] = part if first else dq[r, :] + part
            dk[g, keys, :] = dk_sum
            dv[g, keys, :] = dv_sum

    block_walk(me, own, rows, zone, pair)
    cos, sin = cos_ref[:, pl.ds(here, rows)], sin_ref[:, pl.ds(here, rows)]
    scale = 1.0 / math.sqrt(HEAD_SIZE)
    for h in range(heads):
        at = h * HEAD_SIZE
        a = dq[at : at + HALF, :] * scale
        b = dq[at + HALF : at + HEAD_SIZE, :] * scale
        dq_ref[at : at + HALF, :] = (a * cos + b * sin).astype(BF16)
        dq_ref[at + HALF : at + HEAD_SIZE, :] = (b * cos - a * sin).astype(BF16)

    if base:

        @pl.when(step == pl.num_programs(0) - 1)
        def _():
            every_cos, every_sin = cos_ref[...], sin_ref[...]
            for g in range(groups):
                at = g * HEAD_SIZE
                turned = dk[g].T
                a, b = turned[:HALF], turned[HALF:]
                dkv_ref[at : at + HALF, :] = (a * every_cos + b * every_sin).astype(BF16)
                dkv_ref[at + HALF : at + HEAD_SIZE, :] = (b * every_cos - a * every_sin).astype(BF16)
                at = (groups + g) * HEAD_SIZE
                dkv_ref[at : at + HEAD_SIZE, :] = dv[g].T.astype(BF16)


def attend_back(scalars, q, o, lse, k, kt, v, cos, sin, w_out, da_parts, rows, zone, base, sums):
    q_cols, size = q.shape
    groups, total, _ = k.shape
    heads = q_cols // HEAD_SIZE
    parts = len(da_parts)
    block = lambda i, s: (0, i)
    sum_shape = (groups, total, HEAD_SIZE)
    inputs = [q, o, lse, k, kt, v, cos, sin, w_out, *da_parts]
    in_specs = [
        pl.BlockSpec((q_cols, rows), block),
        pl.BlockSpec((q_cols, rows), block),
        pl.BlockSpec((heads, rows), block),
    ] + [once(a.shape) for a in inputs[3:]]
    out_specs = [pl.BlockSpec((q_cols, rows), block)]
    out_shape = [jax.ShapeDtypeStruct((q_cols, size), BF16)]
    scratch = [pltpu.VMEM((q_cols, rows), F32)]
    if base:
        inputs += list(sums)
        in_specs += [once(sum_shape)] * 2
        out_specs += [once((2 * groups * HEAD_SIZE, total))]
        out_shape += [jax.ShapeDtypeStruct((2 * groups * HEAD_SIZE, total), BF16)]
        scratch += [pltpu.VMEM(sum_shape, F32)] * 2
    else:
        out_specs += [once(sum_shape)] * 2
        out_shape += [jax.ShapeDtypeStruct(sum_shape, F32)] * 2
    scratch += [pltpu.VMEM((8, rows), F32), pltpu.VMEM((parts, q_cols, rows), BF16)]
    return pl.pallas_call(
        functools.partial(attend_back_kernel, rows, zone, heads, groups, base, parts),
        grid_spec=pltpu.PrefetchScalarGridSpec(
            num_scalar_prefetch=1,
            grid=(size // rows,),
            in_specs=in_specs,
            out_specs=out_specs,
            scratch_shapes=scratch,
        ),
        out_shape=out_shape,
        compiler_params=params(),
        cost_estimate=cost(30),
        name="attend_back",
    )(scalars, *inputs)


def input_grad_kernel(dq_ref, dkv_ref, w_ref, *out_refs):
    q_cols = dq_ref.shape[0]
    rows = out_refs[0].shape[0]
    for b, out_ref in enumerate(out_refs):
        here = slice(b * rows, (b + 1) * rows)
        out = dot(dq_ref[:, here], w_ref[:q_cols, :], 0, 0)
        out = out + dot(dkv_ref[:, here], w_ref[q_cols:, :], 0, 0)
        out_ref[...] = out.astype(BF16)


def input_grads(dq, dkv, w_all_t, rows, half):
    q_cols, size = dq.shape
    cols, width = w_all_t.shape
    count = size // rows
    return pl.pallas_call(
        input_grad_kernel,
        grid=(1,),
        in_specs=[
            once((q_cols, size)),
            pl.BlockSpec((cols - q_cols, size), lambda i: (0, half)),
            once((cols, width)),
        ],
        out_specs=[once((rows, width))] * count,
        out_shape=[jax.ShapeDtypeStruct((rows, width), BF16)] * count,
        compiler_params=params(),
        cost_estimate=cost(5),
        name="input_grads",
    )(dq, dkv, w_all_t)


def qkv_grad_kernel(parts, *refs):
    h_refs = refs[: 2 * parts]
    near_ref, far_ref, dkv_ref, w_ref, gain_ref, grad_ref, gain_grad_ref = refs[2 * parts :]
    rows = h_refs[0].shape[0]
    sums = [0.0, 0.0]
    for b in range(2 * parts):
        dq_ref, at = (near_ref, b) if b < parts else (far_ref, b - parts)
        h = h_refs[b][...]
        sums[0] = sums[0] + dot(dq_ref[:, at * rows : (at + 1) * rows], h)
        sums[1] = sums[1] + dot(dkv_ref[:, b * rows : (b + 1) * rows], h)
    q_cols = near_ref.shape[0]
    grad_ref[:, :q_cols] = sums[0].T.astype(BF16)
    grad_ref[:, q_cols:] = sums[1].T.astype(BF16)
    gain = jnp.sum(sums[0] * w_ref[:q_cols, :].astype(F32), axis=0, keepdims=True)
    gain = gain + jnp.sum(sums[1] * w_ref[q_cols:, :].astype(F32), axis=0, keepdims=True)
    gain_grad_ref[...] = gain / gain_ref[...]


def qkv_grads(h_parts, dq_near, dq_far, dkv, w_all_t, gain):
    cols, width = w_all_t.shape
    inputs = [*h_parts, dq_near, dq_far, dkv, w_all_t, gain[None, :]]
    return pl.pallas_call(
        functools.partial(qkv_grad_kernel, len(h_parts) // 2),
        grid=(1,),
        in_specs=[once(a.shape) for a in inputs],
        out_specs=[once((width, cols)), once((1, width))],
        out_shape=[
            jax.ShapeDtypeStruct((width, cols), BF16),
            jax.ShapeDtypeStruct((1, width), F32),
        ],
        compiler_params=params(),
        cost_estimate=cost(10),
        name="qkv_grads",
    )(*inputs)


def out_grad_kernel(parts, finish, *refs):
    da_refs, o_ref, grad_ref = refs[:parts], refs[parts], refs[-1]
    rows = da_refs[0].shape[0]
    total = refs[parts + 1][...] if finish else 0.0
    for b in range(parts):
        total = total + dot(o_ref[:, b * rows : (b + 1) * rows], da_refs[b][...])
    grad_ref[...] = total.T.astype(BF16) if finish else total


def out_grads(da_parts, o, previous):
    q_cols, width = o.shape[0], da_parts[0].shape[1]
    inputs = [*da_parts, o] + ([] if previous is None else [previous])
    finish = previous is not None
    shape = (width, q_cols) if finish else (q_cols, width)
    return pl.pallas_call(
        functools.partial(out_grad_kernel, len(da_parts), finish),
        grid=(1,),
        in_specs=[once(a.shape) for a in inputs],
        out_specs=once(shape),
        out_shape=jax.ShapeDtypeStruct(shape, BF16 if finish else F32),
        compiler_params=params(),
        cost_estimate=cost(4),
        name="out_grads",
    )(*inputs)


def expert_kernel(experts, adds, choices, alone, *refs):
    s_ref, h0, h1, dy0, dy1, router_ref = refs[:6]
    w_choices = refs[6 : 6 + choices]
    old = refs[6 + choices : 6 + choices + (4 if adds else 0)]
    outs = refs[len(refs) - 19 :]
    mix0, mix1, dh0, dh1, act_out, dgu_out = outs[:6]
    h_s, dy_s, w_s, mix_s, dh_s, gates, dgate, mix_o, dh_o, act_o, dgu_o, in_sem, out_sem = outs[6:]
    e = pl.program_id(0)
    last = pl.num_programs(0) - 1
    rows, width = h0.shape
    hidden = w_s.shape[2] // 3
    lane = lax.broadcasted_iota(jnp.int32, (rows, LANES), 1)
    slot = lax.rem(e, 2)

    def fetch_weights(index, into):
        for n in range(choices):

            @pl.when(s_ref[0] == n)
            def _():
                pltpu.make_async_copy(
                    w_choices[n].at[index], w_s.at[into], in_sem.at[4 + into]
                ).start()

    tokens_in = [
        pltpu.make_async_copy(src, dst, in_sem.at[n])
        for n, (src, dst) in enumerate(
            ((h0, h_s.at[0]), (dy0, dy_s.at[0]), (h1, h_s.at[1]), (dy1, dy_s.at[1]))
        )
    ]
    old_in = [
        pltpu.make_async_copy(src, dst, in_sem.at[6 + n])
        for n, (src, dst) in enumerate(zip(old, (mix_o.at[0], mix_o.at[1], dh_o.at[0], dh_o.at[1])))
    ]

    @pl.when(e == 0)
    def _():
        tokens_in[0].start()
        fetch_weights(0, 0)
        for copy in tokens_in[1:] + old_in:
            copy.start()

    @pl.when(e < last)
    def _():
        fetch_weights(e + 1, 1 - slot)

    def block(i, carry):
        for n in range(2):

            @pl.when((e == 0) & (i == n))
            def _():
                tokens_in[2 * n].wait()
                tokens_in[2 * n + 1].wait()
                for copy in old_in[n::2]:
                    copy.wait()

        @pl.when(e == 0)
        def _():
            logits = dot(h_s[i], router_ref[...])
            logits = jnp.where(lane < experts, logits, MASK_FILL)
            weights = jnp.exp(logits - jnp.max(logits, axis=1, keepdims=True))
            weights = weights / jnp.sum(weights, axis=1, keepdims=True)
            gates[i] = weights * dy_s[i, :, width:].astype(F32)

        @pl.when(i == 0)
        def _():
            pltpu.make_async_copy(w_choices[0].at[0], w_s.at[slot], in_sem.at[4 + slot]).wait()

        mine = lane == s_ref[1 + e]
        gate = jnp.sum(jnp.where(mine, gates[i], 0.0), axis=1, keepdims=True)
        both = dot(h_s[i], w_s[slot, :, : 2 * hidden])
        gp, up = both[:, :hidden], both[:, hidden:]
        sg = jax.nn.sigmoid(gp)
        silu = gp * sg
        act = (silu * up).astype(BF16).astype(F32)
        dact = dot(dy_s[i, :, :width], w_s[slot, :, 2 * hidden :])
        chosen = dy_s[i, :, width:].astype(F32)
        own_dgate = jnp.where(mine, chosen * jnp.sum(act * dact, axis=1, keepdims=True), 0.0)
        scaled = (gate * act).astype(BF16)
        dact = gate * dact
        dgp = (dact * up * sg * (1.0 + gp * (1.0 - sg))).astype(BF16)
        dup = (dact * silu).astype(BF16)
        here = pl.ds(pl.multiple_of(i * rows, rows), rows)
        act_copy = pltpu.make_async_copy(act_o.at[i], act_out.at[e, here, :], out_sem.at[i])
        dgu_copy = pltpu.make_async_copy(dgu_o.at[i], dgu_out.at[e, here, :], out_sem.at[2 + i])

        @pl.when(e > 0)
        def _():
            act_copy.wait()
            dgu_copy.wait()

        act_o[i] = scaled
        dgu_o[i, :, :hidden] = dgp
        dgu_o[i, :, hidden:] = dup
        act_copy.start()
        dgu_copy.start()
        mix = dot(scaled, w_s[slot, :, 2 * hidden :], 1, 1)
        dh = dot(dgu_o[i], w_s[slot, :, : 2 * hidden], 1, 1)

        def finish(mix, dh, own_dgate):
            mix_o[i] = mix.astype(BF16)
            dh_o[i, :, :width] = dh.astype(BF16)
            high = own_dgate.astype(BF16).astype(F32)
            low = own_dgate - high
            dh_o[i, :, width:] = (high + pltpu.roll(low, LANES // 2, 1)).astype(BF16)

        if adds:
            kept = dh_o[i, :, width:].astype(F32)
            kept = kept + pltpu.roll(kept, LANES // 2, 1)
            kept = jnp.where(lane < LANES // 2, kept, 0.0)
        if adds and alone:
            finish(mix + mix_o[i].astype(F32), dh + dh_o[i, :, :width].astype(F32), own_dgate + kept)
        elif alone:
            finish(mix, dh, own_dgate)
        else:

            @pl.when(e == 0)
            def _():
                if adds:
                    mix_s[i] = mix + mix_o[i].astype(F32)
                    dh_s[i] = dh + dh_o[i, :, :width].astype(F32)
                    dgate[i] = own_dgate + kept
                else:
                    mix_s[i] = mix
                    dh_s[i] = dh
                    dgate[i] = own_dgate

            @pl.when(e > 0)
            def _():
                mix_s[i] += mix
                dh_s[i] += dh
                dgate[i] += own_dgate

            @pl.when(e == last)
            def _():
                finish(mix_s[i], dh_s[i], dgate[i])

        for n in range(2):

            @pl.when((e == last) & (i == n))
            def _():
                pltpu.make_async_copy(mix_o.at[n], (mix0, mix1)[n], out_sem.at[4 + n]).start()
                pltpu.make_async_copy(dh_o.at[n], (dh0, dh1)[n], out_sem.at[6 + n]).start()

        return carry

    lax.fori_loop(0, 2, block, 0)

    @pl.when(e == last)
    def _():
        for i in range(2):
            here = pl.ds(i * rows, rows)
            pltpu.make_async_copy(act_o.at[i], act_out.at[e, here, :], out_sem.at[i]).wait()
            pltpu.make_async_copy(dgu_o.at[i], dgu_out.at[e, here, :], out_sem.at[2 + i]).wait()
            pltpu.make_async_copy(mix_o.at[i], (mix0, mix1)[i], out_sem.at[4 + i]).wait()
            pltpu.make_async_copy(dh_o.at[i], (dh0, dh1)[i], out_sem.at[6 + i]).wait()


def run_experts(scalars, h_parts, dy_parts, router, choices, experts, micros, old=()):
    rows, width = h_parts[0].shape
    wide = width + LANES
    mine, _, cols = choices[0].shape
    hidden = cols // 3
    anywhere = pl.BlockSpec(memory_space=pl.ANY)
    return pl.pallas_call(
        functools.partial(expert_kernel, experts, bool(old), len(choices), mine == 1),
        grid_spec=pltpu.PrefetchScalarGridSpec(
            num_scalar_prefetch=1,
            grid=(mine,),
            in_specs=[anywhere] * 4 + [once((width, LANES))] + [anywhere] * (len(choices) + len(old)),
            out_specs=[anywhere] * 6,
            scratch_shapes=[
                pltpu.VMEM((2, rows, width), BF16),
                pltpu.VMEM((2, rows, wide), BF16),
                pltpu.VMEM((2, width, cols), BF16),
                pltpu.VMEM((2, rows, width), F32),
                pltpu.VMEM((2, rows, width), F32),
                pltpu.VMEM((2, rows, LANES), F32),
                pltpu.VMEM((2, rows, LANES), F32),
                pltpu.VMEM((2, rows, width), BF16),
                pltpu.VMEM((2, rows, wide), BF16),
                pltpu.VMEM((2, rows, hidden), BF16),
                pltpu.VMEM((2, rows, 2 * hidden), BF16),
                pltpu.SemaphoreType.DMA((10,)),
                pltpu.SemaphoreType.DMA((8,)),
            ],
        ),
        out_shape=[jax.ShapeDtypeStruct((rows, width), BF16)] * 2
        + [jax.ShapeDtypeStruct((rows, wide), BF16)] * 2
        + [
            jax.ShapeDtypeStruct((mine, 2 * rows, hidden), BF16),
            jax.ShapeDtypeStruct((mine, 2 * rows, 2 * hidden), BF16),
        ],
        compiler_params=params(),
        cost_estimate=cost(micros),
        name="experts",
    )(scalars, *h_parts, *dy_parts, router, *choices, *old)


def expert_grad_kernel(*refs):
    h_refs, dy_refs, acts, dgus = refs[:4], refs[4:8], refs[8:10], refs[10:12]
    out_ref, h_s, dy_s, act_s, dgu_s, sem = refs[12:]
    e = pl.program_id(0)
    rows, width = h_refs[0].shape
    hidden = act_s.shape[1]
    first, second = [], []
    for b in range(4):
        here = pl.ds(b * rows, rows)
        first.append(pltpu.make_async_copy(h_refs[b], h_s.at[here, :], sem.at[b]))
        second.append(
            pltpu.make_async_copy(dy_refs[b].at[:, pl.ds(0, width)], dy_s.at[here, :], sem.at[4 + b])
        )
    per_expert = []
    for b in range(2):
        here = pl.ds(2 * b * rows, 2 * rows)
        per_expert.append(pltpu.make_async_copy(dgus[b].at[e], dgu_s.at[here, :], sem.at[8 + b]))
    for b in range(2):
        here = pl.ds(2 * b * rows, 2 * rows)
        per_expert.append(pltpu.make_async_copy(acts[b].at[e], act_s.at[here, :], sem.at[10 + b]))
    for copy in per_expert[:2]:
        copy.start()

    @pl.when(e == 0)
    def _():
        for copy in first:
            copy.start()

    for copy in per_expert[2:]:
        copy.start()

    @pl.when(e == 0)
    def _():
        for copy in second:
            copy.start()
        for copy in first:
            copy.wait()

    for copy in per_expert[:2]:
        copy.wait()

    def rows_of(c):
        return pl.ds(pl.multiple_of(c * (width // 3), width // 3), width // 3)

    def gate_up(c, carry):
        out_ref[0, rows_of(c), : 2 * hidden] = dot(h_s[:, rows_of(c)], dgu_s[...], 0, 0).astype(BF16)
        return carry

    lax.fori_loop(0, 3, gate_up, 0)

    @pl.when(e == 0)
    def _():
        for copy in second:
            copy.wait()

    for copy in per_expert[2:]:
        copy.wait()

    def down(c, carry):
        out_ref[0, rows_of(c), 2 * hidden :] = dot(dy_s[:, rows_of(c)], act_s[...], 0, 0).astype(BF16)
        return carry

    lax.fori_loop(0, 3, down, 0)


def expert_grads(h_parts, dy_parts, acts, dgus):
    rows, width = h_parts[0].shape
    mine, _, hidden = acts[0].shape
    anywhere = pl.BlockSpec(memory_space=pl.ANY)
    return pl.pallas_call(
        expert_grad_kernel,
        grid=(mine,),
        in_specs=[anywhere] * 12,
        out_specs=pl.BlockSpec((1, width, 3 * hidden), lambda e: (e, 0, 0)),
        out_shape=jax.ShapeDtypeStruct((mine, width, 3 * hidden), BF16),
        scratch_shapes=[
            pltpu.VMEM((4 * rows, width), BF16),
            pltpu.VMEM((4 * rows, width), BF16),
            pltpu.VMEM((4 * rows, hidden), BF16),
            pltpu.VMEM((4 * rows, 2 * hidden), BF16),
            pltpu.SemaphoreType.DMA((12,)),
        ],
        compiler_params=params(),
        cost_estimate=cost(12),
        name="expert_grads",
    )(*h_parts, *dy_parts, *acts, *dgus)


def body(
    sizes,
    tokens,
    norm1_gain,
    w_query,
    key_weight,
    value_weight,
    w_out,
    norm2_gain,
    w_router,
    w_gate,
    w_up,
    w_down,
    routes,
    piece_first_position,
    piece_length,
    grad_out,
):
    nz, nx = sizes
    rows, width = tokens.shape
    blocks = 2 * nx
    half = blocks // 2
    q_cols, kv_cols = w_query.shape[1], key_weight.shape[1]
    experts = w_router.shape[1]
    hidden = w_gate.shape[2]
    zone = SEQUENCE_LENGTH // piece_length.shape[1]
    iz, iy, ix, ic = (lax.axis_index(a) for a in "zyxc")
    me = ix * 2 + ic

    def tp_swap(value, bit):
        if bit == 0:
            return lax.ppermute(value, "c", [(0, 1), (1, 0)])
        return lax.ppermute(value, "x", [(i, i ^ (1 << (bit - 1))) for i in range(nx)])

    def y_swap(value):
        return lax.ppermute(value, "y", [(0, 1), (1, 0)])

    bits = blocks.bit_length() - 1

    def fold(parts, kind):
        parts = dict(enumerate(parts))
        for bit in range(bits - 1):
            for i in sorted(parts, reverse=True):
                if i & (1 << bit):
                    parts[i] = tp_swap(parts[i], bit)
            for i in sorted(parts, reverse=True):
                if i & (1 << bit):
                    total = parts[i ^ (1 << bit)].astype(F32) + parts.pop(i).astype(F32)
                    parts[i ^ (1 << bit)] = total.astype(BF16 if bit < bits - 2 else kind)
        return parts[0]

    def sum_all(value):
        step = 1
        while step < nz:
            value = value + lax.ppermute(value, "z", [(i, i ^ step) for i in range(nz)])
            step *= 2
        value = value + y_swap(value)
        for bit in range(bits):
            value = value + tp_swap(value, bit)
        return value

    def own_columns(value):
        each = width // (nz * 4 * nx)
        index = (iz * 2 + iy) * blocks + me
        return lax.dynamic_slice_in_dim(value, index * each, each, 1)

    each = width // (2 * nz)

    def pick(grad, at):
        grad = grad.reshape(nz, 2, each, grad.shape[1])
        return lax.dynamic_index_in_dim(grad, at, 1, keepdims=False)

    x = tokens.astype(F32)
    r1 = lax.rsqrt(jnp.mean(x * x, axis=-1, keepdims=True) + EPSILON)
    h1 = (x * r1 * norm1_gain).astype(BF16)
    h_parts = {0: h1}
    for bit in reversed(range(bits)):
        for i in list(h_parts):
            if i < half:
                h_parts[i | (1 << bit)] = tp_swap(h_parts[i], bit)

    w_all = jnp.concatenate([w_query, key_weight, value_weight], axis=1)
    w_all_t = w_all.T
    order = me ^ jnp.arange(blocks, dtype=jnp.int32)
    position = (order[:, None] * rows + jnp.arange(rows, dtype=jnp.int32)[None, :]).reshape(-1)
    frequency = ROPE_BASE ** (-(jnp.arange(HALF, dtype=F32) * (2.0 / HEAD_SIZE)))
    angles = frequency[:, None] * position.astype(F32)[None, :]
    cos, sin = jnp.cos(angles), jnp.sin(angles)
    scalars = jnp.concatenate(
        [me.astype(jnp.int32)[None], piece_first_position[0], piece_length[0]]
    )
    near_rows = [h_parts[i] for i in range(half)]
    q_near, *kv = project_qkv(near_rows, w_all_t, cos, sin, q_cols, kv_cols, 0, None)
    h_parts[half] = after(h_parts[half], q_near)
    for bit in reversed(range(bits - 1)):
        for i in list(h_parts):
            if i >= half:
                h_parts[i | (1 << bit)] = tp_swap(h_parts[i], bit)
    h_parts = [h_parts[i] for i in range(blocks)]

    mask = jnp.zeros((rows, LANES), jnp.bool_)
    for j in range(routes.shape[1]):
        mask = mask | (routes[:, j : j + 1] == jnp.arange(LANES, dtype=jnp.int32)[None, :])
    dy_own = after(jnp.concatenate([grad_out, mask.astype(BF16)], axis=1), q_near)
    dy_side = y_swap(dy_own)

    mine = nz // 2
    cut = mine // 2
    weight = after(jnp.concatenate([w_gate[0], w_up[0], w_down[0].T], axis=1), h_parts[1])[None]
    if nz == 4:
        ids = jnp.where(ic == 0, jnp.arange(2), 3 - jnp.arange(2)) * 2 + iy
        along = jnp.where(ic == 0, iz, 3 - iz)

        def shift(value, moves):
            perm = [(s * 2, d * 2) for s, d in moves]
            perm += [((3 - s) * 2 + 1, (3 - d) * 2 + 1) for s, d in moves]
            return lax.ppermute(value, ("z", "c"), perm)

        from_outer = shift(weight, [(0, 1), (1, 2)])
        from_inner = shift(weight, [(1, 0)])
    else:
        ids = (ic * mine + jnp.arange(mine)) * 2 + iy
        along = ic * 0

    q_far, k, kt, v, vt = project_qkv(h_parts[half:], w_all_t, cos, sin, q_cols, kv_cols, 1, kv)
    quarter = half // 2
    run = lambda q, at, count, base, micros: attend(
        scalars, q, at, count, k, vt, w_out, rows, zone, base, micros
    )
    o_3, lse_3, *out_3 = run(q_far, quarter, quarter, half + quarter, 9)
    early = ()
    if nz == 4:
        early = (from_outer,)
        second = shift(after(from_outer, out_3[0]), [(1, 2), (2, 3)])
    o_2, lse_2, *out_2 = run(after(q_far, out_3[0], *early), 0, quarter, half, 2)
    side = fold([*out_2, *out_3], BF16)
    if nz == 4:
        o_near, lse_near, *out_near = run(after(q_near, side), 0, half, 0, 2)
    else:
        o_near, lse_near, *out_near = run(after(q_near, side), 0, half, 0, 2)
    o_far = jnp.concatenate([o_2, o_3], axis=1)
    lse_far = jnp.concatenate([lse_2, lse_3], axis=1)
    dy_parts = [dy_own, tp_swap(after(dy_own, out_3[0]), 0), dy_side]
    dy_parts.append(tp_swap(after(dy_side, out_2[0]), 0))
    near_sum = fold(out_near, F32)
    attended = near_sum + after(tp_swap(side, bits - 1), out_near[0]).astype(F32)
    if nz == 4:
        third = shift(after(second, near_sum), [(2, 3)])
        outer = (weight, from_outer, second, third)
        inner = (from_inner, weight, from_outer, second)
    else:
        every = lax.all_gather(weight, "z", axis=0, tiled=True)
        every = lax.dynamic_slice_in_dim(every, ic * mine, mine, 0)
        outer, inner = (every[:cut],), (every[cut:],)
    x1 = (after(x, second, dy_side, from_inner) if nz == 4 else x) + attended
    r2 = lax.rsqrt(jnp.mean(x1 * x1, axis=-1, keepdims=True) + EPSILON)
    n2 = x1 * r2
    h2 = (n2 * norm2_gain).astype(BF16)

    router_wide = jnp.pad(w_router, ((0, 0), (0, LANES - experts)))
    h2_side = y_swap(h2)
    h2_parts = [h2, tp_swap(h2, 0), h2_side]
    head = along.astype(jnp.int32)[None]
    outer_ids = jnp.concatenate([head, ids[:cut].astype(jnp.int32)])
    inner_ids = jnp.concatenate([head, ids[cut:].astype(jnp.int32)])
    through = lambda s, at, w, old=(): run_experts(
        s, h2_parts[at : at + 2], dy_parts[at : at + 2], router_wide, w, experts, 8 * cut, old
    )
    first = through(inner_ids, 0, inner)
    h2_parts.append(tp_swap(after(h2_side, first[4]), 0))
    third_pass = through(inner_ids, 2, inner)
    near = through(after(outer_ids, third_pass[4]), 0, outer, first[:4])
    far = through(after(outer_ids, near[4]), 2, outer, third_pass[:4])

    join = lambda a, b: (a.astype(F32) + tp_swap(b, 0).astype(F32)).astype(BF16)
    dh_side = join(far[2], far[3])
    dh_own = near[2].astype(F32) + tp_swap(near[3], 0).astype(F32)
    grads_inner = expert_grads(
        [after(h2_parts[0], dh_side), *h2_parts[1:]],
        dy_parts,
        (first[4], third_pass[4]),
        (first[5], third_pass[5]),
    )
    grads_outer = expert_grads(
        [after(h2_parts[0], grads_inner), *h2_parts[1:]],
        dy_parts,
        (near[4], far[4]),
        (near[5], far[5]),
    )
    dh_sum = after(dh_own, grads_outer) + after(y_swap(dh_side), grads_outer).astype(F32)
    probs = jax.nn.softmax(dot(h2, w_router), axis=-1)
    dprobs = dh_sum[:, width : width + experts]
    dprobs = dprobs + dh_sum[:, width + LANES // 2 : width + LANES // 2 + experts]
    dlogits = (
        probs * (dprobs - jnp.sum(probs * dprobs, axis=-1, keepdims=True))
    ).astype(BF16)
    dh2 = dot(dlogits, w_router, 1, 1) + dh_sum[:, :width]
    scaled = dh2 * norm2_gain
    dx1 = grad_out.astype(F32) + r2 * (
        scaled - n2 * jnp.mean(scaled * n2, axis=-1, keepdims=True)
    )
    router_part = dot(dlogits, h2, 0, 0)
    gain2 = jnp.sum(dh2 * n2, axis=0, keepdims=True)

    if nz == 4:
        reduce = lambda g: lax.psum_scatter(g, "z", scatter_dimension=0, tiled=True)
        inner, outer = reduce(grads_inner[0]), reduce(grads_outer[0])
    else:
        inner, outer = grads_inner, grads_outer

    da = dx1.astype(BF16)
    da_parts = {0: da}
    for bit in reversed(range(bits)):
        for i in list(da_parts):
            if i < half:
                da_parts[i | (1 << bit)] = tp_swap(da_parts[i], bit)
    back = lambda q, o, lse, da, base, sums: attend_back(
        scalars, q, o, lse, k, kt, v, cos, sin, w_out, da, rows, zone, base, sums
    )
    near_parts = [da_parts[i] for i in range(half)]
    dq_near, *sums = back(q_near, o_near, lse_near, near_parts, 0, None)
    da_parts[half] = after(da_parts[half], dq_near)
    for bit in reversed(range(bits - 1)):
        for i in list(da_parts):
            if i >= half:
                da_parts[i | (1 << bit)] = tp_swap(da_parts[i], bit)
    da_parts = [da_parts[i] for i in range(blocks)]
    out_part = out_grads(
        [after(da_parts[0], dq_near), *da_parts[1:half]], o_near, None
    )
    out_part = out_grads(da_parts[half:], o_far, out_part)
    mixed_side = join(after(far[0], dq_near), after(far[1], dq_near))
    mixed_core = tp_swap(after(near[1], dq_near), 0)
    before = [out_part, mixed_side, mixed_core]
    if nz == 4:

        rows_of = lambda g, at: lax.dynamic_slice_in_dim(g, at * each, each, 0)
        inner_side = tp_swap(rows_of(inner, 1 - ix), 1)
        before.append(inner)
    dq_far, dkv = back(after(q_far, *before), o_far, lse_far, da_parts[half:], half, sums)
    out_side = after(y_swap(pick(out_part, 1 - iy)), dkv)
    mixed_side = after(y_swap(mixed_side), dkv)
    qkv_grad, gain1 = qkv_grads(
        h_parts, dq_near, dq_far, dkv, w_all_t, norm1_gain)
    qkv_side = y_swap(pick(qkv_grad, 1 - iy))
    dh1_far = input_grads(after(dq_far, qkv_grad), dkv, w_all_t, rows, 1)
    dh1_side = fold(dh1_far, BF16)
    qkv_side = after(qkv_side, dh1_side)
    dh1_near = input_grads(
        dq_near, after(dkv, dh1_side, qkv_side), w_all_t, rows, 0
    )
    dh1 = fold(dh1_near, F32) + after(tp_swap(dh1_side, bits - 1), dh1_near[0]).astype(F32)
    output = after(x1, dh1_side) + near[0].astype(F32) + mixed_core.astype(F32) + mixed_side.astype(F32)
    n1 = x * r1
    scaled = dh1 * norm1_gain
    grad_input = dx1 + r1 * (scaled - n1 * jnp.mean(scaled * n1, axis=-1, keepdims=True))

    summed = jnp.concatenate(
        [
            after(pick(qkv_grad, iy), dh1_side).astype(F32) + qkv_side.astype(F32),
            pick(out_part, iy).astype(F32) + out_side.astype(F32),
        ],
        axis=2,
    )
    summed = lax.psum_scatter(
        summed.astype(BF16).reshape(nz * each, -1), "z", scatter_dimension=0, tiled=True
    ).astype(F32)
    grad_qkv, grad_outproj = summed[:, : q_cols + 2 * kv_cols], summed[:, q_cols + 2 * kv_cols :].T
    small = jnp.concatenate([router_part, gain2, gain1], axis=0)
    small = own_columns(sum_all(after(small, dh1_side)))
    if nz == 4:
        inner = rows_of(inner, ix).astype(F32) + after(inner_side, dh1_side).astype(F32)
        outer_side = tp_swap(rows_of(after(outer, dh1_side), 1 - ix), 1)
        outer = rows_of(outer, ix).astype(F32) + outer_side.astype(F32)
        inner, outer = inner.astype(BF16), outer.astype(BF16)
        home = lambda c, inside: (3 - inside if c else inside)
        moves = [
            [
                ((z * 2 + x_) * 2 + c, home(c, int(x_ == first_)) * 4 + z)
                for z in range(4)
                for x_ in range(2)
                for c in range(2)
            ]
            for first_ in range(2)
        ]
        zxc = ("z", "x", "c")
        one = lax.ppermute(jnp.where(ix == 0, inner, outer), zxc, moves[0])
        two = lax.ppermute(jnp.where(ix == 0, outer, inner), zxc, moves[1])
        inside = (iz == 1) | (iz == 2)
        part = jnp.concatenate(
            [jnp.where(inside, one, two), jnp.where(inside, two, one)], axis=0
        ).astype(F32)
    else:
        stacked = jnp.concatenate([grads_outer, grads_inner], axis=0)
        every = jnp.zeros((nz, width, 3 * hidden), BF16)
        every = lax.dynamic_update_slice_in_dim(every, stacked, ic * mine, 0)
        part = lax.psum_scatter(
            every.reshape(nz * width, 3 * hidden), "z", scatter_dimension=0, tiled=True
        )
        part = lax.psum_scatter(part, ("x", "c"), scatter_dimension=0, tiled=True).astype(F32)
    grad_gate = part[None, :, :hidden]
    grad_up = part[None, :, hidden : 2 * hidden]
    grad_down = part[:, 2 * hidden :].T[None]
    return (
        output,
        grad_input,
        small[experts + 1],
        grad_qkv[:, :q_cols],
        grad_qkv[:, q_cols : q_cols + kv_cols],
        grad_qkv[:, q_cols + kv_cols :],
        grad_outproj,
        small[experts],
        small[:experts].T,
        grad_gate,
        grad_up,
        grad_down,
    )


def solution(mesh):
    ep, tp = mesh.shape["ep"], mesh.shape["tp"]
    nz, nx = ep // 2, tp // 2
    grid = Mesh(mesh.devices.reshape(nz, 2, nx, 2), ("z", "y", "x", "c"))
    e, t = ("z", "y"), ("x", "c")
    every = ("z", "y", "x", "c")
    return jax.shard_map(
        functools.partial(body, (nz, nx)),
        mesh=grid,
        in_specs=(
            P(every, None),
            P(),
            P(None, t),
            P(None, t),
            P(None, t),
            P(t, None),
            P(),
            P(),
            P(e, None, None),
            P(e, None, None),
            P(e, None, None),
            P(every, None),
            P(e, None),
            P(e, None),
            P(every, None),
        ),
        out_specs=(
            P(every, None),
            P(every, None),
            P(every),
            P(e, t),
            P(e, t),
            P(e, t),
            P(t, e),
            P(every),
            P(every, None),
            P(e, t, None),
            P(e, t, None),
            P(e, None, t),
        ),
        check_vma=False,
    )
```
